32 devices in a mesh: seq: 2 (over x), fsdp: 4 (over z), dp: 4 (over y, core).
Axes of the slice: x: 2, y: 2, z: 4, core: 2. Of those that a mesh axis runs over, the one named last changes fastest.
Arguments:
- image_in: bfloat16 [32, 1024, 1536], P(('fsdp', 'dp'), 'seq'), may hold values from -6 to 6
- text_in: bfloat16 [32, 154, 1536], P(('fsdp', 'dp'), 'seq'), may hold values from -6 to 6
- modulation: float32 [32, 2, 6, 1536], P(('fsdp', 'dp')), may hold values from -3 to 3
- text_len: int32 [32], P(('fsdp', 'dp')), may hold values from 1 to 154, as said below
- w_qkv: bfloat16 [2, 1536, 4608], P(None, 'fsdp'), may hold values from -0.15625 to 0.15625
- b_qkv: bfloat16 [2, 4608], P(None, 'fsdp'), may hold values from -0.59765625 to 0.59765625
- w_out: bfloat16 [2, 1536, 1536], P(None, 'fsdp'), may hold values from -0.875 to 0.875
- b_out: bfloat16 [2, 1536], P(None, 'fsdp'), may hold values from -3 to 3
- w_up: bfloat16 [2, 1536, 6144], P(None, 'fsdp'), may hold values from -0.15625 to 0.15625
- b_up: bfloat16 [2, 6144], P(None, 'fsdp'), may hold values from -3 to 3
- w_down: bfloat16 [2, 6144, 1536], P(None, 'fsdp'), may hold values from -0.078125 to 0.078125
- b_down: bfloat16 [2, 1536], P(None, 'fsdp'), may hold values from -3 to 3
- d_image: bfloat16 [32, 1024, 1536], P(('fsdp', 'dp'), 'seq'), may hold values from -6 to 6
- d_text: bfloat16 [32, 154, 1536], P(('fsdp', 'dp'), 'seq'), may hold values from -6 to 6
Outputs:
- out_image: bfloat16 [32, 1024, 1536], P(('fsdp', 'dp'), 'seq')
- out_text: bfloat16 [32, 154, 1536], P(('fsdp', 'dp'), 'seq')
- grad_image: float32 [32, 1024, 1536], P(('fsdp', 'dp'), 'seq')
- grad_text: float32 [32, 154, 1536], P(('fsdp', 'dp'), 'seq')
- grad_modulation: float32 [32, 2, 6, 1536], P(('fsdp', 'dp'))
- grad_w_qkv: float32 [2, 1536, 4608], P(None, ('seq', 'fsdp', 'dp'))
- grad_b_qkv: float32 [2, 4608], P(None, ('seq', 'fsdp', 'dp'))
- grad_w_out: float32 [2, 1536, 1536], P(None, ('seq', 'fsdp', 'dp'))
- grad_b_out: float32 [2, 1536], P(None, ('seq', 'fsdp', 'dp'))
- grad_w_up: float32 [2, 1536, 6144], P(None, ('seq', 'fsdp', 'dp'))
- grad_b_up: float32 [2, 6144], P(None, ('seq', 'fsdp', 'dp'))
- grad_w_down: float32 [2, 6144, 1536], P(None, ('seq', 'fsdp', 'dp'))
- grad_b_down: float32 [2, 1536], P(None, ('seq', 'fsdp', 'dp'))
The draws below stay inside these ranges and needn't reach their ends.
Inputs may be any that keep to these rules, and one draw needn't show every extreme that they name: Each sequence has text_len real text tokens among its 154 text slots.
All inputs are finite; a program needn't handle non-finite values.
Results may differ from the reference program's by a relative error of at most 0.0085.
Values may be sent and summed in bfloat16 or wider, within the bound.
A program may use at most 768 MiB of HBM per device.

```python
import math
import jax
import jax.numpy as jnp
from jax import lax

D = 1536
HEADS = 24
HEAD_DIM = 64
FF = 6144
IMG = 1024
TXT = 154
SEQS = 32


def draw_text_len(key, part):
    counts = jax.random.randint(key, (SEQS,), 1, TXT + 1, dtype=jnp.int32)
    counts = counts.at[0].set(TXT)
    counts = counts.at[SEQS - 1].set(1)
    return counts


def shard_levels(stream_key, extent, cuts, least, top_value):
    level = 1.0
    for dim, blocks in cuts:
        draws = jax.random.uniform(jax.random.fold_in(jax.random.fold_in(stream_key, 6), dim), (blocks,), jnp.float32, least / len(cuts), top_value / len(cuts))
        level = level * jnp.repeat(jnp.exp(draws), extent[dim] // blocks).reshape((-1,) + (1,) * (len(extent) - 1 - dim))
    return level


def normal_values(own_key, dims, deviation, most, shards=(), kind=jnp.bfloat16):
    result = deviation * jax.random.normal(own_key, dims, jnp.float32)
    if shards:
        result = result * shard_levels(own_key, dims, shards, -0.22, 0.18)
    return jnp.clip(result, -most, most).astype(kind)


def setup_inputs(seed: int = 0) -> dict:
    arg_keys = jax.random.split(jax.random.key(seed), 15)
    image_in = normal_values(arg_keys[0], (SEQS, IMG, D), 1.0, 6.0, ((0, 16), (1, 2)))
    text_in = normal_values(arg_keys[1], (SEQS, TXT, D), 1.0, 6.0, ((0, 16), (1, 2)))
    modulation = normal_values(arg_keys[2], (SEQS, 2, 6, D), 0.5, 3.0, ((0, 16),), jnp.float32)
    text_len = draw_text_len(jax.random.fold_in(arg_keys[14], 71), 0)
    w_qkv = normal_values(arg_keys[4], (2, D, 3 * D), D ** -0.5, 0.15625, ((1, 4),))
    b_qkv = normal_values(arg_keys[5], (2, 3 * D), 0.1, 0.59765625, ((1, 4),))
    w_out = normal_values(arg_keys[6], (2, D, D), (D // 32) ** -0.5, 0.875, ((1, 4),))
    b_out = normal_values(arg_keys[7], (2, D), 0.5, 3.0, ((1, 4),))
    w_up = normal_values(arg_keys[8], (2, D, FF), D ** -0.5, 0.15625, ((1, 4),))
    b_up = normal_values(arg_keys[9], (2, FF), 0.5, 3.0, ((1, 4),))
    w_down = normal_values(arg_keys[10], (2, FF, D), FF ** -0.5, 0.078125, ((1, 4),))
    b_down = normal_values(arg_keys[11], (2, D), 0.5, 3.0, ((1, 4),))
    d_image = normal_values(arg_keys[12], (SEQS, IMG, D), 1.0, 6.0, ((0, 16), (1, 2)))
    d_text = normal_values(arg_keys[13], (SEQS, TXT, D), 1.0, 6.0, ((0, 16), (1, 2)))
    return {"image_in": image_in, "text_in": text_in, "modulation": modulation, "text_len": text_len, "w_qkv": w_qkv, "b_qkv": b_qkv, "w_out": w_out, "b_out": b_out, "w_up": w_up, "b_up": b_up, "w_down": w_down, "b_down": b_down, "d_image": d_image, "d_text": d_text}


@jax.custom_vjp
def low(v):
    return lax.optimization_barrier(v.astype(jnp.bfloat16)).astype(jnp.float32)

@jax.custom_vjp
def low_back(v):
    return v

def low_keep(v):
    return (low(v), None)

def low_pass(kept, grad):
    return (grad,)

def back_keep(v):
    return (v, None)

def back_low(kept, grad):
    return (low(grad),)
low.defvjp(low_keep, low_pass)
low_back.defvjp(back_keep, back_low)
EPSILON = 1e-06
MASKED = -1000000000.0
HIGH = lax.Precision.HIGHEST

def normalize(values):
    row_mean = lax.optimization_barrier(jnp.mean(values, axis=-1, keepdims=True))
    centred = values - row_mean
    variance = lax.optimization_barrier(jnp.mean(centred * centred, axis=-1, keepdims=True))
    return centred * lax.rsqrt(variance + EPSILON)

def linear(values, weight, offset):
    return jnp.dot(values, weight, precision=HIGH) + offset

def head_block(queries, key_rows, values, key_valid):
    scores = jnp.einsum('hqd,hkd->hqk', queries, key_rows, precision=HIGH) * queries.shape[-1] ** (-0.5)
    scores = low_back(scores)
    scores = jnp.where(key_valid[None, None, :], scores, MASKED)
    attn_probs = jax.nn.softmax(scores, axis=-1)
    return jnp.einsum('hqk,hkd->hqd', low(attn_probs), values, precision=HIGH)

def joint_attention(joint_rows, key_valid):
    length = joint_rows.shape[0]
    model_width = joint_rows.shape[1] // 3
    head_group = math.gcd(HEADS, 8)

    def by_heads(columns):
        return columns.reshape(length, HEADS // head_group, head_group, HEAD_DIM).transpose(1, 2, 0, 3)

    def one_group(tensors):
        return head_block(tensors[0], tensors[1], tensors[2], key_valid)
    outputs = lax.map(jax.checkpoint(one_group), (by_heads(joint_rows[:, :model_width]), by_heads(joint_rows[:, model_width:2 * model_width]), by_heads(joint_rows[:, 2 * model_width:])))
    return outputs.transpose(2, 0, 1, 3).reshape(length, model_width)

def forward_layer(params, image, text, modulation, key_valid):
    w_qkv, b_qkv, w_out, b_out, w_up, b_up, w_down, b_down = params
    streams = (image, text)
    fronts = []
    for stream in range(2):
        gains = modulation[stream]
        modded = low(normalize(streams[stream]) * (1.0 + gains[1]) + gains[0])
        fronts.append(low(low_back(linear(modded, w_qkv[stream], b_qkv[stream]))))
    attended = low(low_back(joint_attention(jnp.concatenate(fronts, axis=0), key_valid)))
    results = []
    for stream in range(2):
        gains = modulation[stream]
        attn_rows = attended[:IMG] if stream == 0 else attended[IMG:]
        branch = low_back(linear(attn_rows, w_out[stream], b_out[stream]))
        middle = streams[stream] + gains[2] * branch
        modded_two = low(normalize(middle) * (1.0 + gains[4]) + gains[3])
        hidden = low_back(linear(modded_two, w_up[stream], b_up[stream]))
        active = low(jax.nn.gelu(hidden, approximate=True))
        mlp_out = low_back(linear(active, w_down[stream], b_down[stream]))
        results.append(middle + gains[5] * mlp_out)
    return (results[0], results[1])

def reference(image_in, text_in, modulation, text_len, w_qkv, b_qkv, w_out, b_out, w_up, b_up, w_down, b_down, d_image, d_text):
    params = (w_qkv.astype(jnp.float32), b_qkv.astype(jnp.float32), w_out.astype(jnp.float32), b_out.astype(jnp.float32), w_up.astype(jnp.float32), b_up.astype(jnp.float32), w_down.astype(jnp.float32), b_down.astype(jnp.float32))
    text_positions = jnp.arange(TXT, dtype=jnp.int32)

    def per_sequence(running, tensors):
        image, text, gains, text_count, cot_image, cot_text = tensors
        key_valid = jnp.concatenate([jnp.ones((IMG,), dtype=bool), text_positions < text_count])

        def forward_fn(weights, image_rows, text_rows, gain_rows):
            return forward_layer(weights, image_rows, text_rows, gain_rows, key_valid)
        results, pullback = jax.vjp(forward_fn, params, image.astype(jnp.float32), text.astype(jnp.float32), gains)
        grad_params, grad_img, grad_txt, grad_gains = pullback((cot_image.astype(jnp.float32), cot_text.astype(jnp.float32)))
        running = tuple((total_term + new_term for total_term, new_term in zip(running, grad_params)))
        return (running, (results[0].astype(jnp.bfloat16), results[1].astype(jnp.bfloat16), grad_img, grad_txt, grad_gains))
    zero_sums = tuple((jnp.zeros(tensor.shape, jnp.float32) for tensor in params))
    param_sums, per_rows = lax.scan(per_sequence, zero_sums, (image_in, text_in, modulation, text_len, d_image, d_text))
    return (per_rows[0], per_rows[1], per_rows[2], per_rows[3], per_rows[4], param_sums[0], param_sums[1], param_sums[2], param_sums[3], param_sums[4], param_sums[5], param_sums[6], param_sums[7])
```

```python
import functools

import jax
import jax.numpy as jnp
from jax import lax
from jax.experimental import pallas as pl
from jax.experimental.pallas import tpu as pltpu
from jax.sharding import PartitionSpec as P

EPSILON = 1e-06
HEAD_DIM=64
MASKED=-1000000000.0
def dot(a,b,ca,cb):
    return lax.dot_general(a,b,(((ca,),(cb,)),((),())),preferred_element_type=jnp.float32)

def attn_fwd_kernel(ti,tt,tq,len_ref,qi,ki,vi,qt,kt,vt,oi,ot,lse,ktp,vtp):
    tp=ktp.shape[0]
    ktp[...]=jnp.zeros_like(ktp); vtp[...]=jnp.zeros_like(vtp)
    ktp[:tt,:]=kt[...]; vtp[:tt,:]=vt[...]
    n_len=len_ref[0]; half=len_ref[1]; mine=len_ref[2]
    r=lax.broadcasted_iota(jnp.int32,(1,tp),1)
    pos=jnp.where(r<half,mine*half+r,(1-mine)*half+r-half)
    valid=(r<2*half)&(pos<n_len)
    lane=lax.broadcasted_iota(jnp.int32,(1,2*HEAD_DIM),1)
    k_img=ki[...]; v_img=vi[...]; k_txt=ktp[...]; v_txt=vtp[...]
    def one(q,rows):
        outs=[];lses=[]
        for h in range(2):
            qh=jnp.where((lane<HEAD_DIM)==(h==0),q.astype(jnp.float32)*(HEAD_DIM**-0.5),0.0).astype(jnp.bfloat16)
            s1=dot(qh,k_img,1,1); s2=dot(qh,k_txt,1,1)
            s2=jnp.where(valid,s2,MASKED)
            m=jnp.maximum(jnp.max(s1,axis=1,keepdims=True),jnp.max(s2,axis=1,keepdims=True))
            e1=jnp.exp(s1-m); e2=jnp.exp(s2-m)
            l=jnp.sum(e1,axis=1,keepdims=True)+jnp.sum(e2,axis=1,keepdims=True)
            inv=1.0/l
            o=dot((e1*inv).astype(jnp.bfloat16),v_img,1,0)+dot((e2*inv).astype(jnp.bfloat16),v_txt,1,0)
            outs.append(o); lses.append(m+jnp.log(l))
        o=jnp.where(lane<HEAD_DIM,outs[0],outs[1]).astype(jnp.bfloat16)
        both=jnp.where(lane<HEAD_DIM,jnp.broadcast_to(lses[0],(rows,128)),jnp.broadcast_to(lses[1],(rows,128)))
        return o,both.T
    def step(i,_):
        start=pl.multiple_of(i*tq,tq)
        o,b=one(qi[pl.ds(start,tq),:],tq)
        oi[pl.ds(start,tq),:]=o
        lse[0,0:1,pl.ds(start,tq)]=b[0:1]; lse[0,1:2,pl.ds(start,tq)]=b[64:65]
        return 0
    lax.fori_loop(0,ti//tq,step,0)
    qpad=jnp.concatenate([qt[...],jnp.zeros((tp-tt,128),jnp.bfloat16)],axis=0)
    o,b=one(qpad,tp)
    ot[...]=o[:tt]
    lse[0,0:1,ti:ti+tp]=b[0:1]; lse[0,1:2,ti:ti+tp]=b[64:65]

def attn_fwd(qkv_i,qkv_t,info,tq=256):
    ti,w3=qkv_i.shape; tt=qkv_t.shape[0]; w=w3//3; n=w//128; tp=256
    bi=lambda off: pl.BlockSpec((ti,128),lambda p,s,off=off:(0,p+off*n))
    bt=lambda off: pl.BlockSpec((tt,128),lambda p,s,off=off:(0,p+off*n))
    return pl.pallas_call(functools.partial(attn_fwd_kernel,ti,tt,tq),
        grid_spec=pltpu.PrefetchScalarGridSpec(num_scalar_prefetch=1,grid=(n,),
            in_specs=[bi(0),bi(1),bi(2),bt(0),bt(1),bt(2)],
            out_specs=[bi(0),bt(0),pl.BlockSpec((1,8,ti+tp),lambda p,s:(p,0,0))],
            scratch_shapes=[pltpu.VMEM((tp,128),jnp.bfloat16)]*2),
        out_shape=[jax.ShapeDtypeStruct((ti,w),jnp.bfloat16),jax.ShapeDtypeStruct((tt,w),jnp.bfloat16),
                   jax.ShapeDtypeStruct((n,8,ti+tp),jnp.float32)],
        compiler_params=pltpu.CompilerParams(vmem_limit_bytes=48<<20),
        cost_estimate=pl.CostEstimate(flops=8*(ti+tt)*(ti+tt)*w,bytes_accessed=8*(ti+tt)*w,transcendentals=2*n*(ti+tt)*(ti+tt)),
        name="attn_fwd")(info,qkv_i,qkv_i,qkv_i,qkv_t,qkv_t,qkv_t)

def attn_bwd_kernel(ti,tt,tq,len_ref,qi,ki,vi,qt,kt,vt,oi,ot,di,dt,lse,outi,outt,ktp,vtp,dk1,dk2,dv1,dv2,dqi,dqt):
    j=pl.program_id(1)
    tp=ktp.shape[0]
    @pl.when(j==0)
    def _():
        ktp[...]=jnp.zeros_like(ktp); vtp[...]=jnp.zeros_like(vtp)
        ktp[:tt,:]=kt[...]; vtp[:tt,:]=vt[...]
        n_len=len_ref[0]; half=len_ref[1]; mine=len_ref[2]
        r=lax.broadcasted_iota(jnp.int32,(tp,1),0)
        pos=jnp.where(r<half,mine*half+r,(1-mine)*half+r-half)
        valid=(r<2*half)&(pos<n_len)
        lane=lax.broadcasted_iota(jnp.int32,(1,128),1)
        sub=lax.broadcasted_iota(jnp.int32,(8,128),0); lane8=lax.broadcasted_iota(jnp.int32,(8,128),1)
        sel=jnp.where((lane8//HEAD_DIM)==sub,1.0,0.0).astype(jnp.bfloat16)
        k_img=ki[...]; v_img=vi[...]; k_txt=ktp[...]; v_txt=vtp[...]
        for ref in (dk1,dk2,dv1,dv2): ref[...]=jnp.zeros_like(ref)
        def one(q,do,o,ls):
            prod=do.astype(jnp.float32)*o.astype(jnp.float32)
            hi=prod.astype(jnp.bfloat16); lo=(prod-hi.astype(jnp.float32)).astype(jnp.bfloat16)
            dsum=dot(sel,hi,1,1)+dot(sel,lo,1,1)
            qs=(q.astype(jnp.float32)*(HEAD_DIM**-0.5))
            dof=do.astype(jnp.float32)
            dqs=[]
            for h in range(2):
                mk=(lane<HEAD_DIM)==(h==0)
                qh=jnp.where(mk,qs,0.0).astype(jnp.bfloat16)
                dh=jnp.where(mk,dof,0.0).astype(jnp.bfloat16)
                L=ls[h:h+1]; D=dsum[h:h+1]
                s1=dot(k_img,qh,1,1); s2=dot(k_txt,qh,1,1)
                p1=jnp.exp(s1-L); p2=jnp.where(valid,jnp.exp(s2-L),0.0)
                dp1=dot(v_img,dh,1,1); dp2=dot(v_txt,dh,1,1)
                ds1=(p1*(dp1-D)).astype(jnp.bfloat16); ds2=(p2*(dp2-D)).astype(jnp.bfloat16)
                dv1[...]+=dot(p1.astype(jnp.bfloat16),dh,1,0)
                dv2[...]+=dot(p2.astype(jnp.bfloat16),dh,1,0)
                dk1[...]+=dot(ds1,qh,1,0)
                dk2[...]+=dot(ds2,qh,1,0)
                dqs.append(dot(ds1,k_img,0,0)+dot(ds2,k_txt,0,0))
            return (jnp.where(lane<HEAD_DIM,dqs[0],dqs[1])*(HEAD_DIM**-0.5)).astype(jnp.bfloat16)
        def step(i,_):
            start=pl.multiple_of(i*tq,tq)
            sl=pl.ds(start,tq)
            dqi[sl,:]=one(qi[sl,:],di[sl,:],oi[sl,:],lse[0,:,sl])
            return 0
        lax.fori_loop(0,ti//tq,step,0)
        pad=lambda a: jnp.concatenate([a,jnp.zeros((tp-tt,128),jnp.bfloat16)],axis=0)
        dqt[...]=one(pad(qt[...]),pad(dt[...]),pad(ot[...]),lse[0,:,ti:ti+tp])[:tt]
        outi[...]=dqi[...]; outt[...]=dqt[...]
    @pl.when(j==1)
    def _():
        outi[...]=dk1[...].astype(jnp.bfloat16); outt[...]=dk2[:tt,:].astype(jnp.bfloat16)
    @pl.when(j==2)
    def _():
        outi[...]=dv1[...].astype(jnp.bfloat16); outt[...]=dv2[:tt,:].astype(jnp.bfloat16)

def attn_bwd(qkv_i,qkv_t,o_i,o_t,d_i,d_t,lse,info,tq=256):
    ti,w3=qkv_i.shape; tt=qkv_t.shape[0]; w=w3//3; n=w//128; tp=256
    bi=lambda off: pl.BlockSpec((ti,128),lambda p,j,s,off=off:(0,p+off*n))
    bt=lambda off: pl.BlockSpec((tt,128),lambda p,j,s,off=off:(0,p+off*n))
    return pl.pallas_call(functools.partial(attn_bwd_kernel,ti,tt,tq),
        grid_spec=pltpu.PrefetchScalarGridSpec(num_scalar_prefetch=1,grid=(n,3),
            in_specs=[bi(0),bi(1),bi(2),bt(0),bt(1),bt(2),bi(0),bt(0),bi(0),bt(0),pl.BlockSpec((1,8,ti+tp),lambda p,j,s:(p,0,0))],
            out_specs=[pl.BlockSpec((ti,128),lambda p,j,s:(0,p+j*n)),pl.BlockSpec((tt,128),lambda p,j,s:(0,p+j*n))],
            scratch_shapes=[pltpu.VMEM((tp,128),jnp.bfloat16)]*2+[pltpu.VMEM((ti,128),jnp.float32),pltpu.VMEM((tp,128),jnp.float32)]*2
              +[pltpu.VMEM((ti,128),jnp.bfloat16),pltpu.VMEM((tt,128),jnp.bfloat16)]),
        out_shape=[jax.ShapeDtypeStruct((ti,w3),jnp.bfloat16),jax.ShapeDtypeStruct((tt,w3),jnp.bfloat16)],
        compiler_params=pltpu.CompilerParams(vmem_limit_bytes=56<<20),
        cost_estimate=pl.CostEstimate(flops=20*(ti+tt)*(ti+tt)*w,bytes_accessed=16*(ti+tt)*w,transcendentals=2*n*(ti+tt)*(ti+tt)),
        name="attn_bwd")(info,qkv_i,qkv_i,qkv_i,qkv_t,qkv_t,qkv_t,o_i,o_t,d_i,d_t,lse)


def normalize(values):
    row_mean = jnp.mean(values, axis=-1, keepdims=True)
    centred = values - row_mean
    variance = jnp.mean(centred * centred, axis=-1, keepdims=True)
    inverse = lax.rsqrt(variance + EPSILON)
    return (centred * inverse, inverse)


def normalize_back(normed, inverse, upstream):
    mean_one = jnp.mean(upstream, axis=-1, keepdims=True)
    mean_two = jnp.mean(upstream * normed, axis=-1, keepdims=True)
    return inverse * (upstream - mean_one - normed * mean_two)


def linear(values, weight, offset):
    return jnp.dot(values, weight, preferred_element_type=jnp.float32) + offset.astype(jnp.float32)


def linear_back(upstream, weight):
    return dot(upstream, weight, 1, 1)


def gelu_tanh(values):
    return jax.nn.gelu(values, approximate=True)


def coords():
    dp = lax.axis_index("dp")
    return lax.axis_index("seq"), lax.axis_index("fsdp"), dp // 4, (dp // 2) % 2, dp % 2


def flip_x(a):
    return lax.ppermute(a, "seq", [(0, 1), (1, 0)])


def flip_y(a):
    return lax.ppermute(a, "dp", [(i, i ^ 2) for i in range(lax.axis_size("dp"))])


def flip_core(a):
    return lax.ppermute(a, "dp", [(i, i ^ 1) for i in range(lax.axis_size("dp"))])


def shift_z(a, k):
    n = lax.axis_size("fsdp")
    return lax.ppermute(a, "fsdp", [(i, (i + k) % n) for i in range(n)])


def shift_group(a, k):
    n = lax.axis_size("dp")
    return lax.ppermute(a, "dp", [(i, (i + 4 * k) % n) for i in range(n)])


def assemble(shard, parts):
    s, r, cols = shard.shape
    fs = parts[0][1].shape[0] + 1
    q, h = r // 4, cols // 2
    width = next(t for t in (768, 384, 256, 128) if h % t == 0 and fs * r * t * 2 <= (5 << 20))
    steps = [(i, j) for i in range(s) for j in range(cols // width)]

    def kernel(*refs):
        own, ins = refs[0], refs[1 : 1 + len(parts)]
        outs = refs[1 + len(parts) : 1 + len(parts) + s]
        buf, in_sem, out_sem = refs[1 + len(parts) + s :]
        x, z, _, y, c = coords()

        def loads(step):
            i, j = steps[step]
            slot = step % 2
            jobs = [(own.at[i, :, pl.ds(j * width, width)], z * r, r)]
            return i, j, slot, jobs

        def run(c_val):
            def copies(step):
                i, j, slot, jobs = loads(step)
                half = j * width // h
                dc_need = half ^ c_val
                for ref, ((dx, dy, dc), _) in zip(ins, parts):
                    if dc != dc_need:
                        continue
                    for k in range(1, fs):
                        src_z = lax.rem(z - k + fs, fs)
                        xx = x + dx - 2 * x * dx
                        yy = y + dy - 2 * y * dy
                        jobs.append(
                            (ref.at[k - 1, i, :, pl.ds(j * width - half * h, width)], src_z * r + (xx * 2 + yy) * q, q)
                        )
                return [
                    pltpu.make_async_copy(src, buf.at[slot, pl.ds(pl.multiple_of(row, 16), n), :], in_sem.at[slot, m])
                    for m, (src, row, n) in enumerate(jobs)
                ]

            def store(step):
                i, j = steps[step]
                return pltpu.make_async_copy(buf.at[step % 2], outs[i].at[:, pl.ds(j * width, width)], out_sem.at[step % 2])

            for cp in copies(0):
                cp.start()
            for step in range(len(steps)):
                if step + 1 < len(steps):
                    if step >= 1:
                        store(step - 1).wait()
                    for cp in copies(step + 1):
                        cp.start()
                for cp in copies(step):
                    cp.wait()
                store(step).start()
            if len(steps) > 1:
                store(len(steps) - 2).wait()
            store(len(steps) - 1).wait()

        for c_val in range(2):
            @pl.when(c == c_val)
            def _():
                run(c_val)

    n_in = 1 + 4 * (fs - 1)
    return pl.pallas_call(
        kernel,
        out_shape=[jax.ShapeDtypeStruct((r * fs, cols), shard.dtype)] * s,
        in_specs=[pl.BlockSpec(memory_space=pl.ANY)] * (1 + len(parts)),
        out_specs=[pl.BlockSpec(memory_space=pl.ANY)] * s,
        scratch_shapes=[
            pltpu.VMEM((2, fs * r, width), shard.dtype),
            pltpu.SemaphoreType.DMA((2, n_in)),
            pltpu.SemaphoreType.DMA((2,)),
        ],
        compiler_params=pltpu.CompilerParams(vmem_limit_bytes=32 << 20),
        cost_estimate=pl.CostEstimate(flops=0, bytes_accessed=4 * s * r * fs * cols, transcendentals=0),
        name="assemble",
    )(shard, *[a for _, a in parts])


def gather_weight(shard, x_first):
    fs = lax.axis_size("fsdp")
    x, z, _, y, c = coords()
    s, r, cols = shard.shape
    q, h = r // 4, cols // 2
    piece = lax.dynamic_slice(shard, (0, (x * 2 + y) * q, c * h), (s, q, h))
    slots, current = [], piece
    for _ in range(1, fs):
        current = shift_z(current, 1)
        slots.append(current)
    own = jnp.stack(slots)
    if x_first:
        first = flip_x(own)
        parts = [((0, 0, 0), own), ((1, 0, 0), first), ((0, 1, 0), flip_y(own)), ((1, 1, 0), flip_y(first))]
    else:
        first = flip_y(own)
        parts = [((0, 0, 0), own), ((0, 1, 0), first), ((1, 0, 0), flip_x(own)), ((1, 1, 0), flip_x(first))]
    parts = parts + [((dx, dy, 1), flip_core(a)) for (dx, dy, _), a in parts]
    return assemble(shard, parts)


def wgrad_kernel(sel_ref, a0, b0, a1, b1, out):
    out[...] = (dot(a0[...], b0[...], 0, 0) + dot(a1[...], b1[...], 0, 0)).astype(out.dtype)


def wgrad(a0, b0, a1, b1, row_half, col_half):
    tokens, rows = a0.shape
    cols = b0.shape[1]
    tr = tc = 768
    nr, nc = rows // 2 // tr, cols // 2 // tc
    a_spec = pl.BlockSpec((tokens, tr), lambda i, j, s: (0, s[0] * nr + i))
    b_spec = pl.BlockSpec((tokens, tc), lambda i, j, s: (0, s[1] * nc + j))
    return pl.pallas_call(
        wgrad_kernel,
        grid_spec=pltpu.PrefetchScalarGridSpec(
            num_scalar_prefetch=1,
            grid=(nr, nc),
            in_specs=[a_spec, b_spec, a_spec, b_spec],
            out_specs=pl.BlockSpec((tr, tc), lambda i, j, s: (i, j)),
        ),
        out_shape=jax.ShapeDtypeStruct((rows // 2, cols // 2), jnp.bfloat16),
        compiler_params=pltpu.CompilerParams(vmem_limit_bytes=48 << 20),
        cost_estimate=pl.CostEstimate(
            flops=2 * 2 * tokens * rows * cols // 4,
            bytes_accessed=2 * (tokens * rows + tokens * cols) + rows * cols // 2,
            transcendentals=0,
        ),
        name="wgrad",
    )(jnp.stack([row_half, col_half]).astype(jnp.int32), a0, b0, a1, b1)


def reduce_weight(pairs):
    fs, groups = lax.axis_size("fsdp"), lax.axis_size("dp") // 4
    x, z, g, y, c = coords()
    finals = []
    for left, right in pairs:
        far_left, far_right = flip_core(left), flip_core(right)
        send = wgrad(left, right, far_left, far_right, 1 - x, c)
        recv = flip_x(send)
        keep = wgrad(left, right, far_left, far_right, x, c)
        half_rows, half_cols = keep.shape
        q = half_rows // (fs * groups * 2)
        view = lambda a: a.reshape(fs, groups, 2, q, half_cols)
        at = lambda a, i, axis: lax.dynamic_index_in_dim(a, i, axis, keepdims=False)
        send_y = (
            at(view(keep), 1 - y, 2).astype(jnp.float32) + at(view(recv), 1 - y, 2).astype(jnp.float32)
        ).astype(jnp.bfloat16)
        recv_y = flip_y(send_y)

        def block(index):
            return (
                at(at(view(keep), y, 2), index, 0).astype(jnp.float32)
                + at(at(view(recv), y, 2), index, 0).astype(jnp.float32)
                + at(recv_y, index, 0).astype(jnp.float32)
            )

        total = block(z)
        for k in range(1, fs):
            total = total + shift_z(block((z + k) % fs).astype(jnp.bfloat16), k).astype(jnp.float32)
        mine = at(total, g, 0)
        for k in range(1, groups):
            mine = mine + shift_group(at(total, (g + k) % groups, 0), k)
        rows = q // 2
        near = lax.dynamic_slice_in_dim(mine, c * rows, rows, 0)
        far = flip_core(lax.dynamic_slice_in_dim(mine, (1 - c) * rows, rows, 0))
        finals.append(
            jnp.concatenate([jnp.where(c == 0, near, far), jnp.where(c == 0, far, near)], axis=1)
        )
    return jnp.stack(finals)


def local(
    image_in,
    text_in,
    modulation,
    text_len,
    w_qkv,
    b_qkv,
    w_out,
    b_out,
    w_up,
    b_up,
    w_down,
    b_down,
    d_image,
    d_text,
):
    x, z, g, y, c = coords()
    image_half, text_half = image_in.shape[1], text_in.shape[1]
    width = image_in.shape[2]
    text_rows = -(-2 * text_half // 16) * 16

    def take(arr):
        return lax.dynamic_index_in_dim(arr, x, 0, keepdims=False)

    def give(arr):
        return flip_x(lax.dynamic_index_in_dim(arr, 1 - x, 0, keepdims=False))

    def join(arr, rows):
        near, far = take(arr), give(arr)
        pad = jnp.zeros((rows - 2 * near.shape[0], width), near.dtype)
        return jnp.concatenate([near, far, pad], axis=0)

    def unjoin(arr, half, kind):
        near = arr[:half].astype(kind)
        far = flip_x(arr[half : 2 * half].astype(jnp.bfloat16)).astype(kind)
        return jnp.where(x == 0, jnp.stack([near, far]), jnp.stack([far, near]))

    streams = (join(image_in, 2 * image_half), join(text_in, text_rows))
    weight_qkv = gather_weight(w_qkv, True)
    small = lax.all_gather(
        jnp.concatenate([b_qkv, b_out, b_up, b_down], axis=1), "fsdp", axis=0, tiled=False
    )
    edges = [0]
    for b in (b_qkv, b_out, b_up, b_down):
        edges.append(edges[-1] + b.shape[1])
    biases = [
        small[:, :, edges[i] : edges[i + 1]].transpose(1, 0, 2).reshape(2, -1) for i in range(4)
    ]
    bias_qkv, bias_out, bias_up, bias_down = biases
    weight_out = gather_weight(w_out, False)
    weight_up = gather_weight(w_up, True)
    weight_down = gather_weight(w_down, False)
    cotangents = (join(d_image, 2 * image_half), join(d_text, text_rows))
    gains = take(modulation)
    info = jnp.stack([take(text_len), jnp.int32(text_half), x.astype(jnp.int32)])

    fronts = []
    for s in range(2):
        mod = gains[s]
        normed, inverse = normalize(streams[s].astype(jnp.float32))
        modded = (normed * (1.0 + mod[1]) + mod[0]).astype(jnp.bfloat16)
        projected = linear(modded, weight_qkv[s], bias_qkv[s]).astype(jnp.bfloat16)
        fronts.append((normed, inverse, modded, projected))
    att_i, att_t, lse = attn_fwd(fronts[0][3], fronts[1][3], info, tq=2 * image_half)
    attended = (att_i, att_t)
    outs, state = [], []
    for s in range(2):
        mod = gains[s]
        branch = linear(attended[s], weight_out[s], bias_out[s])
        middle = streams[s].astype(jnp.float32) + mod[2] * branch
        normed_two, inverse_two = normalize(middle)
        modded_two = (normed_two * (1.0 + mod[4]) + mod[3]).astype(jnp.bfloat16)
        hidden = linear(modded_two, weight_up[s], bias_up[s])
        active = gelu_tanh(hidden).astype(jnp.bfloat16)
        mlp_out = linear(active, weight_down[s], bias_down[s])
        outs.append((middle + mod[5] * mlp_out).astype(jnp.bfloat16))
        upstream = cotangents[s].astype(jnp.float32)
        d_gate_two = jnp.sum(upstream * mlp_out, axis=0)
        d_mlp = (mod[5] * upstream).astype(jnp.bfloat16)
        state.append((branch, normed_two, inverse_two, modded_two, hidden, active, upstream, d_gate_two, d_mlp))
    grads_down = reduce_weight([(state[s][5], state[s][8]) for s in range(2)])
    backs = []
    for s in range(2):
        mod = gains[s]
        branch, normed_two, inverse_two, modded_two, hidden, active, upstream, d_gate_two, d_mlp = state[s]
        d_active = linear_back(d_mlp, weight_down[s])
        d_hidden = jax.vjp(gelu_tanh, hidden)[1](d_active)[0].astype(jnp.bfloat16)
        d_modded_two = linear_back(d_hidden, weight_up[s])
        d_shift_two = jnp.sum(d_modded_two, axis=0)
        d_scale_two = jnp.sum(d_modded_two * normed_two, axis=0)
        d_middle = upstream + normalize_back(normed_two, inverse_two, d_modded_two * (1.0 + mod[4]))
        d_gate_one = jnp.sum(d_middle * branch, axis=0)
        d_branch = (mod[2] * d_middle).astype(jnp.bfloat16)
        d_attended = linear_back(d_branch, weight_out[s]).astype(jnp.bfloat16)
        backs.append((d_hidden, d_shift_two, d_scale_two, d_middle, d_gate_one, d_branch, d_attended))
    grads_up = reduce_weight([(state[s][3], backs[s][0]) for s in range(2)])
    grads_out = reduce_weight([(attended[s], backs[s][5]) for s in range(2)])
    d_front = attn_bwd(
        fronts[0][3], fronts[1][3], att_i, att_t, backs[0][6], backs[1][6], lse, info, tq=image_half
    )
    grads_qkv = reduce_weight([(fronts[s][2], d_front[s]) for s in range(2)])
    input_grads, gain_grads = [], []
    for s in range(2):
        mod = gains[s]
        normed, inverse, modded, _ = fronts[s]
        d_hidden, d_shift_two, d_scale_two, d_middle, d_gate_one, d_branch, _ = backs[s]
        d_modded = linear_back(d_front[s], weight_qkv[s])
        d_shift_one = jnp.sum(d_modded, axis=0)
        d_scale_one = jnp.sum(d_modded * normed, axis=0)
        input_grads.append(d_middle + normalize_back(normed, inverse, d_modded * (1.0 + mod[1])))
        gain_grads.append(
            jnp.stack([d_shift_one, d_scale_one, d_gate_one, d_shift_two, d_scale_two, state[s][7]])
        )
    mine = jnp.stack(gain_grads)
    theirs = flip_x(mine)
    grad_modulation = jnp.where(x == 0, jnp.stack([mine, theirs]), jnp.stack([theirs, mine]))

    axes = ("seq", "fsdp", "dp")
    count = lax.axis_size(axes)

    def bias_rows(right):
        total = jnp.stack([jnp.sum(r.astype(jnp.float32), axis=0) for r in right])
        return total.reshape(2, count, -1).transpose(1, 0, 2).reshape(count, -1)

    def reduce_bias(rights):
        rows = [bias_rows(r) for r in rights]
        cut = lax.psum_scatter(jnp.concatenate(rows, axis=1), axes, scatter_dimension=0, tiled=True)[0]
        result, start = [], 0
        for r in rows:
            result.append(cut[start : start + r.shape[1]].reshape(2, -1))
            start += r.shape[1]
        return result

    gb_out, gb_up, gb_down = reduce_bias(
        [[backs[s][5] for s in range(2)], [backs[s][0] for s in range(2)], [state[s][8] for s in range(2)]]
    )
    (gb_qkv,) = reduce_bias([d_front])
    return (
        unjoin(outs[0], image_half, jnp.bfloat16),
        unjoin(outs[1], text_half, jnp.bfloat16),
        unjoin(input_grads[0], image_half, jnp.float32),
        unjoin(input_grads[1], text_half, jnp.float32),
        grad_modulation,
        grads_qkv,
        gb_qkv,
        grads_out,
        gb_out,
        grads_up,
        gb_up,
        grads_down,
        gb_down,
    )


def solution(mesh):
    tokens = P(("fsdp", "dp"), "seq", None)
    weight, bias = P(None, "fsdp", None), P(None, "fsdp")
    in_specs = (tokens, tokens, P(("fsdp", "dp"), None, None, None), P(("fsdp", "dp")))
    in_specs += (weight, bias) * 4 + (tokens, tokens)
    grad_w, grad_b = P(None, ("seq", "fsdp", "dp"), None), P(None, ("seq", "fsdp", "dp"))
    out_specs = (tokens,) * 4 + (P(("fsdp", "dp"), None, None, None),) + (grad_w, grad_b) * 4
    return jax.shard_map(local, mesh=mesh, in_specs=in_specs, out_specs=out_specs, check_vma=False)
```

```python
import functools

import jax
import jax.numpy as jnp
from jax import lax
from jax.experimental import pallas as pl
from jax.experimental.pallas import tpu as pltpu
from jax.sharding import Mesh, PartitionSpec as P

EPSILON = 1e-06
HEAD_DIM=64
MASKED=-1000000000.0
def dot(a,b,ca,cb):
    return lax.dot_general(a,b,(((ca,),(cb,)),((),())),preferred_element_type=jnp.float32)

def attn_fwd_kernel(ti,tt,tq,len_ref,qi,ki,vi,qt,kt,vt,oi,ot,lse,ktp,vtp):
    tp=ktp.shape[0]
    ktp[...]=jnp.zeros_like(ktp); vtp[...]=jnp.zeros_like(vtp)
    ktp[:tt,:]=kt[...]; vtp[:tt,:]=vt[...]
    n_len=len_ref[0]; half=len_ref[1]; mine=len_ref[2]
    r=lax.broadcasted_iota(jnp.int32,(1,tp),1)
    pos=jnp.where(r<half,mine*half+r,(1-mine)*half+r-half)
    valid=(r<2*half)&(pos<n_len)
    lane=lax.broadcasted_iota(jnp.int32,(1,2*HEAD_DIM),1)
    k_img=ki[...]; v_img=vi[...]; k_txt=ktp[...]; v_txt=vtp[...]
    def one(q,rows):
        outs=[];lses=[]
        for h in range(2):
            qh=jnp.where((lane<HEAD_DIM)==(h==0),q.astype(jnp.float32)*(HEAD_DIM**-0.5),0.0).astype(jnp.bfloat16)
            s1=dot(qh,k_img,1,1); s2=dot(qh,k_txt,1,1)
            s2=jnp.where(valid,s2,MASKED)
            m=jnp.maximum(jnp.max(s1,axis=1,keepdims=True),jnp.max(s2,axis=1,keepdims=True))
            e1=jnp.exp(s1-m); e2=jnp.exp(s2-m)
            l=jnp.sum(e1,axis=1,keepdims=True)+jnp.sum(e2,axis=1,keepdims=True)
            inv=1.0/l
            o=dot((e1*inv).astype(jnp.bfloat16),v_img,1,0)+dot((e2*inv).astype(jnp.bfloat16),v_txt,1,0)
            outs.append(o); lses.append(m+jnp.log(l))
        o=jnp.where(lane<HEAD_DIM,outs[0],outs[1]).astype(jnp.bfloat16)
        both=jnp.where(lane<HEAD_DIM,jnp.broadcast_to(lses[0],(rows,128)),jnp.broadcast_to(lses[1],(rows,128)))
        return o,both.T
    def step(i,_):
        start=pl.multiple_of(i*tq,tq)
        o,b=one(qi[pl.ds(start,tq),:],tq)
        oi[pl.ds(start,tq),:]=o
        lse[0,0:1,pl.ds(start,tq)]=b[0:1]; lse[0,1:2,pl.ds(start,tq)]=b[64:65]
        return 0
    lax.fori_loop(0,ti//tq,step,0)
    qpad=jnp.concatenate([qt[...],jnp.zeros((tp-tt,128),jnp.bfloat16)],axis=0)
    o,b=one(qpad,tp)
    ot[...]=o[:tt]
    lse[0,0:1,ti:ti+tp]=b[0:1]; lse[0,1:2,ti:ti+tp]=b[64:65]

def attn_fwd(qkv_i,qkv_t,info,tq=256):
    ti,w3=qkv_i.shape; tt=qkv_t.shape[0]; w=w3//3; n=w//128; tp=256
    bi=lambda off: pl.BlockSpec((ti,128),lambda p,s,off=off:(0,p+off*n))
    bt=lambda off: pl.BlockSpec((tt,128),lambda p,s,off=off:(0,p+off*n))
    return pl.pallas_call(functools.partial(attn_fwd_kernel,ti,tt,tq),
        grid_spec=pltpu.PrefetchScalarGridSpec(num_scalar_prefetch=1,grid=(n,),
            in_specs=[bi(0),bi(1),bi(2),bt(0),bt(1),bt(2)],
            out_specs=[bi(0),bt(0),pl.BlockSpec((1,8,ti+tp),lambda p,s:(p,0,0))],
            scratch_shapes=[pltpu.VMEM((tp,128),jnp.bfloat16)]*2),
        out_shape=[jax.ShapeDtypeStruct((ti,w),jnp.bfloat16),jax.ShapeDtypeStruct((tt,w),jnp.bfloat16),
                   jax.ShapeDtypeStruct((n,8,ti+tp),jnp.float32)],
        compiler_params=pltpu.CompilerParams(vmem_limit_bytes=48<<20),
        cost_estimate=pl.CostEstimate(flops=8*(ti+tt)*(ti+tt)*w,bytes_accessed=8*(ti+tt)*w,transcendentals=2*n*(ti+tt)*(ti+tt)),
        name="attn_fwd")(info,qkv_i,qkv_i,qkv_i,qkv_t,qkv_t,qkv_t)

def attn_bwd_kernel(ti,tt,tq,len_ref,qi,ki,vi,qt,kt,vt,oi,ot,di,dt,lse,outi,outt,ktp,vtp,dk1,dk2,dv1,dv2,dqi,dqt):
    j=pl.program_id(1)
    tp=ktp.shape[0]
    @pl.when(j==0)
    def _():
        ktp[...]=jnp.zeros_like(ktp); vtp[...]=jnp.zeros_like(vtp)
        ktp[:tt,:]=kt[...]; vtp[:tt,:]=vt[...]
        n_len=len_ref[0]; half=len_ref[1]; mine=len_ref[2]
        r=lax.broadcasted_iota(jnp.int32,(tp,1),0)
        pos=jnp.where(r<half,mine*half+r,(1-mine)*half+r-half)
        valid=(r<2*half)&(pos<n_len)
        lane=lax.broadcasted_iota(jnp.int32,(1,128),1)
        sub=lax.broadcasted_iota(jnp.int32,(8,128),0); lane8=lax.broadcasted_iota(jnp.int32,(8,128),1)
        sel=jnp.where((lane8//HEAD_DIM)==sub,1.0,0.0).astype(jnp.bfloat16)
        k_img=ki[...]; v_img=vi[...]; k_txt=ktp[...]; v_txt=vtp[...]
        for ref in (dk1,dk2,dv1,dv2): ref[...]=jnp.zeros_like(ref)
        def one(q,do,o,ls):
            prod=do.astype(jnp.float32)*o.astype(jnp.float32)
            hi=prod.astype(jnp.bfloat16); lo=(prod-hi.astype(jnp.float32)).astype(jnp.bfloat16)
            dsum=dot(sel,hi,1,1)+dot(sel,lo,1,1)
            qs=(q.astype(jnp.float32)*(HEAD_DIM**-0.5))
            dof=do.astype(jnp.float32)
            dqs=[]
            for h in range(2):
                mk=(lane<HEAD_DIM)==(h==0)
                qh=jnp.where(mk,qs,0.0).astype(jnp.bfloat16)
                dh=jnp.where(mk,dof,0.0).astype(jnp.bfloat16)
                L=ls[h:h+1]; D=dsum[h:h+1]
                s1=dot(k_img,qh,1,1); s2=dot(k_txt,qh,1,1)
                p1=jnp.exp(s1-L); p2=jnp.where(valid,jnp.exp(s2-L),0.0)
                dp1=dot(v_img,dh,1,1); dp2=dot(v_txt,dh,1,1)
                ds1=(p1*(dp1-D)).astype(jnp.bfloat16); ds2=(p2*(dp2-D)).astype(jnp.bfloat16)
                dv1[...]+=dot(p1.astype(jnp.bfloat16),dh,1,0)
                dv2[...]+=dot(p2.astype(jnp.bfloat16),dh,1,0)
                dk1[...]+=dot(ds1,qh,1,0)
                dk2[...]+=dot(ds2,qh,1,0)
                dqs.append(dot(ds1,k_img,0,0)+dot(ds2,k_txt,0,0))
            return (jnp.where(lane<HEAD_DIM,dqs[0],dqs[1])*(HEAD_DIM**-0.5)).astype(jnp.bfloat16)
        def step(i,_):
            start=pl.multiple_of(i*tq,tq)
            sl=pl.ds(start,tq)
            dqi[sl,:]=one(qi[sl,:],di[sl,:],oi[sl,:],lse[0,:,sl])
            return 0
        lax.fori_loop(0,ti//tq,step,0)
        pad=lambda a: jnp.concatenate([a,jnp.zeros((tp-tt,128),jnp.bfloat16)],axis=0)
        dqt[...]=one(pad(qt[...]),pad(dt[...]),pad(ot[...]),lse[0,:,ti:ti+tp])[:tt]
        outi[...]=dqi[...]; outt[...]=dqt[...]
    @pl.when(j==1)
    def _():
        outi[...]=dk1[...].astype(jnp.bfloat16); outt[...]=dk2[:tt,:].astype(jnp.bfloat16)
    @pl.when(j==2)
    def _():
        outi[...]=dv1[...].astype(jnp.bfloat16); outt[...]=dv2[:tt,:].astype(jnp.bfloat16)

def attn_bwd(qkv_i,qkv_t,o_i,o_t,d_i,d_t,lse,info,tq=256):
    ti,w3=qkv_i.shape; tt=qkv_t.shape[0]; w=w3//3; n=w//128; tp=256
    bi=lambda off: pl.BlockSpec((ti,128),lambda p,j,s,off=off:(0,p+off*n))
    bt=lambda off: pl.BlockSpec((tt,128),lambda p,j,s,off=off:(0,p+off*n))
    return pl.pallas_call(functools.partial(attn_bwd_kernel,ti,tt,tq),
        grid_spec=pltpu.PrefetchScalarGridSpec(num_scalar_prefetch=1,grid=(n,3),
            in_specs=[bi(0),bi(1),bi(2),bt(0),bt(1),bt(2),bi(0),bt(0),bi(0),bt(0),pl.BlockSpec((1,8,ti+tp),lambda p,j,s:(p,0,0))],
            out_specs=[pl.BlockSpec((ti,128),lambda p,j,s:(0,p+j*n)),pl.BlockSpec((tt,128),lambda p,j,s:(0,p+j*n))],
            scratch_shapes=[pltpu.VMEM((tp,128),jnp.bfloat16)]*2+[pltpu.VMEM((ti,128),jnp.float32),pltpu.VMEM((tp,128),jnp.float32)]*2
              +[pltpu.VMEM((ti,128),jnp.bfloat16),pltpu.VMEM((tt,128),jnp.bfloat16)]),
        out_shape=[jax.ShapeDtypeStruct((ti,w3),jnp.bfloat16),jax.ShapeDtypeStruct((tt,w3),jnp.bfloat16)],
        compiler_params=pltpu.CompilerParams(vmem_limit_bytes=56<<20),
        cost_estimate=pl.CostEstimate(flops=20*(ti+tt)*(ti+tt)*w,bytes_accessed=16*(ti+tt)*w,transcendentals=2*n*(ti+tt)*(ti+tt)),
        name="attn_bwd")(info,qkv_i,qkv_i,qkv_i,qkv_t,qkv_t,qkv_t,o_i,o_t,d_i,d_t,lse)


def normalize(values):
    row_mean = jnp.mean(values, axis=-1, keepdims=True)
    centred = values - row_mean
    variance = jnp.mean(centred * centred, axis=-1, keepdims=True)
    inverse = lax.rsqrt(variance + EPSILON)
    return (centred * inverse, inverse)


def normalize_back(normed, inverse, upstream):
    mean_one = jnp.mean(upstream, axis=-1, keepdims=True)
    mean_two = jnp.mean(upstream * normed, axis=-1, keepdims=True)
    return inverse * (upstream - mean_one - normed * mean_two)


def linear(values, weight, offset):
    return jnp.dot(values, weight, preferred_element_type=jnp.float32) + offset.astype(jnp.float32)


def linear_back(upstream, weight):
    return dot(upstream, weight, 1, 1)


def gelu_tanh(values):
    return jax.nn.gelu(values, approximate=True)


DP = ("y", "core")


def coords():
    dp = lax.axis_index(DP)
    return lax.axis_index("seq"), lax.axis_index("fsdp"), dp // 4, (dp // 2) % 2, dp % 2


def flip_x(a):
    return lax.ppermute(a, "seq", [(0, 1), (1, 0)])


def flip_y(a):
    return lax.ppermute(a, DP, [(i, i ^ 2) for i in range(lax.axis_size(DP))])


def flip_core(a):
    return lax.ppermute(a, DP, [(i, i ^ 1) for i in range(lax.axis_size(DP))])


def shift_z(a, k):
    n = lax.axis_size("fsdp")
    return lax.ppermute(a, "fsdp", [(i, (i + k) % n) for i in range(n)])


def shift_group(a, k):
    n = lax.axis_size(DP)
    return lax.ppermute(a, DP, [(i, (i + 4 * k) % n) for i in range(n)])


def after(value, *earlier):
    return lax.optimization_barrier((value, *earlier))[0]


def enter(z_too=True, y_too=True, core_too=True):
    fs = lax.axis_size("fsdp")
    x, z, _, y, c = coords()
    targets = [{"seq": 1 - x}]
    if y_too:
        targets.append({"y": lax.axis_index("y") + 1 - 2 * y})
    if core_too:
        targets.append({"core": 1 - c})
    if z_too:
        targets += [{"fsdp": lax.rem(z + k, fs)} for k in range(1, fs)]
    barrier = pltpu.get_barrier_semaphore()
    for target in targets:
        pl.semaphore_signal(barrier, inc=1, device_id=target, device_id_type=pl.DeviceIdType.MESH)
    pl.semaphore_wait(barrier, len(targets))


def swap_copies(srcs, dsts, sems):
    x = lax.axis_index("seq")
    return [
        pltpu.make_async_remote_copy(
            src_ref=src,
            dst_ref=dst,
            send_sem=sems.at[i, 0],
            recv_sem=sems.at[i, 1],
            device_id={"seq": 1 - x},
            device_id_type=pl.DeviceIdType.MESH,
        )
        for i, (src, dst) in enumerate(zip(srcs, dsts))
    ]


def gather_weights(units, swaps, collective_id):
    fs = lax.axis_size("fsdp")
    count = len(units)
    kinds = ("first", "second", "core0", "forward", "core1", "core2", "core3")

    def kernel(*refs):
        n = count + len(swaps)
        shards, near, outs, far = refs[:count], refs[count:n], refs[n : n + count], refs[n + count : 2 * n]
        bufs = refs[2 * n : 2 * n + count]
        local_sem, send_sem, recv_sem, swap_sem = refs[2 * n + count :]
        x, z, _, y, c = coords()
        y_full = lax.axis_index("y")
        to_x, to_y, to_core = {"seq": 1 - x}, {"y": y_full + 1 - 2 * y}, {"core": 1 - c}
        enter()
        swapped = swap_copies(near, far, swap_sem)
        for cp in swapped:
            cp.start()

        def remote(src, dst, u, slot, target):
            return pltpu.make_async_remote_copy(
                src_ref=src,
                dst_ref=dst,
                send_sem=send_sem.at[u, slot],
                recv_sem=recv_sem.at[u, slot],
                device_id=target,
                device_id_type=pl.DeviceIdType.MESH,
            )

        def spot(u, from_z, dx, dy, cc):
            _, r, cols = units[u][0].shape
            q, h = r // 4, cols // 2
            xx = 1 - x if dx else x
            yy = 1 - y if dy else y
            row = pl.multiple_of(from_z * r + (xx * 2 + yy) * q, 16)
            return outs[u].at[pl.ds(row, q), pl.ds(pl.multiple_of(cc * h, 128), h)]

        def copy(u, kind, k):
            _, r, cols = units[u][0].shape
            q, h = r // 4, cols // 2
            if kind == "z":
                row = pl.multiple_of((x * 2 + y) * q, 16)
                src = shards[u].at[units[u][1], pl.ds(row, q), pl.ds(pl.multiple_of(c * h, 128), h)]
                return remote(src, spot(u, z, 0, 0, c), u, k - 1, {"fsdp": lax.rem(z + k, fs)})
            x_first = units[u][2]
            slot = (1 + kinds.index(kind)) * (fs - 1) + k - 1
            via = (1, 0) if x_first else (0, 1)
            other = (0, 1) if x_first else (1, 0)
            where, target = {
                "first": ((0, 0), to_x if x_first else to_y),
                "second": ((0, 0), to_y if x_first else to_x),
                "core0": ((0, 0), to_core),
                "forward": (via, to_y if x_first else to_x),
                "core1": (via, to_core),
                "core2": (other, to_core),
                "core3": ((1, 1), to_core),
            }[kind]
            place = spot(u, lax.rem(z - k + fs, fs), *where, c)
            return remote(place, place, u, slot, target)

        for u in range(count):
            pltpu.make_async_copy(shards[u].at[units[u][1]], bufs[u], local_sem.at[u, 0]).start()
            for k in range(1, fs):
                copy(u, "z", k).start()

        def own(u):
            r = units[u][0].shape[1]
            return pltpu.make_async_copy(
                bufs[u], outs[u].at[pl.ds(pl.multiple_of(z * r, 16), r), :], local_sem.at[u, 1]
            )

        for u in range(count):
            pltpu.make_async_copy(shards[u].at[units[u][1]], bufs[u], local_sem.at[u, 0]).wait()
            own(u).start()
        for t in range(count + 2):
            for u, arrived, send in (
                (t, "z", ("first", "second", "core0")),
                (t - 1, "first", ("forward", "core1")),
                (t - 2, "second", ("core2",)),
                (t - 2, "forward", ("core3",)),
            ):
                if not 0 <= u < count:
                    continue
                for k in range(1, fs):
                    copy(u, arrived, k).wait_recv()
                    for kind in send:
                        copy(u, kind, k).start()
        for u in range(count):
            for k in range(1, fs):
                for kind in ("core0", "core1", "core2", "core3"):
                    copy(u, kind, k).wait_recv()
                for kind in ("z",) + kinds:
                    copy(u, kind, k).wait_send()
            own(u).wait()
        for cp in swapped:
            cp.wait()

    total = sum(2 * u[0].shape[1] * fs * u[0].shape[2] for u in units)
    results = pl.pallas_call(
        kernel,
        out_shape=[jax.ShapeDtypeStruct((u[0].shape[1] * fs, u[0].shape[2]), u[0].dtype) for u in units]
        + [jax.ShapeDtypeStruct(a.shape, a.dtype) for a in swaps],
        in_specs=[pl.BlockSpec(memory_space=pl.ANY)] * (count + len(swaps)),
        out_specs=[pl.BlockSpec(memory_space=pl.ANY)] * (count + len(swaps)),
        scratch_shapes=[pltpu.VMEM(u[0].shape[1:], u[0].dtype) for u in units]
        + [
            pltpu.SemaphoreType.DMA((count, 2)),
            pltpu.SemaphoreType.DMA((count, 8 * (fs - 1))),
            pltpu.SemaphoreType.DMA((count, 8 * (fs - 1))),
            pltpu.SemaphoreType.DMA((max(len(swaps), 1), 2)),
        ],
        compiler_params=pltpu.CompilerParams(
            collective_id=collective_id, has_side_effects=True, vmem_limit_bytes=48 << 20
        ),
        cost_estimate=pl.CostEstimate(flops=0, bytes_accessed=8 * total, transcendentals=0),
        name="gather_weights",
    )(*[u[0] for u in units], *swaps)
    return results[:count], results[count:]


def reduce_weights(partials, units, swaps, collective_id):
    fs, groups = lax.axis_size("fsdp"), lax.axis_size(DP) // 4
    arrays = [p.reshape(2, fs, groups, 2, -1, p.shape[1]) for p in partials]
    count, held = len(units), len(arrays)

    def kernel(*refs):
        n = held + len(swaps)
        ins, near, outs, far = refs[:held], refs[held:n], refs[n : n + held], refs[n + held : 2 * n]
        scratch = refs[2 * n : 2 * n + 6 * count]
        load_sem, send_sem, recv_sem, swap_sem = refs[2 * n + 6 * count :]
        x, z, _, y, _ = coords()
        to_x, to_y = {"seq": 1 - x}, {"y": lax.axis_index("y") + 1 - 2 * y}
        enter(core_too=False)
        f32 = lambda a: a.astype(jnp.float32)

        def remote(u, slot, src, dst, target):
            return pltpu.make_async_remote_copy(
                src_ref=src,
                dst_ref=dst,
                send_sem=send_sem.at[u, slot],
                recv_sem=recv_sem.at[u, slot],
                device_id=target,
                device_id_type=pl.DeviceIdType.MESH,
            )

        def rows(u, k, mine):
            index, x_first, start, width = units[u]
            zz = lax.rem(z + k, fs)
            cols = pl.ds(start, width)
            if x_first:
                return ins[index].at[x if mine else 1 - x, zz, :, :, :, cols]
            return ins[index].at[:, zz, :, y if mine else 1 - y, :, cols]

        def load(u, k):
            return pltpu.make_async_copy(rows(u, k, True), scratch[6 * u].at[k - 1], load_sem.at[u, k - 1])

        def hop(u, stage, k):
            part, recv_one, send_two, recv_two, send_three, recv_three = scratch[6 * u : 6 * u + 6]
            x_first = units[u][1]
            if stage == 1:
                return remote(u, k - 1, rows(u, k, False), recv_one.at[k - 1], to_x if x_first else to_y)
            if stage == 2:
                return remote(u, fs + k - 1, send_two.at[k - 1], recv_two.at[k - 1], to_y if x_first else to_x)
            return remote(
                u, 2 * fs + k - 1, send_three.at[k - 1], recv_three.at[k - 1], {"fsdp": lax.rem(z + k, fs)}
            )

        def side(u, ref, k, mine):
            x_first = units[u][1]
            index = (y if mine else 1 - y) if x_first else (x if mine else 1 - x)
            return f32(ref[k - 1, :, index]) if x_first else f32(ref[k - 1, index])

        def second(u, k):
            part, recv_one, send_two = scratch[6 * u : 6 * u + 3]
            load(u, k).wait()
            hop(u, 1, k).wait_recv()
            send_two[k - 1] = (side(u, part, k, False) + side(u, recv_one, k, False)).astype(jnp.bfloat16)
            hop(u, 2, k).start()

        def third(u, k):
            part, recv_one, _, recv_two, send_three, _ = scratch[6 * u : 6 * u + 6]
            hop(u, 2, k).wait_recv()
            total = side(u, part, k, True) + side(u, recv_one, k, True) + f32(recv_two[k - 1])
            if k < fs:
                send_three[k - 1] = total.astype(jnp.bfloat16)
                hop(u, 3, k).start()
            else:
                index, _, start, width = units[u]
                outs[index][:, :, start : start + width] = total

        swapped = swap_copies(near, far, swap_sem)
        for k in range(1, fs + 1):
            for u in range(count):
                hop(u, 1, k).start()
                load(u, k).start()
        for cp in swapped:
            cp.start()
        for k in range(1, fs + 2):
            for u in range(count):
                if k <= fs:
                    second(u, k)
            for u in range(count):
                if k > 1:
                    third(u, k - 1)
        for u in range(count):
            index, _, start, width = units[u]
            total = outs[index][:, :, start : start + width]
            for k in range(1, fs):
                hop(u, 3, k).wait_recv()
                total = total + f32(scratch[6 * u + 5][k - 1])
            outs[index][:, :, start : start + width] = total
        for u in range(count):
            for k in range(1, fs + 1):
                for stage in (1, 2, 3) if k < fs else (1, 2):
                    hop(u, stage, k).wait_send()
        for cp in swapped:
            cp.wait()

    scratch = []
    for index, x_first, _, width in units:
        q = arrays[index].shape[4]
        both = (groups, 2, q, width) if x_first else (2, groups, q, width)
        for shape in ((fs, *both), (fs, *both)) + ((fs, groups, q, width),) * 2 + ((fs - 1, groups, q, width),) * 2:
            scratch.append(pltpu.VMEM(shape, jnp.bfloat16))
    results = pl.pallas_call(
        kernel,
        out_shape=[jax.ShapeDtypeStruct((groups, a.shape[4], a.shape[5]), jnp.float32) for a in arrays]
        + [jax.ShapeDtypeStruct(a.shape, a.dtype) for a in swaps],
        in_specs=[pl.BlockSpec(memory_space=pl.ANY)] * (held + len(swaps)),
        out_specs=[pl.BlockSpec(memory_space=pltpu.VMEM)] * held + [pl.BlockSpec(memory_space=pl.ANY)] * len(swaps),
        scratch_shapes=scratch
        + [
            pltpu.SemaphoreType.DMA((count, fs)),
            pltpu.SemaphoreType.DMA((count, 3 * fs)),
            pltpu.SemaphoreType.DMA((count, 3 * fs)),
            pltpu.SemaphoreType.DMA((max(len(swaps), 1), 2)),
        ],
        compiler_params=pltpu.CompilerParams(
            collective_id=collective_id, has_side_effects=True, vmem_limit_bytes=56 << 20
        ),
        cost_estimate=pl.CostEstimate(
            flops=0, bytes_accessed=8 * sum(p.size for p in partials), transcendentals=0
        ),
        name="reduce_weights",
    )(*arrays, *swaps)
    finals = []
    for total in results[:held]:
        g = lax.axis_index(DP) // 4
        at = lambda i: lax.dynamic_index_in_dim(total, i, 0, keepdims=False)
        mine = at(g)
        for k in range(1, groups):
            mine = mine + shift_group(at((g + k) % groups), k)
        finals.append(swap_halves(mine))
    return finals, results[held:]


def gather_offloaded(shard, stream, earlier=()):
    x, _, _, _, _ = coords()
    share = shard.shape[1] // (2 * lax.axis_size(DP))
    start = (x * lax.axis_size(DP) + lax.axis_index(DP)) * share
    piece = lax.dynamic_slice(shard, (stream, start, 0), (1, share, shard.shape[2]))[0]
    return lax.all_gather(after(piece, *earlier), ("fsdp", "seq", "y", "core"), axis=0, tiled=True)


def gather_plane(left, right):
    both = lax.all_gather(jnp.concatenate([left, right], axis=1), ("seq", "y", "core"), axis=0, tiled=True)
    return both[:, : left.shape[1]], both[:, left.shape[1] :]


def own_blocks(values, axis):
    fs, n = lax.axis_size("fsdp"), lax.axis_size(DP)
    lead, tail = values.shape[:axis], values.shape[axis + 1 :]
    split = values.reshape(*lead, 2, fs, n, -1, *tail)
    split = lax.dynamic_index_in_dim(split, lax.axis_index("seq"), axis, keepdims=False)
    split = lax.dynamic_index_in_dim(split, lax.axis_index(DP), axis + 1, keepdims=False)
    return split.reshape(*lead, -1, *tail)


def sum_fsdp(total):
    fs, z = lax.axis_size("fsdp"), lax.axis_index("fsdp")
    block = lambda i: lax.dynamic_index_in_dim(total, i, 0, keepdims=False)
    mine = block(z)
    for k in range(1, fs):
        mine = mine + shift_z(block((z + k) % fs).astype(jnp.bfloat16), k).astype(jnp.float32)
    return mine


def plane_grad(left, right):
    total = dot(own_blocks(left, 1), right, 0, 0)
    return sum_fsdp(total.reshape(lax.axis_size("fsdp"), -1, total.shape[1]))


def plane_mlp_grads(modded, d_mlp, weight_up, bias_up, weight_down):
    fs, n = lax.axis_size("fsdp"), lax.axis_size(DP)
    x = lax.axis_index("seq")
    hidden = linear(modded, own_blocks(weight_up, 1), own_blocks(bias_up, 0))
    active = gelu_tanh(hidden).astype(jnp.bfloat16)
    d_active = linear_back(d_mlp, own_blocks(weight_down, 0))
    d_hidden = jax.vjp(gelu_tanh, hidden)[1](d_active)[0].astype(jnp.bfloat16)
    down = dot(active, d_mlp, 0, 0)
    grad_down = sum_fsdp(down.reshape(fs, -1, down.shape[1]))
    up = dot(modded, d_hidden, 0, 0)
    rows, units = up.shape
    up = up.reshape(2, fs, rows // (2 * fs), units).transpose(1, 0, 2, 3)
    mine = sum_fsdp(up).reshape(rows // fs, units).astype(jnp.bfloat16)
    spread = lax.all_gather(mine, ("seq", "y", "core"), axis=0)
    spread = spread.reshape(2 * n, 2, n, rows // (2 * fs * n), units)
    spread = lax.dynamic_index_in_dim(spread, x, 1, keepdims=False)
    spread = lax.dynamic_index_in_dim(spread, lax.axis_index(DP), 1, keepdims=False)
    spread = spread.reshape(2, n, spread.shape[1], fs, -1).transpose(2, 0, 3, 1, 4)
    return grad_down, spread.reshape(spread.shape[0], -1).astype(jnp.float32)


def swap_halves(mine_rows):
    _, _, _, _, c = coords()
    rows = mine_rows.shape[0] // 2
    near = lax.dynamic_slice_in_dim(mine_rows, c * rows, rows, 0)
    far = flip_core(lax.dynamic_slice_in_dim(mine_rows, (1 - c) * rows, rows, 0))
    return jnp.concatenate([jnp.where(c == 0, near, far), jnp.where(c == 0, far, near)], axis=1)


def gather_small(value):
    fs = lax.axis_size("fsdp")
    z = lax.axis_index("fsdp")
    stack = jnp.stack([value] + [shift_z(value, k) for k in range(1, fs)])
    ordered = [lax.dynamic_index_in_dim(stack, (z - j) % fs, 0, keepdims=False) for j in range(fs)]
    return jnp.stack(ordered, axis=1)


def reduce_small(value):
    fs, groups = lax.axis_size("fsdp"), lax.axis_size(DP) // 4
    value = value + flip_core(value)
    value = value + flip_x(value)
    value = value + flip_y(value)
    value = value + sum(shift_z(value, k) for k in range(1, fs))
    if groups > 1:
        value = value + sum(shift_group(value, k) for k in range(1, groups))
    return value


def wgrad_kernel(sel_ref, a0, b0, a1, b1, out, a0t, a1t):
    @pl.when(pl.program_id(1) == 0)
    def _():
        a0t[...] = a0[...].T
        a1t[...] = a1[...].T

    out[...] = (dot(a0t[...], b0[...], 1, 0) + dot(a1t[...], b1[...], 1, 0)).astype(out.dtype)


def wgrad(a0, b0, a1, b1, row_half, col_half):
    tokens, rows = a0.shape
    cols = b0.shape[1]
    tr = tc = 768
    halves = 1 if row_half is None else 2
    nr, nc = rows // halves // tr, cols // 2 // tc
    row_start = jnp.int32(0) if row_half is None else row_half * nr
    a_spec = pl.BlockSpec((tokens, tr), lambda i, j, s: (0, s[0] + i))
    b_spec = pl.BlockSpec((tokens, tc), lambda i, j, s: (0, s[1] + j))
    return pl.pallas_call(
        wgrad_kernel,
        grid_spec=pltpu.PrefetchScalarGridSpec(
            num_scalar_prefetch=1,
            grid=(nr, nc),
            in_specs=[a_spec, b_spec, a_spec, b_spec],
            out_specs=pl.BlockSpec((tr, tc), lambda i, j, s: (i, j)),
            scratch_shapes=[pltpu.VMEM((tr, tokens), a0.dtype)] * 2,
        ),
        out_shape=jax.ShapeDtypeStruct((rows // halves, cols // 2), jnp.bfloat16),
        compiler_params=pltpu.CompilerParams(vmem_limit_bytes=48 << 20),
        cost_estimate=pl.CostEstimate(
            flops=2 * tokens * (rows // halves) * cols,
            bytes_accessed=2 * tokens * (rows + cols) + rows * cols,
            transcendentals=0,
        ),
        name="wgrad",
    )(jnp.stack([row_start, col_half * nc]).astype(jnp.int32), a0, b0, a1, b1)


def partial_grad(left, right, far_left, far_right):
    return wgrad(left, right, far_left, far_right, None, lax.axis_index("core"))


def local(
    image_in,
    text_in,
    modulation,
    text_len,
    w_qkv,
    b_qkv,
    w_out,
    b_out,
    w_up,
    b_up,
    w_down,
    b_down,
    d_image,
    d_text,
):
    x, z, g, y, c = coords()
    image_half, text_half = image_in.shape[1], text_in.shape[1]
    width = image_in.shape[2]
    text_rows = -(-2 * text_half // 16) * 16

    def take(arr, index=x):
        return lax.dynamic_index_in_dim(arr, index, 0, keepdims=False)

    def join(near, far, rows):
        pad = jnp.zeros((rows - 2 * near.shape[0], width), near.dtype)
        return jnp.concatenate([near, far, pad], axis=0)

    def in_order(near, far):
        return jnp.where(x == 0, jnp.stack([near, far]), jnp.stack([far, near]))

    gathered, far = gather_weights(
        [(w_qkv, 0, True), (w_qkv, 1, False)], [take(image_in, 1 - x), take(text_in, 1 - x)], 0
    )
    weight_qkv = gathered
    streams = (join(take(image_in), far[0], 2 * image_half), join(take(text_in), far[1], text_rows))
    text_weights = [gather_offloaded(w, 1, (weight_qkv[0],)) for w in (w_out, w_up, w_down)]
    image_weights, far = gather_weights(
        [(w_out, 0, True), (w_up, 0, False), (after(w_down, weight_qkv[0]), 0, True)],
        [take(d_image, 1 - x), take(d_text, 1 - x)],
        1,
    )
    cotangents = (join(take(d_image), far[0], 2 * image_half), join(take(d_text), far[1], text_rows))
    weight_out, weight_up, weight_down = zip(image_weights, text_weights)
    gains = take(modulation)
    info = jnp.stack([take(text_len), jnp.int32(text_half), x.astype(jnp.int32)])
    small = gather_small(jnp.concatenate([b_qkv, b_out, b_up, b_down], axis=1))
    biases, start = [], 0
    for b in (b_qkv, b_out, b_up, b_down):
        biases.append(small[:, :, start : start + b.shape[1]].reshape(2, -1).astype(jnp.float32))
        start += b.shape[1]
    bias_qkv, bias_out, bias_up, bias_down = biases

    fronts = []
    for s in range(2):
        mod = gains[s]
        normed, inverse = normalize(streams[s].astype(jnp.float32))
        modded = (normed * (1.0 + mod[1]) + mod[0]).astype(jnp.bfloat16)
        projected = linear(modded, weight_qkv[s], bias_qkv[s]).astype(jnp.bfloat16)
        fronts.append((normed, inverse, modded, projected))
    att_i, att_t, lse = attn_fwd(fronts[0][3], fronts[1][3], info, tq=2 * image_half)

    outs, backs, column_sums, parts = [], [], [], {}
    token = att_i
    for s in range(2):
        mod = gains[s]
        attended = after((att_i, att_t)[s], token)
        upstream = cotangents[s].astype(jnp.float32)
        d_mlp = (mod[5] * upstream).astype(jnp.bfloat16)
        branch = linear(attended, weight_out[s], bias_out[s])
        middle = streams[s].astype(jnp.float32) + mod[2] * branch
        normed_two, inverse_two = normalize(middle)
        modded_two = (normed_two * (1.0 + mod[4]) + mod[3]).astype(jnp.bfloat16)
        if s == 1:
            text_mlp = gather_plane(modded_two, d_mlp)
        hidden = linear(modded_two, weight_up[s], bias_up[s])
        active = gelu_tanh(hidden).astype(jnp.bfloat16)
        if s == 0:
            far_active, far_d_mlp = flip_core(active), flip_core(d_mlp)
        mlp_out = linear(active, weight_down[s], bias_down[s])
        outs.append((middle + mod[5] * mlp_out).astype(jnp.bfloat16))
        d_gate_two = jnp.sum(upstream * mlp_out, axis=0)
        if s == 0:
            parts["down"] = partial_grad(after(active, outs[s]), d_mlp, far_active, far_d_mlp)
            d_mlp = after(d_mlp, parts["down"])
        d_active = linear_back(d_mlp, weight_down[s])
        d_hidden = jax.vjp(gelu_tanh, hidden)[1](d_active)[0].astype(jnp.bfloat16)
        if s == 0:
            far_d_hidden, far_modded_two = flip_core(d_hidden), flip_core(modded_two)
        d_modded_two = linear_back(d_hidden, weight_up[s])
        d_shift_two = jnp.sum(d_modded_two, axis=0)
        d_scale_two = jnp.sum(d_modded_two * normed_two, axis=0)
        d_middle = upstream + normalize_back(normed_two, inverse_two, d_modded_two * (1.0 + mod[4]))
        d_gate_one = jnp.sum(d_middle * branch, axis=0)
        d_branch = (mod[2] * d_middle).astype(jnp.bfloat16)
        if s == 0:
            parts["up"] = partial_grad(after(modded_two, d_branch), d_hidden, far_modded_two, far_d_hidden)
            far_attended, far_d_branch = flip_core(attended), flip_core(d_branch)
            d_branch = after(d_branch, parts["up"])
        else:
            text_out = gather_plane(attended, d_branch)
        d_attended = linear_back(d_branch, weight_out[s]).astype(jnp.bfloat16)
        if s == 0:
            parts["out"] = partial_grad(after(attended, d_attended), d_branch, far_attended, far_d_branch)
            token = parts["out"]
        column_sums.append([jnp.sum(a.astype(jnp.float32), axis=0) for a in (d_branch, d_hidden, d_mlp)])
        backs.append((d_attended, d_middle, d_gate_one, d_shift_two, d_scale_two, d_gate_two))
    d_front = attn_bwd(
        fronts[0][3], fronts[1][3], att_i, att_t, backs[0][0], backs[1][0], lse, info, tq=image_half
    )
    text_qkv = gather_plane(fronts[1][2], d_front[1])
    far_front, far_modded = flip_core(d_front[0]), flip_core(fronts[0][2])
    sent = [outs[0][image_half:], outs[1][text_half : 2 * text_half]]
    reduced, far_outs = reduce_weights(
        [after(parts["down"], d_front[0]), parts["up"], parts["out"]],
        [(0, True, 0, parts["down"].shape[1]), (1, False, 0, parts["up"].shape[1]), (2, True, 0, parts["out"].shape[1])],
        sent,
        2,
    )
    grads = {("down", 0): reduced[0], ("up", 0): reduced[1], ("out", 0): reduced[2]}
    grads["down", 1], grads["up", 1] = plane_mlp_grads(*text_mlp, weight_up[1], bias_up[1], weight_down[1])
    grads["out", 1] = plane_grad(*text_out)
    input_grads, gain_grads = [], []
    for s in range(2):
        mod = gains[s]
        normed, inverse, modded, _ = fronts[s]
        d_attended, d_middle, d_gate_one, d_shift_two, d_scale_two, d_gate_two = backs[s]
        d_modded = linear_back(after(d_front[s], far_outs[0]), weight_qkv[s])
        d_shift_one = jnp.sum(d_modded, axis=0)
        d_scale_one = jnp.sum(d_modded * normed, axis=0)
        input_grads.append(d_middle + normalize_back(normed, inverse, d_modded * (1.0 + mod[1])))
        gain_grads.append(
            jnp.stack([d_shift_one, d_scale_one, d_gate_one, d_shift_two, d_scale_two, d_gate_two])
        )
    mine = jnp.stack(gain_grads)
    part = partial_grad(after(fronts[0][2], *input_grads), d_front[0], far_modded, far_front)
    cols = part.shape[1]
    sent = [input_grads[0][image_half:].astype(jnp.bfloat16), input_grads[1][text_half : 2 * text_half].astype(jnp.bfloat16)]
    reduced, far_grads = reduce_weights(
        [part], [(0, True, 0, cols // 2), (0, False, cols // 2, cols // 2)], sent + [mine.reshape(-1, width)], 3
    )
    grads["qkv", 0] = reduced[0]
    grads["qkv", 1] = plane_grad(*text_qkv)
    grad_modulation = in_order(mine, far_grads[2].reshape(mine.shape))

    count = lax.axis_size(("seq", "fsdp") + DP)
    index = lax.axis_index(("seq", "fsdp") + DP)

    def cut_bias(total):
        return lax.dynamic_index_in_dim(total.reshape(2, count, -1), index, 1, keepdims=False)

    sizes = [a.shape[0] for a in column_sums[0]]
    summed = reduce_small(jnp.stack([jnp.concatenate(column_sums[s]) for s in range(2)]))
    gb_out, gb_up, gb_down = [
        cut_bias(a) for a in jnp.split(summed, [sizes[0], sizes[0] + sizes[1]], axis=1)
    ]
    gb_qkv = cut_bias(reduce_small(jnp.stack([jnp.sum(d_front[s].astype(jnp.float32), axis=0) for s in range(2)])))
    grads_qkv, grads_out, grads_up, grads_down = [
        jnp.stack([grads[name, s] for s in range(2)]) for name in ("qkv", "out", "up", "down")
    ]
    halves = (image_half, text_half)
    return (
        *[in_order(outs[s][: halves[s]], far_outs[s]) for s in range(2)],
        *[in_order(input_grads[s][: halves[s]], far_grads[s].astype(jnp.float32)) for s in range(2)],
        grad_modulation,
        grads_qkv,
        gb_qkv,
        grads_out,
        gb_out,
        grads_up,
        gb_up,
        grads_down,
        gb_down,
    )


def solution(mesh):
    seq, fsdp, dp = (mesh.shape[name] for name in ("seq", "fsdp", "dp"))
    split = Mesh(mesh.devices.reshape(seq, fsdp, dp // 2, 2), ("seq", "fsdp", "y", "core"))
    batch = ("fsdp",) + DP
    tokens = P(batch, "seq", None)
    weight, bias = P(None, "fsdp", None), P(None, "fsdp")
    in_specs = (tokens, tokens, P(batch, None, None, None), P(batch))
    in_specs += (weight, bias) * 4 + (tokens, tokens)
    everywhere = ("seq",) + batch
    grad_w, grad_b = P(None, everywhere, None), P(None, everywhere)
    out_specs = (tokens,) * 4 + (P(batch, None, None, None),) + (grad_w, grad_b) * 4
    return jax.shard_map(local, mesh=split, in_specs=in_specs, out_specs=out_specs, check_vma=False)
```

```python
import functools

import jax
import jax.numpy as jnp
from jax import lax
from jax.experimental import pallas as pl
from jax.experimental.pallas import tpu as pltpu
from jax.sharding import Mesh, PartitionSpec as P

EPSILON = 1e-06
HEAD_DIM=64
MASKED=-1000000000.0
def dot(a,b,ca,cb):
    return lax.dot_general(a,b,(((ca,),(cb,)),((),())),preferred_element_type=jnp.float32)

def attn_fwd_kernel(ti,tt,tq,len_ref,qi,ki,vi,qt,kt,vt,oi,ot,lse,ktp,vtp):
    tp=ktp.shape[0]
    ktp[...]=jnp.zeros_like(ktp); vtp[...]=jnp.zeros_like(vtp)
    ktp[:tt,:]=kt[...]; vtp[:tt,:]=vt[...]
    n_len=len_ref[0]; half=len_ref[1]; mine=len_ref[2]
    r=lax.broadcasted_iota(jnp.int32,(1,tp),1)
    pos=jnp.where(r<half,mine*half+r,(1-mine)*half+r-half)
    valid=(r<2*half)&(pos<n_len)
    lane=lax.broadcasted_iota(jnp.int32,(1,2*HEAD_DIM),1)
    k_img=ki[...]; v_img=vi[...]; k_txt=ktp[...]; v_txt=vtp[...]
    def one(q,rows):
        outs=[];lses=[]
        for h in range(2):
            qh=jnp.where((lane<HEAD_DIM)==(h==0),q.astype(jnp.float32)*(HEAD_DIM**-0.5),0.0).astype(jnp.bfloat16)
            s1=dot(qh,k_img,1,1); s2=dot(qh,k_txt,1,1)
            s2=jnp.where(valid,s2,MASKED)
            m=jnp.maximum(jnp.max(s1,axis=1,keepdims=True),jnp.max(s2,axis=1,keepdims=True))
            e1=jnp.exp(s1-m); e2=jnp.exp(s2-m)
            l=jnp.sum(e1,axis=1,keepdims=True)+jnp.sum(e2,axis=1,keepdims=True)
            inv=1.0/l
            o=dot((e1*inv).astype(jnp.bfloat16),v_img,1,0)+dot((e2*inv).astype(jnp.bfloat16),v_txt,1,0)
            outs.append(o); lses.append(m+jnp.log(l))
        o=jnp.where(lane<HEAD_DIM,outs[0],outs[1]).astype(jnp.bfloat16)
        both=jnp.where(lane<HEAD_DIM,jnp.broadcast_to(lses[0],(rows,128)),jnp.broadcast_to(lses[1],(rows,128)))
        return o,both.T
    def step(i,_):
        start=pl.multiple_of(i*tq,tq)
        o,b=one(qi[pl.ds(start,tq),:],tq)
        oi[pl.ds(start,tq),:]=o
        lse[0,0:1,pl.ds(start,tq)]=b[0:1]; lse[0,1:2,pl.ds(start,tq)]=b[64:65]
        return 0
    lax.fori_loop(0,ti//tq,step,0)
    qpad=jnp.concatenate([qt[...],jnp.zeros((tp-tt,128),jnp.bfloat16)],axis=0)
    o,b=one(qpad,tp)
    ot[...]=o[:tt]
    lse[0,0:1,ti:ti+tp]=b[0:1]; lse[0,1:2,ti:ti+tp]=b[64:65]

def attn_bwd_kernel(ti,tt,tq,len_ref,qi,ki,vi,qt,kt,vt,oi,ot,di,dt,lse,outi,outt,ktp,vtp,dk1,dk2,dv1,dv2,dqi,dqt):
    j=pl.program_id(1)
    tp=ktp.shape[0]
    @pl.when(j==0)
    def _():
        ktp[...]=jnp.zeros_like(ktp); vtp[...]=jnp.zeros_like(vtp)
        ktp[:tt,:]=kt[...]; vtp[:tt,:]=vt[...]
        n_len=len_ref[0]; half=len_ref[1]; mine=len_ref[2]
        r=lax.broadcasted_iota(jnp.int32,(tp,1),0)
        pos=jnp.where(r<half,mine*half+r,(1-mine)*half+r-half)
        valid=(r<2*half)&(pos<n_len)
        lane=lax.broadcasted_iota(jnp.int32,(1,128),1)
        sub=lax.broadcasted_iota(jnp.int32,(8,128),0); lane8=lax.broadcasted_iota(jnp.int32,(8,128),1)
        sel=jnp.where((lane8//HEAD_DIM)==sub,1.0,0.0).astype(jnp.bfloat16)
        k_img=ki[...]; v_img=vi[...]; k_txt=ktp[...]; v_txt=vtp[...]
        for ref in (dk1,dk2,dv1,dv2): ref[...]=jnp.zeros_like(ref)
        def one(q,do,o,ls):
            prod=do.astype(jnp.float32)*o.astype(jnp.float32)
            hi=prod.astype(jnp.bfloat16); lo=(prod-hi.astype(jnp.float32)).astype(jnp.bfloat16)
            dsum=dot(sel,hi,1,1)+dot(sel,lo,1,1)
            qs=(q.astype(jnp.float32)*(HEAD_DIM**-0.5))
            dof=do.astype(jnp.float32)
            dqs=[]
            for h in range(2):
                mk=(lane<HEAD_DIM)==(h==0)
                qh=jnp.where(mk,qs,0.0).astype(jnp.bfloat16)
                dh=jnp.where(mk,dof,0.0).astype(jnp.bfloat16)
                L=ls[h:h+1]; D=dsum[h:h+1]
                s1=dot(k_img,qh,1,1); s2=dot(k_txt,qh,1,1)
                p1=jnp.exp(s1-L); p2=jnp.where(valid,jnp.exp(s2-L),0.0)
                dp1=dot(v_img,dh,1,1); dp2=dot(v_txt,dh,1,1)
                ds1=(p1*(dp1-D)).astype(jnp.bfloat16); ds2=(p2*(dp2-D)).astype(jnp.bfloat16)
                dv1[...]+=dot(p1.astype(jnp.bfloat16),dh,1,0)
                dv2[...]+=dot(p2.astype(jnp.bfloat16),dh,1,0)
                dk1[...]+=dot(ds1,qh,1,0)
                dk2[...]+=dot(ds2,qh,1,0)
                dqs.append(dot(ds1,k_img,0,0)+dot(ds2,k_txt,0,0))
            return (jnp.where(lane<HEAD_DIM,dqs[0],dqs[1])*(HEAD_DIM**-0.5)).astype(jnp.bfloat16)
        def step(i,_):
            start=pl.multiple_of(i*tq,tq)
            sl=pl.ds(start,tq)
            dqi[sl,:]=one(qi[sl,:],di[sl,:],oi[sl,:],lse[0,:,sl])
            return 0
        lax.fori_loop(0,ti//tq,step,0)
        pad=lambda a: jnp.concatenate([a,jnp.zeros((tp-tt,128),jnp.bfloat16)],axis=0)
        dqt[...]=one(pad(qt[...]),pad(dt[...]),pad(ot[...]),lse[0,:,ti:ti+tp])[:tt]
        outi[...]=dqi[...]; outt[...]=dqt[...]
    @pl.when(j==1)
    def _():
        outi[...]=dk1[...].astype(jnp.bfloat16); outt[...]=dk2[:tt,:].astype(jnp.bfloat16)
    @pl.when(j==2)
    def _():
        outi[...]=dv1[...].astype(jnp.bfloat16); outt[...]=dv2[:tt,:].astype(jnp.bfloat16)


def normalize(values):
    row_mean = jnp.mean(values, axis=-1, keepdims=True)
    centred = values - row_mean
    variance = jnp.mean(centred * centred, axis=-1, keepdims=True)
    inverse = lax.rsqrt(variance + EPSILON)
    return (centred * inverse, inverse)


def normalize_back(normed, inverse, upstream):
    mean_one = jnp.mean(upstream, axis=-1, keepdims=True)
    mean_two = jnp.mean(upstream * normed, axis=-1, keepdims=True)
    return inverse * (upstream - mean_one - normed * mean_two)


def linear(values, weight, offset):
    return jnp.dot(values, weight, preferred_element_type=jnp.float32) + offset.astype(jnp.float32)


def linear_back(upstream, weight):
    return dot(upstream, weight, 1, 1)


def gelu_both(values):
    inner = jnp.tanh(0.7978845608028654 * values * (1.0 + 0.044715 * values * values))
    half = 0.5 * (1.0 + inner)
    slope = half + 0.5 * values * (1.0 - inner * inner) * (0.7978845608028654 * (1.0 + 0.134145 * values * values))
    return (values * half).astype(jnp.bfloat16), slope.astype(jnp.bfloat16)


DP = ("y", "core")


def coords():
    dp = lax.axis_index(DP)
    return lax.axis_index("seq"), lax.axis_index("fsdp"), dp // 4, (dp // 2) % 2, dp % 2


def flip_x(a):
    return lax.ppermute(a, "seq", [(0, 1), (1, 0)])


def flip_y(a):
    return lax.ppermute(a, DP, [(i, i ^ 2) for i in range(lax.axis_size(DP))])


def flip_core(a):
    return lax.ppermute(a, DP, [(i, i ^ 1) for i in range(lax.axis_size(DP))])


def shift_z(a, k):
    n = lax.axis_size("fsdp")
    return lax.ppermute(a, "fsdp", [(i, (i + k) % n) for i in range(n)])


def shift_group(a, k):
    n = lax.axis_size(DP)
    return lax.ppermute(a, DP, [(i, (i + 4 * k) % n) for i in range(n)])


def after(value, *earlier):
    return lax.optimization_barrier((value, *earlier))[0]


def enter(z_too=True, y_too=True, core_too=True):
    fs = lax.axis_size("fsdp")
    x, z, _, y, c = coords()
    targets = [{"seq": 1 - x}]
    if y_too:
        targets.append({"y": lax.axis_index("y") + 1 - 2 * y})
    if core_too:
        targets.append({"core": 1 - c})
    if z_too:
        targets += [{"fsdp": lax.rem(z + k, fs)} for k in range(1, fs)]
    barrier = pltpu.get_barrier_semaphore()
    for target in targets:
        pl.semaphore_signal(barrier, inc=1, device_id=target, device_id_type=pl.DeviceIdType.MESH)
    pl.semaphore_wait(barrier, len(targets))


def swap_copies(srcs, dsts, sems):
    x = lax.axis_index("seq")
    return [
        pltpu.make_async_remote_copy(
            src_ref=src,
            dst_ref=dst,
            send_sem=sems.at[i, 0],
            recv_sem=sems.at[i, 1],
            device_id={"seq": 1 - x},
            device_id_type=pl.DeviceIdType.MESH,
        )
        for i, (src, dst) in enumerate(zip(srcs, dsts))
    ]


def gather_plan(units, shards, outs, bufs, local_sem, send_sem, recv_sem):
    fs = lax.axis_size("fsdp")
    count = len(units)
    kinds = ("first", "second", "core0", "forward", "core1", "core2", "core3")
    x, z, _, y, c = coords()
    to_x, to_y, to_core = {"seq": 1 - x}, {"y": lax.axis_index("y") + 1 - 2 * y}, {"core": 1 - c}

    def remote(src, dst, u, slot, target):
        return pltpu.make_async_remote_copy(
            src_ref=src,
            dst_ref=dst,
            send_sem=send_sem.at[u, slot],
            recv_sem=recv_sem.at[u, slot],
            device_id=target,
            device_id_type=pl.DeviceIdType.MESH,
        )

    def spot(u, from_z, dx, dy, cc):
        _, r, cols = units[u][0].shape
        q, h = r // 4, cols // 2
        xx = 1 - x if dx else x
        yy = 1 - y if dy else y
        row = pl.multiple_of(from_z * r + (xx * 2 + yy) * q, 16)
        return outs[u].at[pl.ds(row, q), pl.ds(pl.multiple_of(cc * h, 128), h)]

    def copy(u, kind, k):
        _, r, cols = units[u][0].shape
        q, h = r // 4, cols // 2
        if kind == "z":
            dst = spot(u, lax.rem(z - k + 1 + fs, fs), 0, 0, c)
            row = pl.multiple_of((x * 2 + y) * q, 16)
            own_piece = shards[u].at[units[u][1], pl.ds(row, q), pl.ds(pl.multiple_of(c * h, 128), h)]
            return remote(own_piece if k == 1 else dst, dst, u, k - 1, {"fsdp": lax.rem(z + 1, fs)})
        x_first = units[u][2]
        slot = (1 + kinds.index(kind)) * (fs - 1) + k - 1
        via = (1, 0) if x_first else (0, 1)
        other = (0, 1) if x_first else (1, 0)
        where, target = {
            "first": ((0, 0), to_x if x_first else to_y),
            "second": ((0, 0), to_y if x_first else to_x),
            "core0": ((0, 0), to_core),
            "forward": (via, to_y if x_first else to_x),
            "core1": (via, to_core),
            "core2": (other, to_core),
            "core3": ((1, 1), to_core),
        }[kind]
        place = spot(u, lax.rem(z - k + fs, fs), *where, c)
        return remote(place, place, u, slot, target)

    def fetch(u):
        return pltpu.make_async_copy(shards[u].at[units[u][1]], bufs[u], local_sem.at[u, 0])

    def own(u):
        r = units[u][0].shape[1]
        return pltpu.make_async_copy(
            bufs[u], outs[u].at[pl.ds(pl.multiple_of(z * r, 16), r), :], local_sem.at[u, 1]
        )

    ahead = min(2, count)
    order = [(u, k) for k in range(1, fs) for u in range(count)]

    def begin():
        for u, k in order[:ahead]:
            copy(u, "z", k).start()
        for u in range(count):
            fetch(u).start()
        for u in range(count):
            fetch(u).wait()
            own(u).start()

    def act(i):
        if i < len(order):
            u, k = order[i]
            copy(u, "z", k).wait_recv()
            if i + ahead < len(order):
                copy(order[i + ahead][0], "z", order[i + ahead][1]).start()
            for kind in ("first", "second", "core0"):
                copy(u, kind, k).start()
        if 0 <= i - lag < len(order):
            u, k = order[i - lag]
            copy(u, "first", k).wait_recv()
            copy(u, "forward", k).start()
            copy(u, "core1", k).start()
        if 0 <= i - 2 * lag < len(order):
            u, k = order[i - 2 * lag]
            copy(u, "second", k).wait_recv()
            copy(u, "core2", k).start()
            copy(u, "forward", k).wait_recv()
            copy(u, "core3", k).start()

    lag = 2
    actions = [functools.partial(act, i) for i in range(len(order) + 2 * lag)]

    def end():
        for u in range(count):
            for k in range(1, fs):
                for kind in ("core0", "core1", "core2", "core3"):
                    copy(u, kind, k).wait_recv()
                for kind in ("z",) + kinds:
                    copy(u, kind, k).wait_send()
            own(u).wait()

    return begin, actions, end


def gather_shapes(units):
    fs = lax.axis_size("fsdp")
    return [jax.ShapeDtypeStruct((u[0].shape[1] * fs, u[0].shape[2]), u[0].dtype) for u in units]


def gather_scratch(units, swaps):
    fs = lax.axis_size("fsdp")
    return [pltpu.VMEM(u[0].shape[1:], u[0].dtype) for u in units] + [
        pltpu.SemaphoreType.DMA((len(units), 2)),
        pltpu.SemaphoreType.DMA((len(units), 8 * (fs - 1))),
        pltpu.SemaphoreType.DMA((len(units), 8 * (fs - 1))),
        pltpu.SemaphoreType.DMA((max(len(swaps), 1), 2)),
    ]


def gather_weights(units, swaps, collective_id):
    count, n = len(units), len(units) + len(swaps)

    def kernel(*refs):
        shards, near, outs, far = refs[:count], refs[count:n], refs[n : n + count], refs[n + count : 2 * n]
        enter()
        swapped = swap_copies(near, far, refs[-1])
        for cp in swapped:
            cp.start()
        begin, actions, end = gather_plan(units, shards, outs, refs[2 * n : 2 * n + count], *refs[-4:-1])
        begin()
        for action in actions:
            action()
        end()
        for cp in swapped:
            cp.wait()

    results = pl.pallas_call(
        kernel,
        out_shape=gather_shapes(units) + [jax.ShapeDtypeStruct(a.shape, a.dtype) for a in swaps],
        in_specs=[pl.BlockSpec(memory_space=pl.ANY)] * n,
        out_specs=[pl.BlockSpec(memory_space=pl.ANY)] * n,
        scratch_shapes=gather_scratch(units, swaps),
        compiler_params=pltpu.CompilerParams(
            collective_id=collective_id, has_side_effects=True, vmem_limit_bytes=48 << 20
        ),
        name="gather_weights",
    )(*[u[0] for u in units], *swaps)
    return results[:count], results[count:]


def attend_and_gather(qkv_i, qkv_t, info, tq, units, swaps, collective_id):
    ti, w3 = qkv_i.shape
    tt, w, tp = qkv_t.shape[0], w3 // 3, 256
    steps = w // 128
    count, n = len(units), len(units) + len(swaps)
    bi = lambda off: pl.BlockSpec((ti, 128), lambda p, s, off=off: (0, p + off * steps))
    bt = lambda off: pl.BlockSpec((tt, 128), lambda p, s, off=off: (0, p + off * steps))

    def kernel(*refs):
        info_ref, attn_in = refs[0], refs[1:7]
        shards, near = refs[7 : 7 + count], refs[7 + count : 7 + n]
        attn_out, rest = refs[7 + n : 10 + n], refs[10 + n :]
        outs, far, pads = rest[:count], rest[count:n], rest[n : n + 2]
        step = pl.program_id(0)
        swapped = swap_copies(near, far, refs[-1])
        begin, actions, end = gather_plan(units, shards, outs, rest[n + 2 : n + 2 + count], *refs[-4:-1])

        @pl.when(step == 0)
        def _():
            enter()
            begin()
            for cp in swapped:
                cp.start()

        early = min(steps - 2, len(actions))
        for index in range(early):
            pl.when(step == index + 2)(actions[index])
        attn_fwd_kernel(ti, tt, tq, info_ref, *attn_in, *attn_out, *pads)

        @pl.when(step == steps - 1)
        def _():
            for action in actions[early:]:
                action()
            end()
            for cp in swapped:
                cp.wait()

    results = pl.pallas_call(
        kernel,
        grid_spec=pltpu.PrefetchScalarGridSpec(
            num_scalar_prefetch=1,
            grid=(steps,),
            in_specs=[bi(0), bi(1), bi(2), bt(0), bt(1), bt(2)] + [pl.BlockSpec(memory_space=pl.ANY)] * n,
            out_specs=[bi(0), bt(0), pl.BlockSpec((1, 8, ti + tp), lambda p, s: (p, 0, 0))]
            + [pl.BlockSpec(memory_space=pl.ANY)] * n,
            scratch_shapes=[pltpu.VMEM((tp, 128), jnp.bfloat16)] * 2 + gather_scratch(units, swaps),
        ),
        out_shape=[
            jax.ShapeDtypeStruct((ti, w), jnp.bfloat16),
            jax.ShapeDtypeStruct((tt, w), jnp.bfloat16),
            jax.ShapeDtypeStruct((steps, 8, ti + tp), jnp.float32),
        ]
        + gather_shapes(units)
        + [jax.ShapeDtypeStruct(a.shape, a.dtype) for a in swaps],
        compiler_params=pltpu.CompilerParams(
            collective_id=collective_id, has_side_effects=True, vmem_limit_bytes=56 << 20
        ),
        name="attend_and_gather",
    )(info, qkv_i, qkv_i, qkv_i, qkv_t, qkv_t, qkv_t, *[u[0] for u in units], *swaps)
    return results[:3], results[3 : 3 + count], results[3 + count :]


def reduce_plan(units, ins, outs, scratch, totals, load_sem, send_sem, recv_sem, out_sem):
    fs = lax.axis_size("fsdp")
    count = len(units)
    x, z, _, y, _ = coords()
    to_x, to_y = {"seq": 1 - x}, {"y": lax.axis_index("y") + 1 - 2 * y}
    f32 = lambda a: a.astype(jnp.float32)

    def remote(u, slot, src, dst, target):
        return pltpu.make_async_remote_copy(
            src_ref=src,
            dst_ref=dst,
            send_sem=send_sem.at[u, slot],
            recv_sem=recv_sem.at[u, slot],
            device_id=target,
            device_id_type=pl.DeviceIdType.MESH,
        )

    def rows(u, k, mine):
        index, x_first, start, width = units[u]
        zz = lax.rem(z + k, fs)
        cols = pl.ds(start, width)
        if x_first:
            return ins[index].at[x if mine else 1 - x, zz, :, :, :, cols]
        return ins[index].at[:, zz, :, y if mine else 1 - y, :, cols]

    def load(u, k):
        return pltpu.make_async_copy(rows(u, k, True), scratch[4 * u].at[k - 1], load_sem.at[u, k - 1])

    def side(u, ref, k, mine):
        x_first = units[u][1]
        index = (y if mine else 1 - y) if x_first else (x if mine else 1 - x)
        return ref.at[k - 1, :, index] if x_first else ref.at[k - 1, index]

    def hop(u, stage, k):
        part, recv_one, recv_two, recv_three = scratch[4 * u : 4 * u + 4]
        x_first = units[u][1]
        if stage == 1:
            return remote(u, k - 1, rows(u, k, False), recv_one.at[k - 1], to_x if x_first else to_y)
        if stage == 2:
            return remote(u, fs + k - 1, side(u, part, k, False), recv_two.at[k - 1], to_y if x_first else to_x)
        return remote(
            u, 2 * fs + k - 1, recv_two.at[k - 1], recv_three.at[k - 1], {"fsdp": lax.rem(z + k, fs)}
        )

    def second(u, k):
        part, recv_one = scratch[4 * u : 4 * u + 2]
        load(u, k).wait()
        if k + ahead > fs:
            hop(u, 1, k).wait_recv()
        spot = side(u, part, k, False)
        spot[...] = (f32(spot[...]) + f32(side(u, recv_one, k, False)[...])).astype(jnp.bfloat16)
        hop(u, 2, k).start()

    def third(u, k):
        part, recv_one, recv_two = scratch[4 * u : 4 * u + 3]
        hop(u, 2, k).wait_recv()
        total = f32(side(u, part, k, True)[...]) + f32(side(u, recv_one, k, True)[...]) + f32(recv_two[k - 1])
        if k < fs:
            recv_two[k - 1] = total.astype(jnp.bfloat16)
            hop(u, 3, k).start()
        else:
            index, _, start, width = units[u]
            totals[index][:, :, start : start + width] = total

    ahead = 2

    def begin():
        for k in range(1, fs + 1):
            for u in range(count):
                if k <= ahead:
                    hop(u, 1, k).start()
                load(u, k).start()

    def stage(k):
        if k + ahead <= fs:
            for u in range(count):
                hop(u, 1, k).wait_recv()
            for u in range(count):
                hop(u, 1, k + ahead).start()
        for u in range(count):
            if k <= fs:
                second(u, k)
        for u in range(count):
            if k > 1:
                third(u, k - 1)

    actions = [functools.partial(stage, k) for k in range(1, fs + 2)]

    def end():
        for u in range(count):
            index, _, start, width = units[u]
            total = totals[index][:, :, start : start + width]
            for k in range(1, fs):
                hop(u, 3, k).wait_recv()
                total = total + f32(scratch[4 * u + 3][k - 1])
            totals[index][:, :, start : start + width] = total
        stores = [pltpu.make_async_copy(totals[i], outs[i], out_sem.at[i]) for i in range(len(outs))]
        for cp in stores:
            cp.start()
        for u in range(count):
            for k in range(1, fs + 1):
                for number in (1, 2, 3) if k < fs else (1, 2):
                    hop(u, number, k).wait_send()
        for cp in stores:
            cp.wait()

    return begin, actions, end


def reduce_views(partials):
    fs, groups = lax.axis_size("fsdp"), lax.axis_size(DP) // 4
    return [p.reshape(2, fs, groups, 2, -1, p.shape[1]) for p in partials]


def reduce_scratch(arrays, units, swaps):
    fs, groups = lax.axis_size("fsdp"), lax.axis_size(DP) // 4
    scratch = []
    for index, x_first, _, width in units:
        q = arrays[index].shape[4]
        both = (groups, 2, q, width) if x_first else (2, groups, q, width)
        for shape in ((fs, *both), (fs, *both), (fs, groups, q, width), (fs - 1, groups, q, width)):
            scratch.append(pltpu.VMEM(shape, jnp.bfloat16))
    scratch += [pltpu.VMEM((groups, a.shape[4], a.shape[5]), jnp.float32) for a in arrays]
    return scratch + [
        pltpu.SemaphoreType.DMA((len(units), fs)),
        pltpu.SemaphoreType.DMA((len(units), 3 * fs)),
        pltpu.SemaphoreType.DMA((len(units), 3 * fs)),
        pltpu.SemaphoreType.DMA((len(arrays),)),
        pltpu.SemaphoreType.DMA((max(len(swaps), 1), 2)),
    ]


def reduce_shapes(arrays, swaps):
    groups = lax.axis_size(DP) // 4
    return [jax.ShapeDtypeStruct((groups, a.shape[4], a.shape[5]), jnp.float32) for a in arrays] + [
        jax.ShapeDtypeStruct(a.shape, a.dtype) for a in swaps
    ]


def finish_reduce(results):
    finals = []
    for total in results:
        groups, g = total.shape[0], lax.axis_index(DP) // 4
        at = lambda i: lax.dynamic_index_in_dim(total, i, 0, keepdims=False)
        mine = at(g)
        for k in range(1, groups):
            mine = mine + shift_group(at((g + k) % groups), k)
        finals.append(swap_halves(mine))
    return finals


def reduce_weights(partials, units, swaps, small, collective_id):
    fs, groups = lax.axis_size("fsdp"), lax.axis_size(DP) // 4
    arrays = reduce_views(partials)
    held = len(arrays)
    n, size = held + len(swaps), 4 * len(units)
    hops = 3 + fs - 1

    def kernel(*refs):
        ins, near, small_in = refs[:held], refs[held:n], refs[n]
        outs, far, small_out = refs[n + 1 : n + 1 + held], refs[n + 1 + held : 2 * n + 1], refs[2 * n + 1]
        rest = refs[2 * n + 2 :]
        scratch, totals = rest[:size], rest[size : size + held]
        staged, landed, small_sem = rest[size + held : size + held + 3]
        x, z, _, y, c = coords()
        enter()
        begin, actions, end = reduce_plan(units, ins, outs, scratch, totals, *refs[-5:-1])
        swapped = swap_copies(near, far, refs[-1])
        targets = [{"core": 1 - c}, {"seq": 1 - x}, {"y": lax.axis_index("y") + 1 - 2 * y}]
        targets += [{"fsdp": lax.rem(z + k, fs)} for k in range(1, fs)]

        def small_hop(i):
            return pltpu.make_async_remote_copy(
                src_ref=staged.at[min(i, 3)],
                dst_ref=landed.at[i],
                send_sem=small_sem.at[0, i],
                recv_sem=small_sem.at[1, i],
                device_id=targets[i],
                device_id_type=pl.DeviceIdType.MESH,
            )

        staged[0] = small_in[...]
        small_hop(0).start()
        begin()
        for cp in swapped:
            cp.start()
        for index, action in enumerate(actions):
            action()
            if index < 3:
                small_hop(index).wait_recv()
                staged[index + 1] = staged[index] + landed[index]
                for i in (index + 1,) if index < 2 else range(3, hops):
                    small_hop(i).start()
        end()
        total = staged[3]
        for i in range(3, hops):
            small_hop(i).wait_recv()
            total = total + landed[i]
        small_out[...] = total
        for i in range(hops):
            small_hop(i).wait_send()
        for cp in swapped:
            cp.wait()

    results = pl.pallas_call(
        kernel,
        out_shape=reduce_shapes(arrays, swaps) + [jax.ShapeDtypeStruct(small.shape, small.dtype)],
        in_specs=[pl.BlockSpec(memory_space=pl.ANY)] * n + [pl.BlockSpec(memory_space=pltpu.VMEM)],
        out_specs=[pl.BlockSpec(memory_space=pl.ANY)] * n + [pl.BlockSpec(memory_space=pltpu.VMEM)],
        scratch_shapes=(lambda base: base[: size + held]
        + [
            pltpu.VMEM((4, *small.shape), small.dtype),
            pltpu.VMEM((hops, *small.shape), small.dtype),
            pltpu.SemaphoreType.DMA((2, hops)),
        ]
        + base[size + held :])(reduce_scratch(arrays, units, swaps)),
        compiler_params=pltpu.CompilerParams(
            collective_id=collective_id, has_side_effects=True, vmem_limit_bytes=56 << 20
        ),
        name="reduce_weights",
    )(*arrays, *swaps, small)
    total = results[-1]
    if groups > 1:
        total = total + sum(shift_group(total, k) for k in range(1, groups))
    return finish_reduce(results[:held]), results[held:-1], total


def attend_back_and_reduce(qkv_i, qkv_t, o_i, o_t, d_i, d_t, lse, info, tq, partials, units, swaps, collective_id):
    ti, w3 = qkv_i.shape
    tt, w, tp = qkv_t.shape[0], w3 // 3, 256
    steps = w // 128
    arrays = reduce_views(partials)
    held = len(arrays)
    n, size = held + len(swaps), 4 * len(units)
    bi = lambda off: pl.BlockSpec((ti, 128), lambda p, j, s, off=off: (0, p + off * steps))
    bt = lambda off: pl.BlockSpec((tt, 128), lambda p, j, s, off=off: (0, p + off * steps))

    def kernel(*refs):
        info_ref, attn_in = refs[0], refs[1:12]
        ins, near = refs[12 : 12 + held], refs[12 + held : 12 + n]
        attn_out, rest = refs[12 + n : 14 + n], refs[14 + n :]
        outs, far, mine = rest[:held], rest[held:n], rest[n : n + 8]
        scratch, totals = rest[n + 8 : n + 8 + size], rest[n + 8 + size : n + 8 + size + held]
        pair, part = pl.program_id(0), pl.program_id(1)
        begin, actions, end = reduce_plan(units, ins, outs, scratch, totals, *refs[-5:-1])
        swapped = swap_copies(near, far, refs[-1])

        @pl.when((pair == 0) & (part == 0))
        def _():
            enter(core_too=False)
            begin()
            for cp in swapped:
                cp.start()

        times = (3, 6, 9, 11)
        early = min(len(times), len(actions) - 1)
        for index, at in zip(range(early), times):
            pl.when((pair == at) & (part == 0))(actions[index])
        attn_bwd_kernel(ti, tt, tq, info_ref, *attn_in, *attn_out, *mine)

        @pl.when((pair == steps - 1) & (part == 2))
        def _():
            for action in actions[early:]:
                action()
            end()
            for cp in swapped:
                cp.wait()

    results = pl.pallas_call(
        kernel,
        grid_spec=pltpu.PrefetchScalarGridSpec(
            num_scalar_prefetch=1,
            grid=(steps, 3),
            in_specs=[bi(0), bi(1), bi(2), bt(0), bt(1), bt(2), bi(0), bt(0), bi(0), bt(0)]
            + [pl.BlockSpec((1, 8, ti + tp), lambda p, j, s: (p, 0, 0))]
            + [pl.BlockSpec(memory_space=pl.ANY)] * n,
            out_specs=[
                pl.BlockSpec((ti, 128), lambda p, j, s: (0, p + j * steps)),
                pl.BlockSpec((tt, 128), lambda p, j, s: (0, p + j * steps)),
            ]
            + [pl.BlockSpec(memory_space=pl.ANY)] * n,
            scratch_shapes=[pltpu.VMEM((tp, 128), jnp.bfloat16)] * 2
            + [pltpu.VMEM((ti, 128), jnp.float32), pltpu.VMEM((tp, 128), jnp.float32)] * 2
            + [pltpu.VMEM((ti, 128), jnp.bfloat16), pltpu.VMEM((tt, 128), jnp.bfloat16)]
            + reduce_scratch(arrays, units, swaps),
        ),
        out_shape=[jax.ShapeDtypeStruct((ti, w3), jnp.bfloat16), jax.ShapeDtypeStruct((tt, w3), jnp.bfloat16)]
        + reduce_shapes(arrays, swaps),
        compiler_params=pltpu.CompilerParams(
            collective_id=collective_id, has_side_effects=True, vmem_limit_bytes=60 << 20
        ),
        name="attend_back_and_reduce",
    )(info, qkv_i, qkv_i, qkv_i, qkv_t, qkv_t, qkv_t, o_i, o_t, d_i, d_t, lse, *arrays, *swaps)
    return results[:2], finish_reduce(results[2 : 2 + held]), results[2 + held :]


def gather_offloaded(shard, stream, earlier=()):
    x, _, _, _, _ = coords()
    share = shard.shape[1] // (2 * lax.axis_size(DP))
    start = (x * lax.axis_size(DP) + lax.axis_index(DP)) * share
    piece = lax.dynamic_slice(shard, (stream, start, 0), (1, share, shard.shape[2]))[0]
    return lax.all_gather(after(piece, *earlier), ("fsdp", "seq", "y", "core"), axis=0, tiled=True)


def gather_plane(*values):
    both = jnp.concatenate(values, axis=1) if len(values) > 1 else values[0]
    both = lax.all_gather(both, ("seq", "y", "core"), axis=0, tiled=True)
    edges = [0]
    for v in values:
        edges.append(edges[-1] + v.shape[1])
    return [both[:, a:b] for a, b in zip(edges, edges[1:])]


def own_blocks(values, axis):
    fs, n = lax.axis_size("fsdp"), lax.axis_size(DP)
    size = values.shape[axis] // (2 * fs * n)
    start = (lax.axis_index("seq") * fs * n + lax.axis_index(DP)) * size
    return jnp.concatenate(
        [lax.dynamic_slice_in_dim(values, start + f * n * size, size, axis) for f in range(fs)], axis=axis
    )


def sum_fsdp(total):
    flat = total.astype(jnp.bfloat16).reshape(-1, total.shape[-1])
    mine = lax.psum_scatter(flat, "fsdp", scatter_dimension=0, tiled=True)
    return mine.reshape(total.shape[1:]).astype(jnp.float32)


def plane_total(left, right):
    total = dot(own_blocks(left, 1), right, 0, 0)
    return total.reshape(lax.axis_size("fsdp"), -1, total.shape[1]).astype(jnp.bfloat16)


def plane_mlp_grads(modded, d_mlp, weight_up, bias_up, weight_down):
    fs, n = lax.axis_size("fsdp"), lax.axis_size(DP)
    x = lax.axis_index("seq")
    hidden = linear(modded, own_blocks(weight_up, 1), own_blocks(bias_up, 0))
    active, slope = gelu_both(hidden)
    d_active = linear_back(d_mlp, own_blocks(weight_down, 0))
    d_hidden = (slope.astype(jnp.float32) * d_active).astype(jnp.bfloat16)
    down = dot(active, d_mlp, 0, 0)
    grad_down = sum_fsdp(down.reshape(fs, -1, down.shape[1]))
    up = dot(modded, d_hidden, 0, 0)
    rows, units = up.shape
    up = up.reshape(2, fs, rows // (2 * fs), units).transpose(1, 0, 2, 3)
    mine = sum_fsdp(up).reshape(rows // fs, units).astype(jnp.bfloat16)
    spread = lax.all_gather(mine, ("seq", "y", "core"), axis=0)
    spread = spread.reshape(2 * n, 2, n, rows // (2 * fs * n), units)
    spread = lax.dynamic_index_in_dim(spread, x, 1, keepdims=False)
    spread = lax.dynamic_index_in_dim(spread, lax.axis_index(DP), 1, keepdims=False)
    spread = spread.reshape(2, n, spread.shape[1], fs, -1).transpose(2, 0, 3, 1, 4)
    return grad_down, spread.reshape(spread.shape[0], -1).astype(jnp.float32)


def swap_halves(mine_rows):
    _, _, _, _, c = coords()
    rows = mine_rows.shape[0] // 2
    near = lax.dynamic_slice_in_dim(mine_rows, c * rows, rows, 0)
    far = flip_core(lax.dynamic_slice_in_dim(mine_rows, (1 - c) * rows, rows, 0))
    return jnp.concatenate([jnp.where(c == 0, near, far), jnp.where(c == 0, far, near)], axis=1)


def gather_small(value):
    fs = lax.axis_size("fsdp")
    z = lax.axis_index("fsdp")
    stack = jnp.stack([value] + [shift_z(value, k) for k in range(1, fs)])
    ordered = [lax.dynamic_index_in_dim(stack, (z - j) % fs, 0, keepdims=False) for j in range(fs)]
    return jnp.stack(ordered, axis=1)


def wgrad_kernel(sel_ref, a0, b0, a1, b1, out, a0t, a1t):
    @pl.when(pl.program_id(1) == 0)
    def _():
        a0t[...] = a0[...].T
        a1t[...] = a1[...].T

    out[...] = (dot(a0t[...], b0[...], 1, 0) + dot(a1t[...], b1[...], 1, 0)).astype(out.dtype)


def wgrad(a0, b0, a1, b1, row_half, col_half):
    tokens, rows = a0.shape
    cols = b0.shape[1]
    tr = tc = 768
    halves = 1 if row_half is None else 2
    nr, nc = rows // halves // tr, cols // 2 // tc
    row_start = jnp.int32(0) if row_half is None else row_half * nr
    a_spec = pl.BlockSpec((tokens, tr), lambda i, j, s: (0, s[0] + i))
    b_spec = pl.BlockSpec((tokens, tc), lambda i, j, s: (0, s[1] + j))
    return pl.pallas_call(
        wgrad_kernel,
        grid_spec=pltpu.PrefetchScalarGridSpec(
            num_scalar_prefetch=1,
            grid=(nr, nc),
            in_specs=[a_spec, b_spec, a_spec, b_spec],
            out_specs=pl.BlockSpec((tr, tc), lambda i, j, s: (i, j)),
            scratch_shapes=[pltpu.VMEM((tr, tokens), a0.dtype)] * 2,
        ),
        out_shape=jax.ShapeDtypeStruct((rows // halves, cols // 2), jnp.bfloat16),
        compiler_params=pltpu.CompilerParams(vmem_limit_bytes=48 << 20),
        cost_estimate=pl.CostEstimate(
            flops=2 * tokens * (rows // halves) * cols,
            bytes_accessed=2 * tokens * (rows + cols) + rows * cols,
            transcendentals=0,
        ),
        name="wgrad",
    )(jnp.stack([row_start, col_half * nc]).astype(jnp.int32), a0, b0, a1, b1)


def partial_grad(left, right, far_left, far_right):
    return wgrad(left, right, far_left, far_right, None, lax.axis_index("core"))


def local(
    image_in,
    text_in,
    modulation,
    text_len,
    w_qkv,
    b_qkv,
    w_out,
    b_out,
    w_up,
    b_up,
    w_down,
    b_down,
    d_image,
    d_text,
):
    x, z, g, y, c = coords()
    image_half, text_half = image_in.shape[1], text_in.shape[1]
    width = image_in.shape[2]
    text_rows = -(-2 * text_half // 16) * 16

    def take(arr, index=x):
        return lax.dynamic_index_in_dim(arr, index, 0, keepdims=False)

    def join(near, far, rows):
        pad = jnp.zeros((rows - 2 * near.shape[0], width), near.dtype)
        return jnp.concatenate([near, far, pad], axis=0)

    def in_order(near, far):
        return jnp.where(x == 0, jnp.stack([near, far]), jnp.stack([far, near]))

    gathered, far = gather_weights(
        [(w_qkv, 0, True), (w_qkv, 1, False)], [take(image_in, 1 - x), take(text_in, 1 - x)], 0
    )
    weight_qkv = gathered
    streams = (join(take(image_in), far[0], 2 * image_half), join(take(text_in), far[1], text_rows))
    text_weights = [gather_offloaded(w_out, 1, (weight_qkv[0],))]
    gains = take(modulation)
    info = jnp.stack([take(text_len), jnp.int32(text_half), x.astype(jnp.int32)])
    small = gather_small(jnp.concatenate([b_qkv, b_out, b_up, b_down], axis=1))
    biases, start = [], 0
    for b in (b_qkv, b_out, b_up, b_down):
        biases.append(small[:, :, start : start + b.shape[1]].reshape(2, -1).astype(jnp.float32))
        start += b.shape[1]
    bias_qkv, bias_out, bias_up, bias_down = biases

    fronts = []
    for s in range(2):
        mod = gains[s]
        normed, inverse = normalize(streams[s].astype(jnp.float32))
        modded = (normed * (1.0 + mod[1]) + mod[0]).astype(jnp.bfloat16)
        projected = linear(modded, weight_qkv[s], bias_qkv[s]).astype(jnp.bfloat16)
        fronts.append((normed, inverse, modded, projected))
    (att_i, att_t, lse), image_weights, far = attend_and_gather(
        fronts[0][3],
        fronts[1][3],
        info,
        2 * image_half,
        [(w_out, 0, True), (w_up, 0, False), (w_down, 0, True)],
        [take(d_image, 1 - x), take(d_text, 1 - x)],
        1,
    )
    cotangents = (join(take(d_image), far[0], 2 * image_half), join(take(d_text), far[1], text_rows))
    text_weights += [gather_offloaded(w, 1, (image_weights[0],)) for w in (w_up, w_down)]
    weight_out, weight_up, weight_down = zip(image_weights, text_weights)

    outs, backs, column_sums, parts = [], [], [], {}
    token = att_i
    for s in range(2):
        mod = gains[s]
        attended = after((att_i, att_t)[s], token)
        upstream = cotangents[s].astype(jnp.float32)
        d_mlp = (mod[5] * upstream).astype(jnp.bfloat16)
        branch = linear(attended, weight_out[s], bias_out[s])
        middle = streams[s].astype(jnp.float32) + mod[2] * branch
        normed_two, inverse_two = normalize(middle)
        modded_two = (normed_two * (1.0 + mod[4]) + mod[3]).astype(jnp.bfloat16)
        if s == 1:
            text_mlp = gather_plane(modded_two, d_mlp, fronts[1][2])
        hidden = linear(modded_two, weight_up[s], bias_up[s])
        active, slope = gelu_both(hidden)
        if s == 0:
            far_active, far_d_mlp = flip_core(active), flip_core(d_mlp)
        mlp_out = linear(active, weight_down[s], bias_down[s])
        outs.append((middle + mod[5] * mlp_out).astype(jnp.bfloat16))
        d_gate_two = jnp.sum(upstream * mlp_out, axis=0)
        if s == 0:
            parts["down"] = partial_grad(after(active, outs[s]), d_mlp, far_active, far_d_mlp)
            d_mlp = after(d_mlp, parts["down"])
        d_active = linear_back(d_mlp, weight_down[s])
        d_hidden = (slope.astype(jnp.float32) * d_active).astype(jnp.bfloat16)
        if s == 0:
            far_d_hidden, far_modded_two = flip_core(d_hidden), flip_core(modded_two)
        d_modded_two = linear_back(d_hidden, weight_up[s])
        d_shift_two = jnp.sum(d_modded_two, axis=0)
        d_scale_two = jnp.sum(d_modded_two * normed_two, axis=0)
        d_middle = upstream + normalize_back(normed_two, inverse_two, d_modded_two * (1.0 + mod[4]))
        d_gate_one = jnp.sum(d_middle * branch, axis=0)
        d_branch = (mod[2] * d_middle).astype(jnp.bfloat16)
        if s == 0:
            parts["up"] = partial_grad(after(modded_two, d_branch), d_hidden, far_modded_two, far_d_hidden)
            far_attended, far_d_branch = flip_core(attended), flip_core(d_branch)
            d_branch = after(d_branch, parts["up"])
        else:
            text_out = gather_plane(attended, d_branch)
        d_attended = linear_back(d_branch, weight_out[s]).astype(jnp.bfloat16)
        if s == 0:
            parts["out"] = partial_grad(after(attended, d_attended), d_branch, far_attended, far_d_branch)
            token = parts["out"]
        column_sums.append([jnp.sum(a.astype(jnp.float32), axis=0) for a in (d_branch, d_hidden, d_mlp)])
        backs.append((d_attended, d_middle, d_gate_one, d_shift_two, d_scale_two, d_gate_two))
    sent = [outs[0][image_half:], outs[1][text_half : 2 * text_half]]
    text_grads = plane_mlp_grads(text_mlp[0], after(text_mlp[1], backs[1][0]), weight_up[1], bias_up[1], weight_down[1])
    far_text_modded = text_mlp[2]
    d_front, reduced, far_outs = attend_back_and_reduce(
        fronts[0][3],
        fronts[1][3],
        att_i,
        att_t,
        backs[0][0],
        backs[1][0],
        lse,
        info,
        image_half // 2,
        [parts["down"], parts["up"], parts["out"]],
        [(0, True, 0, parts["down"].shape[1]), (1, False, 0, parts["up"].shape[1]), (2, True, 0, parts["out"].shape[1])],
        sent,
        2,
    )
    text_qkv = gather_plane(d_front[1])[0]
    text_out = [after(text_out[0], d_front[1]), text_out[1]]
    text_out_total = plane_total(*text_out)
    far_front, far_modded = flip_core(d_front[0]), flip_core(fronts[0][2])
    grads = {("down", 0): reduced[0], ("up", 0): reduced[1], ("out", 0): reduced[2]}
    input_grads, gain_grads = [], []
    for s in range(2):
        mod = gains[s]
        normed, inverse, modded, _ = fronts[s]
        d_attended, d_middle, d_gate_one, d_shift_two, d_scale_two, d_gate_two = backs[s]
        d_modded = linear_back(after(d_front[s], text_out_total), weight_qkv[s])
        d_shift_one = jnp.sum(d_modded, axis=0)
        d_scale_one = jnp.sum(d_modded * normed, axis=0)
        input_grads.append(d_middle + normalize_back(normed, inverse, d_modded * (1.0 + mod[1])))
        gain_grads.append(
            jnp.stack([d_shift_one, d_scale_one, d_gate_one, d_shift_two, d_scale_two, d_gate_two])
        )
    mine = jnp.stack(gain_grads)
    part = partial_grad(after(fronts[0][2], *input_grads), d_front[0], far_modded, far_front)
    text_qkv_total = plane_total(far_text_modded, after(text_qkv, part))
    part = after(part, text_qkv_total)
    cols = part.shape[1]
    sent = [input_grads[0][image_half:].astype(jnp.bfloat16), input_grads[1][text_half : 2 * text_half].astype(jnp.bfloat16)]
    front_sums = [jnp.sum(d_front[s].astype(jnp.float32), axis=0) for s in range(2)]
    small = jnp.concatenate([front_sums[s] for s in range(2)] + [v for s in range(2) for v in column_sums[s]])
    reduced, far_grads, small = reduce_weights(
        [part],
        [(0, True, 0, cols // 2), (0, False, cols // 2, cols // 2)],
        sent + [mine.reshape(-1, width)],
        small.reshape(-1, 128),
        3,
    )
    grads["qkv", 0] = reduced[0]
    grads["down", 1], grads["up", 1] = text_grads
    grads["out", 1] = sum_fsdp(text_out_total)
    grads["qkv", 1] = sum_fsdp(text_qkv_total)
    grad_modulation = in_order(mine, far_grads[2].reshape(mine.shape))

    count = lax.axis_size(("seq", "fsdp") + DP)
    index = lax.axis_index(("seq", "fsdp") + DP)

    def cut_bias(total):
        return lax.dynamic_index_in_dim(total.reshape(2, count, -1), index, 1, keepdims=False)

    small = small.reshape(-1)
    front = front_sums[0].shape[0]
    per_stream = small[2 * front :].reshape(2, -1)
    sizes = [a.shape[0] for a in column_sums[0]]
    gb_qkv = cut_bias(small[: 2 * front].reshape(2, front))
    gb_out, gb_up, gb_down = [
        cut_bias(a) for a in jnp.split(per_stream, [sizes[0], sizes[0] + sizes[1]], axis=1)
    ]
    grads_qkv, grads_out, grads_up, grads_down = [
        jnp.stack([grads[name, s] for s in range(2)]) for name in ("qkv", "out", "up", "down")
    ]
    halves = (image_half, text_half)
    return (
        *[in_order(outs[s][: halves[s]], far_outs[s]) for s in range(2)],
        *[in_order(input_grads[s][: halves[s]], far_grads[s].astype(jnp.float32)) for s in range(2)],
        grad_modulation,
        grads_qkv,
        gb_qkv,
        grads_out,
        gb_out,
        grads_up,
        gb_up,
        grads_down,
        gb_down,
    )


def solution(mesh):
    seq, fsdp, dp = (mesh.shape[name] for name in ("seq", "fsdp", "dp"))
    split = Mesh(mesh.devices.reshape(seq, fsdp, dp // 2, 2), ("seq", "fsdp", "y", "core"))
    batch = ("fsdp",) + DP
    tokens = P(batch, "seq", None)
    weight, bias = P(None, "fsdp", None), P(None, "fsdp")
    in_specs = (tokens, tokens, P(batch, None, None, None), P(batch))
    in_specs += (weight, bias) * 4 + (tokens, tokens)
    everywhere = ("seq",) + batch
    grad_w, grad_b = P(None, everywhere, None), P(None, everywhere)
    out_specs = (tokens,) * 4 + (P(batch, None, None, None),) + (grad_w, grad_b) * 4
    return jax.shard_map(local, mesh=split, in_specs=in_specs, out_specs=out_specs, check_vma=False)
```

```python
import functools

import jax
import jax.numpy as jnp
from jax import lax
from jax.experimental import pallas as pl
from jax.experimental.pallas import tpu as pltpu
from jax.sharding import Mesh, PartitionSpec as P

EPSILON = 1e-06
HEAD_DIM=64
MASKED=-1000000000.0
def dot(a,b,ca,cb):
    return lax.dot_general(a,b,(((ca,),(cb,)),((),())),preferred_element_type=jnp.float32)

def attn_fwd_kernel(ti,tt,tq,len_ref,qi,ki,vi,qt,kt,vt,oi,ot,lse,ktp,vtp):
    tp=ktp.shape[0]
    ktp[...]=jnp.zeros_like(ktp); vtp[...]=jnp.zeros_like(vtp)
    ktp[:tt,:]=kt[...]; vtp[:tt,:]=vt[...]
    n_len=len_ref[0]; half=len_ref[1]; mine=len_ref[2]
    r=lax.broadcasted_iota(jnp.int32,(1,tp),1)
    pos=jnp.where(r<half,mine*half+r,(1-mine)*half+r-half)
    valid=(r<2*half)&(pos<n_len)
    lane=lax.broadcasted_iota(jnp.int32,(1,2*HEAD_DIM),1)
    k_img=ki[...]; v_img=vi[...]; k_txt=ktp[...]; v_txt=vtp[...]
    def one(q,rows):
        outs=[];lses=[]
        for h in range(2):
            qh=jnp.where((lane<HEAD_DIM)==(h==0),q.astype(jnp.float32)*(HEAD_DIM**-0.5),0.0).astype(jnp.bfloat16)
            s1=dot(qh,k_img,1,1); s2=dot(qh,k_txt,1,1)
            s2=jnp.where(valid,s2,MASKED)
            m=jnp.maximum(jnp.max(s1,axis=1,keepdims=True),jnp.max(s2,axis=1,keepdims=True))
            e1=jnp.exp(s1-m); e2=jnp.exp(s2-m)
            l=jnp.sum(e1,axis=1,keepdims=True)+jnp.sum(e2,axis=1,keepdims=True)
            inv=1.0/l
            o=dot((e1*inv).astype(jnp.bfloat16),v_img,1,0)+dot((e2*inv).astype(jnp.bfloat16),v_txt,1,0)
            outs.append(o); lses.append(m+jnp.log(l))
        o=jnp.where(lane<HEAD_DIM,outs[0],outs[1]).astype(jnp.bfloat16)
        both=jnp.where(lane<HEAD_DIM,jnp.broadcast_to(lses[0],(rows,128)),jnp.broadcast_to(lses[1],(rows,128)))
        return o,both.T
    def step(i,_):
        start=pl.multiple_of(i*tq,tq)
        o,b=one(qi[pl.ds(start,tq),:],tq)
        oi[pl.ds(start,tq),:]=o
        lse[0,0:1,pl.ds(start,tq)]=b[0:1]; lse[0,1:2,pl.ds(start,tq)]=b[64:65]
        return 0
    lax.fori_loop(0,ti//tq,step,0)
    qpad=jnp.concatenate([qt[...],jnp.zeros((tp-tt,128),jnp.bfloat16)],axis=0)
    o,b=one(qpad,tp)
    ot[...]=o[:tt]
    lse[0,0:1,ti:ti+tp]=b[0:1]; lse[0,1:2,ti:ti+tp]=b[64:65]

def attn_bwd_kernel(ti,tt,tq,len_ref,qi,ki,vi,qt,kt,vt,oi,ot,di,dt,lse,outi,outt,ktp,vtp,dk1,dk2,dv1,dv2,dqi,dqt):
    j=pl.program_id(1)
    tp=ktp.shape[0]
    @pl.when(j==0)
    def _():
        ktp[...]=jnp.zeros_like(ktp); vtp[...]=jnp.zeros_like(vtp)
        ktp[:tt,:]=kt[...]; vtp[:tt,:]=vt[...]
        n_len=len_ref[0]; half=len_ref[1]; mine=len_ref[2]
        r=lax.broadcasted_iota(jnp.int32,(tp,1),0)
        pos=jnp.where(r<half,mine*half+r,(1-mine)*half+r-half)
        valid=(r<2*half)&(pos<n_len)
        lane=lax.broadcasted_iota(jnp.int32,(1,128),1)
        sub=lax.broadcasted_iota(jnp.int32,(8,128),0); lane8=lax.broadcasted_iota(jnp.int32,(8,128),1)
        sel=jnp.where((lane8//HEAD_DIM)==sub,1.0,0.0).astype(jnp.bfloat16)
        k_img=ki[...]; v_img=vi[...]; k_txt=ktp[...]; v_txt=vtp[...]
        for ref in (dk1,dk2,dv1,dv2): ref[...]=jnp.zeros_like(ref)
        def one(q,do,o,ls):
            prod=do.astype(jnp.float32)*o.astype(jnp.float32)
            hi=prod.astype(jnp.bfloat16); lo=(prod-hi.astype(jnp.float32)).astype(jnp.bfloat16)
            dsum=dot(sel,hi,1,1)+dot(sel,lo,1,1)
            qs=(q.astype(jnp.float32)*(HEAD_DIM**-0.5))
            dof=do.astype(jnp.float32)
            dqs=[]
            for h in range(2):
                mk=(lane<HEAD_DIM)==(h==0)
                qh=jnp.where(mk,qs,0.0).astype(jnp.bfloat16)
                dh=jnp.where(mk,dof,0.0).astype(jnp.bfloat16)
                L=ls[h:h+1]; D=dsum[h:h+1]
                s1=dot(k_img,qh,1,1); s2=dot(k_txt,qh,1,1)
                p1=jnp.exp(s1-L); p2=jnp.where(valid,jnp.exp(s2-L),0.0)
                dp1=dot(v_img,dh,1,1); dp2=dot(v_txt,dh,1,1)
                ds1=(p1*(dp1-D)).astype(jnp.bfloat16); ds2=(p2*(dp2-D)).astype(jnp.bfloat16)
                dv1[...]+=dot(p1.astype(jnp.bfloat16),dh,1,0)
                dv2[...]+=dot(p2.astype(jnp.bfloat16),dh,1,0)
                dk1[...]+=dot(ds1,qh,1,0)
                dk2[...]+=dot(ds2,qh,1,0)
                dqs.append(dot(ds1,k_img,0,0)+dot(ds2,k_txt,0,0))
            return (jnp.where(lane<HEAD_DIM,dqs[0],dqs[1])*(HEAD_DIM**-0.5)).astype(jnp.bfloat16)
        def step(i,_):
            start=pl.multiple_of(i*tq,tq)
            sl=pl.ds(start,tq)
            dqi[sl,:]=one(qi[sl,:],di[sl,:],oi[sl,:],lse[0,:,sl])
            return 0
        lax.fori_loop(0,ti//tq,step,0)
        pad=lambda a: jnp.concatenate([a,jnp.zeros((tp-tt,128),jnp.bfloat16)],axis=0)
        dqt[...]=one(pad(qt[...]),pad(dt[...]),pad(ot[...]),lse[0,:,ti:ti+tp])[:tt]
        outi[...]=dqi[...]; outt[...]=dqt[...]
    @pl.when(j==1)
    def _():
        outi[...]=dk1[...].astype(jnp.bfloat16); outt[...]=dk2[:tt,:].astype(jnp.bfloat16)
    @pl.when(j==2)
    def _():
        outi[...]=dv1[...].astype(jnp.bfloat16); outt[...]=dv2[:tt,:].astype(jnp.bfloat16)


def normalize(values):
    row_mean = jnp.mean(values, axis=-1, keepdims=True)
    centred = values - row_mean
    variance = jnp.mean(centred * centred, axis=-1, keepdims=True)
    inverse = lax.rsqrt(variance + EPSILON)
    return (centred * inverse, inverse)


def normalize_back(normed, inverse, upstream):
    mean_one = jnp.mean(upstream, axis=-1, keepdims=True)
    mean_two = jnp.mean(upstream * normed, axis=-1, keepdims=True)
    return inverse * (upstream - mean_one - normed * mean_two)


def linear(values, weight, offset):
    return jnp.dot(values, weight, preferred_element_type=jnp.float32) + offset.astype(jnp.float32)


def linear_back(upstream, weight):
    return dot(upstream, weight, 1, 1)


def gelu_both(values):
    inner = jnp.tanh(0.7978845608028654 * values * (1.0 + 0.044715 * values * values))
    half = 0.5 * (1.0 + inner)
    slope = half + 0.5 * values * (1.0 - inner * inner) * (0.7978845608028654 * (1.0 + 0.134145 * values * values))
    return (values * half).astype(jnp.bfloat16), slope.astype(jnp.bfloat16)


def column_sum(values):
    return dot(jnp.ones((8, values.shape[0]), values.dtype), values, 1, 0)[0]


DP = ("y", "core")


def coords():
    dp = lax.axis_index(DP)
    return lax.axis_index("seq"), lax.axis_index("fsdp"), dp // 4, (dp // 2) % 2, dp % 2


def flip_x(a):
    return lax.ppermute(a, "seq", [(0, 1), (1, 0)])


def flip_y(a):
    return lax.ppermute(a, DP, [(i, i ^ 2) for i in range(lax.axis_size(DP))])


def flip_core(a):
    return lax.ppermute(a, DP, [(i, i ^ 1) for i in range(lax.axis_size(DP))])


def shift_z(a, k):
    n = lax.axis_size("fsdp")
    return lax.ppermute(a, "fsdp", [(i, (i + k) % n) for i in range(n)])


def shift_group(a, k):
    n = lax.axis_size(DP)
    return lax.ppermute(a, DP, [(i, (i + 4 * k) % n) for i in range(n)])


def after(value, *earlier):
    return lax.optimization_barrier((value, *earlier))[0]


def enter(z_too=True, y_too=True, core_too=True):
    fs = lax.axis_size("fsdp")
    x, z, _, y, c = coords()
    targets = [{"seq": 1 - x}]
    if y_too:
        targets.append({"y": lax.axis_index("y") + 1 - 2 * y})
    if core_too:
        targets.append({"core": 1 - c})
    if z_too:
        targets += [{"fsdp": lax.rem(z + k, fs)} for k in range(1, fs)]
    barrier = pltpu.get_barrier_semaphore()
    for target in targets:
        pl.semaphore_signal(barrier, inc=1, device_id=target, device_id_type=pl.DeviceIdType.MESH)
    pl.semaphore_wait(barrier, len(targets))


def swap_copies(srcs, dsts, sems):
    x = lax.axis_index("seq")
    return [
        pltpu.make_async_remote_copy(
            src_ref=src,
            dst_ref=dst,
            send_sem=sems.at[i, 0],
            recv_sem=sems.at[i, 1],
            device_id={"seq": 1 - x},
            device_id_type=pl.DeviceIdType.MESH,
        )
        for i, (src, dst) in enumerate(zip(srcs, dsts))
    ]


def gather_plan(units, shards, outs, bufs, local_sem, send_sem, recv_sem):
    fs = lax.axis_size("fsdp")
    count = len(units)
    kinds = ("first", "second", "core0", "forward", "core1", "core2", "core3")
    x, z, _, y, c = coords()
    to_x, to_y, to_core = {"seq": 1 - x}, {"y": lax.axis_index("y") + 1 - 2 * y}, {"core": 1 - c}

    def remote(src, dst, u, slot, target):
        return pltpu.make_async_remote_copy(
            src_ref=src,
            dst_ref=dst,
            send_sem=send_sem.at[u, slot],
            recv_sem=recv_sem.at[u, slot],
            device_id=target,
            device_id_type=pl.DeviceIdType.MESH,
        )

    def spot(u, from_z, dx, dy, cc):
        _, r, cols = units[u][0].shape
        q, h = r // 4, cols // 2
        xx = 1 - x if dx else x
        yy = 1 - y if dy else y
        row = pl.multiple_of(from_z * r + (xx * 2 + yy) * q, 16)
        return outs[u].at[pl.ds(row, q), pl.ds(pl.multiple_of(cc * h, 128), h)]

    def copy(u, kind, k):
        _, r, cols = units[u][0].shape
        q, h = r // 4, cols // 2
        if kind == "z":
            dst = spot(u, lax.rem(z - k + 1 + fs, fs), 0, 0, c)
            row = pl.multiple_of((x * 2 + y) * q, 16)
            own_piece = shards[u].at[units[u][1], pl.ds(row, q), pl.ds(pl.multiple_of(c * h, 128), h)]
            return remote(own_piece if k == 1 else dst, dst, u, k - 1, {"fsdp": lax.rem(z + 1, fs)})
        x_first = units[u][2]
        slot = (1 + kinds.index(kind)) * (fs - 1) + k - 1
        via = (1, 0) if x_first else (0, 1)
        other = (0, 1) if x_first else (1, 0)
        where, target = {
            "first": ((0, 0), to_x if x_first else to_y),
            "second": ((0, 0), to_y if x_first else to_x),
            "core0": ((0, 0), to_core),
            "forward": (via, to_y if x_first else to_x),
            "core1": (via, to_core),
            "core2": (other, to_core),
            "core3": ((1, 1), to_core),
        }[kind]
        place = spot(u, lax.rem(z - k + fs, fs), *where, c)
        return remote(place, place, u, slot, target)

    def fetch(u):
        return pltpu.make_async_copy(shards[u].at[units[u][1]], bufs[u], local_sem.at[u, 0])

    def own(u):
        r = units[u][0].shape[1]
        return pltpu.make_async_copy(
            bufs[u], outs[u].at[pl.ds(pl.multiple_of(z * r, 16), r), :], local_sem.at[u, 1]
        )

    ahead = min(2, count)
    order = [(u, k) for k in range(1, fs) for u in range(count)]

    def begin():
        for u, k in order[:ahead]:
            copy(u, "z", k).start()
        for u in range(count):
            fetch(u).start()
        for u in range(count):
            fetch(u).wait()
            own(u).start()

    def act(i):
        if i < len(order):
            u, k = order[i]
            copy(u, "z", k).wait_recv()
            if i + ahead < len(order):
                copy(order[i + ahead][0], "z", order[i + ahead][1]).start()
            for kind in ("first", "second", "core0"):
                copy(u, kind, k).start()
        if 0 <= i - lag < len(order):
            u, k = order[i - lag]
            copy(u, "first", k).wait_recv()
            copy(u, "forward", k).start()
            copy(u, "core1", k).start()
        if 0 <= i - 2 * lag < len(order):
            u, k = order[i - 2 * lag]
            copy(u, "second", k).wait_recv()
            copy(u, "core2", k).start()
            copy(u, "forward", k).wait_recv()
            copy(u, "core3", k).start()

    lag = 2
    actions = [functools.partial(act, i) for i in range(len(order) + 2 * lag)]

    def end():
        for u in range(count):
            for k in range(1, fs):
                for kind in ("core0", "core1", "core2", "core3"):
                    copy(u, kind, k).wait_recv()
                for kind in ("z",) + kinds:
                    copy(u, kind, k).wait_send()
            own(u).wait()

    return begin, actions, end


def gather_shapes(units):
    fs = lax.axis_size("fsdp")
    return [jax.ShapeDtypeStruct((u[0].shape[1] * fs, u[0].shape[2]), u[0].dtype) for u in units]


def gather_scratch(units, swaps):
    fs = lax.axis_size("fsdp")
    return [pltpu.VMEM(u[0].shape[1:], u[0].dtype) for u in units] + [
        pltpu.SemaphoreType.DMA((len(units), 2)),
        pltpu.SemaphoreType.DMA((len(units), 8 * (fs - 1))),
        pltpu.SemaphoreType.DMA((len(units), 8 * (fs - 1))),
        pltpu.SemaphoreType.DMA((max(len(swaps), 1), 2)),
    ]


def gather_weights(units, swaps, collective_id):
    count, n = len(units), len(units) + len(swaps)

    def kernel(*refs):
        shards, near, outs, far = refs[:count], refs[count:n], refs[n : n + count], refs[n + count : 2 * n]
        enter()
        swapped = swap_copies(near, far, refs[-1])
        for cp in swapped:
            cp.start()
        begin, actions, end = gather_plan(units, shards, outs, refs[2 * n : 2 * n + count], *refs[-4:-1])
        begin()
        for action in actions:
            action()
        end()
        for cp in swapped:
            cp.wait()

    results = pl.pallas_call(
        kernel,
        out_shape=gather_shapes(units) + [jax.ShapeDtypeStruct(a.shape, a.dtype) for a in swaps],
        in_specs=[pl.BlockSpec(memory_space=pl.ANY)] * n,
        out_specs=[pl.BlockSpec(memory_space=pl.ANY)] * n,
        scratch_shapes=gather_scratch(units, swaps),
        compiler_params=pltpu.CompilerParams(
            collective_id=collective_id, has_side_effects=True, vmem_limit_bytes=48 << 20
        ),
        name="gather_weights",
    )(*[u[0] for u in units], *swaps)
    return results[:count], results[count:]


def attend_and_gather(qkv_i, qkv_t, info, tq, units, swaps, collective_id):
    ti, w3 = qkv_i.shape
    tt, w, tp = qkv_t.shape[0], w3 // 3, 256
    steps = w // 128
    count, n = len(units), len(units) + len(swaps)
    bi = lambda off: pl.BlockSpec((ti, 128), lambda p, s, off=off: (0, p + off * steps))
    bt = lambda off: pl.BlockSpec((tt, 128), lambda p, s, off=off: (0, p + off * steps))

    def kernel(*refs):
        info_ref, attn_in = refs[0], refs[1:7]
        shards, near = refs[7 : 7 + count], refs[7 + count : 7 + n]
        attn_out, rest = refs[7 + n : 10 + n], refs[10 + n :]
        outs, far, pads = rest[:count], rest[count:n], rest[n : n + 2]
        step = pl.program_id(0)
        swapped = swap_copies(near, far, refs[-1])
        begin, actions, end = gather_plan(units, shards, outs, rest[n + 2 : n + 2 + count], *refs[-4:-1])

        @pl.when(step == 0)
        def _():
            enter()
            begin()
            for cp in swapped:
                cp.start()

        early = min(steps - 2, len(actions))
        for index in range(early):
            pl.when(step == index + 2)(actions[index])
        attn_fwd_kernel(ti, tt, tq, info_ref, *attn_in, *attn_out, *pads)

        @pl.when(step == steps - 1)
        def _():
            for action in actions[early:]:
                action()
            end()
            for cp in swapped:
                cp.wait()

    results = pl.pallas_call(
        kernel,
        grid_spec=pltpu.PrefetchScalarGridSpec(
            num_scalar_prefetch=1,
            grid=(steps,),
            in_specs=[bi(0), bi(1), bi(2), bt(0), bt(1), bt(2)] + [pl.BlockSpec(memory_space=pl.ANY)] * n,
            out_specs=[bi(0), bt(0), pl.BlockSpec((1, 8, ti + tp), lambda p, s: (p, 0, 0))]
            + [pl.BlockSpec(memory_space=pl.ANY)] * n,
            scratch_shapes=[pltpu.VMEM((tp, 128), jnp.bfloat16)] * 2 + gather_scratch(units, swaps),
        ),
        out_shape=[
            jax.ShapeDtypeStruct((ti, w), jnp.bfloat16),
            jax.ShapeDtypeStruct((tt, w), jnp.bfloat16),
            jax.ShapeDtypeStruct((steps, 8, ti + tp), jnp.float32),
        ]
        + gather_shapes(units)
        + [jax.ShapeDtypeStruct(a.shape, a.dtype) for a in swaps],
        compiler_params=pltpu.CompilerParams(
            collective_id=collective_id, has_side_effects=True, vmem_limit_bytes=56 << 20
        ),
        name="attend_and_gather",
    )(info, qkv_i, qkv_i, qkv_i, qkv_t, qkv_t, qkv_t, *[u[0] for u in units], *swaps)
    return results[:3], results[3 : 3 + count], results[3 + count :]


def reduce_plan(units, ins, outs, scratch, totals, load_sem, send_sem, recv_sem, out_sem):
    fs = lax.axis_size("fsdp")
    count = len(units)
    x, z, _, y, c = coords()
    to_x, to_y = {"seq": 1 - x}, {"y": lax.axis_index("y") + 1 - 2 * y}
    f32 = lambda a: a.astype(jnp.float32)

    def remote(u, slot, src, dst, target):
        return pltpu.make_async_remote_copy(
            src_ref=src,
            dst_ref=dst,
            send_sem=send_sem.at[u, slot],
            recv_sem=recv_sem.at[u, slot],
            device_id=target,
            device_id_type=pl.DeviceIdType.MESH,
        )

    def rows(u, k, mine):
        index, x_first, start, width = units[u]
        zz = lax.rem(z + k, fs)
        cols = pl.ds(start, width)
        if x_first:
            return ins[index].at[x if mine else 1 - x, zz, :, :, :, :, cols]
        return ins[index].at[:, zz, :, y if mine else 1 - y, :, :, cols]

    def load(u, k):
        return pltpu.make_async_copy(rows(u, k, True), scratch[4 * u].at[k - 1], load_sem.at[u, k - 1])

    def side(u, ref, k, mine):
        x_first = units[u][1]
        index = (y if mine else 1 - y) if x_first else (x if mine else 1 - x)
        return ref.at[k - 1, :, index] if x_first else ref.at[k - 1, index]

    def hop(u, stage, k):
        part, recv_one, recv_two, recv_three = scratch[4 * u : 4 * u + 4]
        x_first = units[u][1]
        if stage == 1:
            return remote(u, k - 1, rows(u, k, False), recv_one.at[k - 1], to_x if x_first else to_y)
        if stage == 2:
            return remote(u, fs + k - 1, side(u, part, k, False), recv_two.at[k - 1], to_y if x_first else to_x)
        return remote(
            u, 2 * fs + k - 1, recv_two.at[k - 1], recv_three.at[k - 1], {"fsdp": lax.rem(z + k, fs)}
        )

    def second(u, k):
        part, recv_one = scratch[4 * u : 4 * u + 2]
        load(u, k).wait()
        if k + ahead > fs:
            hop(u, 1, k).wait_recv()
        spot = side(u, part, k, False)
        spot[...] = (f32(spot[...]) + f32(side(u, recv_one, k, False)[...])).astype(jnp.bfloat16)
        hop(u, 2, k).start()

    def third(u, k):
        part, recv_one, recv_two = scratch[4 * u : 4 * u + 3]
        hop(u, 2, k).wait_recv()
        total = f32(side(u, part, k, True)[...]) + f32(side(u, recv_one, k, True)[...]) + f32(recv_two[k - 1])
        if k < fs:
            recv_two[k - 1] = total.astype(jnp.bfloat16)
            hop(u, 3, k).start()
        else:
            index, _, start, width = units[u]
            totals[index][:, :, :, start : start + width] = total

    ahead = 1

    def begin():
        for k in range(1, fs + 1):
            for u in range(count):
                if k <= ahead:
                    hop(u, 1, k).start()
                load(u, k).start()

    def stage(k):
        if k + ahead <= fs:
            for u in range(count):
                hop(u, 1, k).wait_recv()
            for u in range(count):
                hop(u, 1, k + ahead).start()
        for u in range(count):
            if k <= fs:
                second(u, k)
        for u in range(count):
            if k > 1:
                third(u, k - 1)

    actions = [functools.partial(stage, k) for k in range(1, fs + 2)]

    def end():
        for u in range(count):
            index, _, start, width = units[u]
            total = totals[index][:, :, :, start : start + width]
            for k in range(1, fs):
                hop(u, 3, k).wait_recv()
                total = total + f32(scratch[4 * u + 3][k - 1])
            totals[index][:, :, :, start : start + width] = total
        stores, sends = [], []
        for i, (total, out) in enumerate(zip(totals, outs)):
            h = total.shape[-1]
            place = out.at[:, :, pl.ds(pl.multiple_of(c * h, 128), h)]
            stores.append(pltpu.make_async_copy(total.at[:, c], place, out_sem.at[i, 0]))
            sends.append(
                pltpu.make_async_remote_copy(
                    src_ref=total.at[:, 1 - c],
                    dst_ref=place,
                    send_sem=out_sem.at[i, 1],
                    recv_sem=out_sem.at[i, 2],
                    device_id={"core": 1 - c},
                    device_id_type=pl.DeviceIdType.MESH,
                )
            )
        for cp in stores + sends:
            cp.start()
        for u in range(count):
            for k in range(1, fs + 1):
                for number in (1, 2, 3) if k < fs else (1, 2):
                    hop(u, number, k).wait_send()
        for cp in stores + sends:
            cp.wait()

    return begin, actions, end


def reduce_views(partials):
    fs, groups = lax.axis_size("fsdp"), lax.axis_size(DP) // 4
    return [p.reshape(2, fs, groups, 2, 2, -1, p.shape[1]) for p in partials]


def reduce_scratch(arrays, units, swaps):
    fs, groups = lax.axis_size("fsdp"), lax.axis_size(DP) // 4
    scratch = []
    for index, x_first, _, width in units:
        rows = arrays[index].shape[5]
        both = (groups, 2, 2, rows, width) if x_first else (2, groups, 2, rows, width)
        one = (groups, 2, rows, width)
        for shape in ((fs, *both), (fs, *both), (fs, *one), (fs - 1, *one)):
            scratch.append(pltpu.VMEM(shape, jnp.bfloat16))
    scratch += [pltpu.VMEM((groups, 2, *a.shape[5:]), jnp.float32) for a in arrays]
    return scratch + [
        pltpu.SemaphoreType.DMA((len(units), fs)),
        pltpu.SemaphoreType.DMA((len(units), 3 * fs)),
        pltpu.SemaphoreType.DMA((len(units), 3 * fs)),
        pltpu.SemaphoreType.DMA((len(arrays), 3)),
        pltpu.SemaphoreType.DMA((max(len(swaps), 1), 2)),
    ]


def reduce_shapes(arrays, swaps):
    groups = lax.axis_size(DP) // 4
    return [jax.ShapeDtypeStruct((groups, a.shape[5], 2 * a.shape[6]), jnp.float32) for a in arrays] + [
        jax.ShapeDtypeStruct(a.shape, a.dtype) for a in swaps
    ]


def finish_reduce(results):
    finals = []
    for total in results:
        groups, g = total.shape[0], lax.axis_index(DP) // 4
        at = lambda i: lax.dynamic_index_in_dim(total, i, 0, keepdims=False)
        mine = at(g)
        for k in range(1, groups):
            mine = mine + shift_group(at((g + k) % groups), k)
        finals.append(mine)
    return finals


def reduce_weights(partials, units, swaps, small, earlier, collective_id):
    fs, groups = lax.axis_size("fsdp"), lax.axis_size(DP) // 4
    arrays = reduce_views(partials)
    held = len(arrays)
    n, size = held + len(swaps), 4 * len(units)
    hops = 3 + fs - 1

    def kernel(*refs):
        ins, near, small_in = refs[:held], refs[held:n], refs[n]
        refs = refs[: n + 1] + refs[n + 1 + len(earlier) :]
        outs, far, small_out = refs[n + 1 : n + 1 + held], refs[n + 1 + held : 2 * n + 1], refs[2 * n + 1]
        rest = refs[2 * n + 2 :]
        scratch, totals = rest[:size], rest[size : size + held]
        staged, landed, small_sem = rest[size + held : size + held + 3]
        x, z, _, y, c = coords()
        enter()
        begin, actions, end = reduce_plan(units, ins, outs, scratch, totals, *refs[-5:-1])
        swapped = swap_copies(near, far, refs[-1])
        targets = [{"core": 1 - c}, {"seq": 1 - x}, {"y": lax.axis_index("y") + 1 - 2 * y}]
        targets += [{"fsdp": lax.rem(z + k, fs)} for k in range(1, fs)]

        def small_hop(i):
            return pltpu.make_async_remote_copy(
                src_ref=staged.at[min(i, 3)],
                dst_ref=landed.at[i],
                send_sem=small_sem.at[0, i],
                recv_sem=small_sem.at[1, i],
                device_id=targets[i],
                device_id_type=pl.DeviceIdType.MESH,
            )

        staged[0] = small_in[...]
        small_hop(0).start()
        begin()
        for cp in swapped:
            cp.start()
        for index, action in enumerate(actions):
            action()
            if index < 3:
                small_hop(index).wait_recv()
                staged[index + 1] = staged[index] + landed[index]
                for i in (index + 1,) if index < 2 else range(3, hops):
                    small_hop(i).start()
        end()
        total = staged[3]
        for i in range(3, hops):
            small_hop(i).wait_recv()
            total = total + landed[i]
        small_out[...] = total
        for i in range(hops):
            small_hop(i).wait_send()
        for cp in swapped:
            cp.wait()

    results = pl.pallas_call(
        kernel,
        out_shape=reduce_shapes(arrays, swaps) + [jax.ShapeDtypeStruct(small.shape, small.dtype)],
        in_specs=[pl.BlockSpec(memory_space=pl.ANY)] * n
        + [pl.BlockSpec(memory_space=pltpu.VMEM)]
        + [pl.BlockSpec(memory_space=pl.ANY)] * len(earlier),
        out_specs=[pl.BlockSpec(memory_space=pl.ANY)] * n + [pl.BlockSpec(memory_space=pltpu.VMEM)],
        scratch_shapes=(lambda base: base[: size + held]
        + [
            pltpu.VMEM((4, *small.shape), small.dtype),
            pltpu.VMEM((hops, *small.shape), small.dtype),
            pltpu.SemaphoreType.DMA((2, hops)),
        ]
        + base[size + held :])(reduce_scratch(arrays, units, swaps)),
        compiler_params=pltpu.CompilerParams(
            collective_id=collective_id, has_side_effects=True, vmem_limit_bytes=56 << 20
        ),
        name="reduce_weights",
    )(*arrays, *swaps, small, *earlier)
    total = results[-1]
    if groups > 1:
        total = total + sum(shift_group(total, k) for k in range(1, groups))
    return finish_reduce(results[:held]), results[held:-1], total


def attend_back_and_reduce(qkv_i, qkv_t, o_i, o_t, d_i, d_t, lse, info, tq, partials, units, swaps, earlier, collective_id):
    ti, w3 = qkv_i.shape
    tt, w, tp = qkv_t.shape[0], w3 // 3, 256
    steps = w // 128
    arrays = reduce_views(partials)
    held = len(arrays)
    n, size = held + len(swaps), 4 * len(units)
    bi = lambda off: pl.BlockSpec((ti, 128), lambda p, j, s, off=off: (0, p + off * steps))
    bt = lambda off: pl.BlockSpec((tt, 128), lambda p, j, s, off=off: (0, p + off * steps))

    def kernel(*refs):
        info_ref, attn_in = refs[0], refs[1:12]
        ins, near = refs[12 : 12 + held], refs[12 + held : 12 + n]
        refs = refs[: 12 + n] + refs[12 + n + len(earlier) :]
        attn_out, rest = refs[12 + n : 14 + n], refs[14 + n :]
        outs, far, mine = rest[:held], rest[held:n], rest[n : n + 8]
        scratch, totals = rest[n + 8 : n + 8 + size], rest[n + 8 + size : n + 8 + size + held]
        pair, part = pl.program_id(0), pl.program_id(1)
        begin, actions, end = reduce_plan(units, ins, outs, scratch, totals, *refs[-5:-1])
        swapped = swap_copies(near, far, refs[-1])

        @pl.when((pair == 0) & (part == 0))
        def _():
            enter()
            begin()
            for cp in swapped:
                cp.start()

        times = (2, 4, 7, 10)
        early = min(len(times), len(actions) - 1)
        for index, at in zip(range(early), times):
            pl.when((pair == at) & (part == 0))(actions[index])
        attn_bwd_kernel(ti, tt, tq, info_ref, *attn_in, *attn_out, *mine)

        @pl.when((pair == steps - 1) & (part == 2))
        def _():
            for action in actions[early:]:
                action()
            end()
            for cp in swapped:
                cp.wait()

    results = pl.pallas_call(
        kernel,
        grid_spec=pltpu.PrefetchScalarGridSpec(
            num_scalar_prefetch=1,
            grid=(steps, 3),
            in_specs=[bi(0), bi(1), bi(2), bt(0), bt(1), bt(2), bi(0), bt(0), bi(0), bt(0)]
            + [pl.BlockSpec((1, 8, ti + tp), lambda p, j, s: (p, 0, 0))]
            + [pl.BlockSpec(memory_space=pl.ANY)] * (n + len(earlier)),
            out_specs=[
                pl.BlockSpec((ti, 128), lambda p, j, s: (0, p + j * steps)),
                pl.BlockSpec((tt, 128), lambda p, j, s: (0, p + j * steps)),
            ]
            + [pl.BlockSpec(memory_space=pl.ANY)] * n,
            scratch_shapes=[pltpu.VMEM((tp, 128), jnp.bfloat16)] * 2
            + [pltpu.VMEM((ti, 128), jnp.float32), pltpu.VMEM((tp, 128), jnp.float32)] * 2
            + [pltpu.VMEM((ti, 128), jnp.bfloat16), pltpu.VMEM((tt, 128), jnp.bfloat16)]
            + reduce_scratch(arrays, units, swaps),
        ),
        out_shape=[jax.ShapeDtypeStruct((ti, w3), jnp.bfloat16), jax.ShapeDtypeStruct((tt, w3), jnp.bfloat16)]
        + reduce_shapes(arrays, swaps),
        compiler_params=pltpu.CompilerParams(
            collective_id=collective_id, has_side_effects=True, vmem_limit_bytes=60 << 20
        ),
        name="attend_back_and_reduce",
    )(info, qkv_i, qkv_i, qkv_i, qkv_t, qkv_t, qkv_t, o_i, o_t, d_i, d_t, lse, *arrays, *swaps, *earlier)
    return results[:2], finish_reduce(results[2 : 2 + held]), results[2 + held :]


def gather_offloaded(shard, stream, earlier=()):
    x, _, _, _, _ = coords()
    share = shard.shape[1] // (2 * lax.axis_size(DP))
    start = (x * lax.axis_size(DP) + lax.axis_index(DP)) * share
    piece = lax.dynamic_slice(shard, (stream, start, 0), (1, share, shard.shape[2]))[0]
    return lax.all_gather(after(piece, *earlier), ("fsdp", "seq", "y", "core"), axis=0, tiled=True)


def gather_plane(*values):
    both = jnp.concatenate(values, axis=1) if len(values) > 1 else values[0]
    both = lax.all_gather(both, ("seq", "y", "core"), axis=0, tiled=True)
    edges = [0]
    for v in values:
        edges.append(edges[-1] + v.shape[1])
    return [both[:, a:b] for a, b in zip(edges, edges[1:])]


def own_blocks(values, axis):
    fs, n = lax.axis_size("fsdp"), lax.axis_size(DP)
    size = values.shape[axis] // (2 * fs * n)
    start = (lax.axis_index("seq") * fs * n + lax.axis_index(DP)) * size
    return jnp.concatenate(
        [lax.dynamic_slice_in_dim(values, start + f * n * size, size, axis) for f in range(fs)], axis=axis
    )


def sum_fsdp(*totals):
    fs = totals[0].shape[0]
    width = totals[0].shape[-1]
    flat = jnp.concatenate([t.astype(jnp.bfloat16).reshape(fs, -1, width) for t in totals], axis=1)
    mine = lax.psum_scatter(flat.reshape(-1, width), "fsdp", scatter_dimension=0, tiled=True)
    result, start = [], 0
    for t in totals:
        rows = t.size // (fs * width)
        result.append(mine[start : start + rows].reshape(t.shape[1:]))
        start += rows
    return result


def plane_total(left, right):
    total = dot(own_blocks(left, 1), right, 0, 0)
    return total.reshape(lax.axis_size("fsdp"), -1, total.shape[1]).astype(jnp.bfloat16)


def plane_mlp_totals(modded, d_mlp, weight_up, bias_up, weight_down):
    fs = lax.axis_size("fsdp")
    hidden = linear(modded, own_blocks(weight_up, 1), own_blocks(bias_up, 0))
    active, slope = gelu_both(hidden)
    d_active = linear_back(d_mlp, own_blocks(weight_down, 0))
    d_hidden = (slope.astype(jnp.float32) * d_active).astype(jnp.bfloat16)
    down = dot(active, d_mlp, 0, 0).astype(jnp.bfloat16)
    up = dot(modded, d_hidden, 0, 0).astype(jnp.bfloat16)
    rows, units = up.shape
    up = up.reshape(2, fs, rows // (2 * fs), units).transpose(1, 0, 2, 3)
    return down.reshape(fs, -1, down.shape[1]), up


def spread_up(mine):
    fs, n = lax.axis_size("fsdp"), lax.axis_size(DP)
    _, rows, units = mine.shape
    spread = lax.all_gather(mine.reshape(-1, units), ("seq", "y", "core"), axis=0, tiled=True)
    spread = spread.reshape(2 * n, 2, n, rows // n, units)
    spread = lax.dynamic_index_in_dim(spread, lax.axis_index("seq"), 1, keepdims=False)
    spread = lax.dynamic_index_in_dim(spread, lax.axis_index(DP), 1, keepdims=False)
    spread = spread.reshape(2, n, spread.shape[1], fs, -1).transpose(2, 0, 3, 1, 4)
    return spread.reshape(spread.shape[0], -1).astype(jnp.float32)


def gather_small(value):
    fs = lax.axis_size("fsdp")
    z = lax.axis_index("fsdp")
    stack = jnp.stack([value] + [shift_z(value, k) for k in range(1, fs)])
    ordered = [lax.dynamic_index_in_dim(stack, (z - j) % fs, 0, keepdims=False) for j in range(fs)]
    return jnp.stack(ordered, axis=1)


def wgrad_kernel(sel_ref, a0, b0, a1, b1, out, a0t, a1t):
    @pl.when(pl.program_id(1) == 0)
    def _():
        a0t[...] = a0[...].T
        a1t[...] = a1[...].T

    out[...] = (dot(a0t[...], b0[...], 1, 0) + dot(a1t[...], b1[...], 1, 0)).astype(out.dtype)


def wgrad(a0, b0, a1, b1, row_half, col_half):
    tokens, rows = a0.shape
    cols = b0.shape[1]
    tr = tc = 768
    halves = 1 if row_half is None else 2
    nr, nc = rows // halves // tr, cols // 2 // tc
    row_start = jnp.int32(0) if row_half is None else row_half * nr
    a_spec = pl.BlockSpec((tokens, tr), lambda i, j, s: (0, s[0] + i))
    b_spec = pl.BlockSpec((tokens, tc), lambda i, j, s: (0, s[1] + j))
    return pl.pallas_call(
        wgrad_kernel,
        grid_spec=pltpu.PrefetchScalarGridSpec(
            num_scalar_prefetch=1,
            grid=(nr, nc),
            in_specs=[a_spec, b_spec, a_spec, b_spec],
            out_specs=pl.BlockSpec((tr, tc), lambda i, j, s: (i, j)),
            scratch_shapes=[pltpu.VMEM((tr, tokens), a0.dtype)] * 2,
        ),
        out_shape=jax.ShapeDtypeStruct((rows // halves, cols // 2), jnp.bfloat16),
        compiler_params=pltpu.CompilerParams(vmem_limit_bytes=48 << 20),
        cost_estimate=pl.CostEstimate(
            flops=2 * tokens * (rows // halves) * cols,
            bytes_accessed=2 * tokens * (rows + cols) + rows * cols,
            transcendentals=0,
        ),
        name="wgrad",
    )(jnp.stack([row_start, col_half * nc]).astype(jnp.int32), a0, b0, a1, b1)


def partial_grad(left, right, far_left, far_right):
    return wgrad(left, right, far_left, far_right, None, lax.axis_index("core"))


def local(
    image_in,
    text_in,
    modulation,
    text_len,
    w_qkv,
    b_qkv,
    w_out,
    b_out,
    w_up,
    b_up,
    w_down,
    b_down,
    d_image,
    d_text,
):
    x, z, g, y, c = coords()
    image_half, text_half = image_in.shape[1], text_in.shape[1]
    width = image_in.shape[2]
    text_rows = -(-2 * text_half // 16) * 16

    def take(arr, index=x):
        return lax.dynamic_index_in_dim(arr, index, 0, keepdims=False)

    def join(near, far, rows):
        pad = jnp.zeros((rows - 2 * near.shape[0], width), near.dtype)
        return jnp.concatenate([near, far, pad], axis=0)

    def in_order(near, far):
        return jnp.where(x == 0, jnp.stack([near, far]), jnp.stack([far, near]))

    gathered, far = gather_weights(
        [(w_qkv, 0, True), (w_qkv, 1, False)], [take(image_in, 1 - x), take(text_in, 1 - x)], 0
    )
    weight_qkv = gathered
    streams = (join(take(image_in), far[0], 2 * image_half), join(take(text_in), far[1], text_rows))
    text_weights = [gather_offloaded(w_out, 1, (weight_qkv[0],))]
    gains = take(modulation)
    info = jnp.stack([take(text_len), jnp.int32(text_half), x.astype(jnp.int32)])
    small = gather_small(jnp.concatenate([b_qkv, b_out, b_up, b_down], axis=1))
    biases, start = [], 0
    for b in (b_qkv, b_out, b_up, b_down):
        biases.append(small[:, :, start : start + b.shape[1]].reshape(2, -1).astype(jnp.float32))
        start += b.shape[1]
    bias_qkv, bias_out, bias_up, bias_down = biases

    fronts = []
    for s in range(2):
        mod = gains[s]
        normed, inverse = normalize(streams[s].astype(jnp.float32))
        modded = (normed * (1.0 + mod[1]) + mod[0]).astype(jnp.bfloat16)
        projected = linear(modded, weight_qkv[s], bias_qkv[s]).astype(jnp.bfloat16)
        fronts.append((normed, inverse, modded, projected))
    (att_i, att_t, lse), image_weights, far = attend_and_gather(
        fronts[0][3],
        fronts[1][3],
        info,
        2 * image_half,
        [(w_out, 0, True), (w_up, 0, False), (w_down, 0, True)],
        [take(d_image, 1 - x), take(d_text, 1 - x)],
        1,
    )
    cotangents = (join(take(d_image), far[0], 2 * image_half), join(take(d_text), far[1], text_rows))
    text_weights += [gather_offloaded(w, 1, (image_weights[0],)) for w in (w_up, w_down)]
    weight_out, weight_up, weight_down = zip(image_weights, text_weights)

    outs, backs, column_sums, parts = [], [], [], {}
    token = att_i
    for s in range(2):
        mod = gains[s]
        attended = after((att_i, att_t)[s], token)
        upstream = cotangents[s].astype(jnp.float32)
        d_mlp = (mod[5] * upstream).astype(jnp.bfloat16)
        branch = linear(attended, weight_out[s], bias_out[s])
        middle = streams[s].astype(jnp.float32) + mod[2] * branch
        normed_two, inverse_two = normalize(middle)
        modded_two = (normed_two * (1.0 + mod[4]) + mod[3]).astype(jnp.bfloat16)
        if s == 1:
            text_mlp = gather_plane(modded_two, d_mlp, fronts[1][2])
        hidden = linear(modded_two, weight_up[s], bias_up[s])
        active, slope = gelu_both(hidden)
        if s == 0:
            far_active, far_d_mlp = flip_core(active), flip_core(d_mlp)
        mlp_out = linear(active, weight_down[s], bias_down[s])
        outs.append((middle + mod[5] * mlp_out).astype(jnp.bfloat16))
        d_gate_two = jnp.sum(upstream * mlp_out, axis=0)
        if s == 0:
            parts["down"] = partial_grad(after(active, outs[s]), d_mlp, far_active, far_d_mlp)
            d_mlp = after(d_mlp, parts["down"])
        d_active = linear_back(d_mlp, weight_down[s])
        d_hidden = (slope.astype(jnp.float32) * d_active).astype(jnp.bfloat16)
        if s == 0:
            far_d_hidden, far_modded_two = flip_core(d_hidden), flip_core(modded_two)
        d_modded_two = linear_back(d_hidden, weight_up[s])
        d_shift_two = jnp.sum(d_modded_two, axis=0)
        d_scale_two = jnp.sum(d_modded_two * normed_two, axis=0)
        d_middle = upstream + normalize_back(normed_two, inverse_two, d_modded_two * (1.0 + mod[4]))
        d_gate_one = jnp.sum(d_middle * branch, axis=0)
        d_branch = (mod[2] * d_middle).astype(jnp.bfloat16)
        if s == 0:
            parts["up"] = partial_grad(after(modded_two, d_branch), d_hidden, far_modded_two, far_d_hidden)
            far_attended, far_d_branch = flip_core(attended), flip_core(d_branch)
            d_branch = after(d_branch, parts["up"])
        else:
            text_out = (attended, d_branch)
        d_attended = linear_back(d_branch, weight_out[s]).astype(jnp.bfloat16)
        if s == 0:
            parts["out"] = partial_grad(after(attended, d_attended), d_branch, far_attended, far_d_branch)
            token = parts["out"]
        column_sums.append([column_sum(a) for a in (d_branch, d_hidden, d_mlp)])
        backs.append((d_attended, d_middle, d_gate_one, d_shift_two, d_scale_two, d_gate_two))
    sent = [outs[0][image_half:], outs[1][text_half : 2 * text_half]]
    text_totals = plane_mlp_totals(text_mlp[0], after(text_mlp[1], backs[1][0]), weight_up[1], bias_up[1], weight_down[1])
    far_text_modded = text_mlp[2]
    d_front, reduced, far_outs = attend_back_and_reduce(
        fronts[0][3],
        fronts[1][3],
        att_i,
        att_t,
        backs[0][0],
        backs[1][0],
        lse,
        info,
        image_half // 2,
        [parts["down"], parts["up"], parts["out"]],
        [(0, True, 0, parts["down"].shape[1]), (1, False, 0, parts["up"].shape[1]), (2, True, 0, parts["out"].shape[1])],
        sent,
        text_totals,
        2,
    )
    text_qkv, *text_out = gather_plane(d_front[1], *text_out)
    text_down, text_up = sum_fsdp(*text_totals)
    text_up = spread_up(text_up)
    text_out_total = plane_total(*text_out)
    far_front, far_modded = flip_core(d_front[0]), flip_core(fronts[0][2])
    grads = {("down", 0): reduced[0], ("up", 0): reduced[1], ("out", 0): reduced[2]}
    input_grads, gain_grads = [], []
    for s in range(2):
        mod = gains[s]
        normed, inverse, modded, _ = fronts[s]
        d_attended, d_middle, d_gate_one, d_shift_two, d_scale_two, d_gate_two = backs[s]
        d_modded = linear_back(d_front[s], weight_qkv[s])
        d_shift_one = jnp.sum(d_modded, axis=0)
        d_scale_one = jnp.sum(d_modded * normed, axis=0)
        input_grads.append(d_middle + normalize_back(normed, inverse, d_modded * (1.0 + mod[1])))
        gain_grads.append(
            jnp.stack([d_shift_one, d_scale_one, d_gate_one, d_shift_two, d_scale_two, d_gate_two])
        )
    mine = jnp.stack(gain_grads)
    part = partial_grad(after(fronts[0][2], *input_grads), d_front[0], far_modded, far_front)
    text_qkv_total = plane_total(far_text_modded, after(text_qkv, part))
    cols = part.shape[1]
    sent = [input_grads[0][image_half:].astype(jnp.bfloat16), input_grads[1][text_half : 2 * text_half].astype(jnp.bfloat16)]
    front_sums = [column_sum(d_front[s]) for s in range(2)]
    small = jnp.concatenate([front_sums[s] for s in range(2)] + [v for s in range(2) for v in column_sums[s]])
    reduced, far_grads, small = reduce_weights(
        [part],
        [(0, True, 0, cols // 2), (0, False, cols // 2, cols // 2)],
        sent + [mine.reshape(-1, width)],
        small.reshape(-1, 128),
        [text_qkv_total, text_out_total],
        3,
    )
    grads["qkv", 0] = reduced[0]
    grads["down", 1], grads["up", 1] = text_down.astype(jnp.float32), text_up
    for name, total in zip(("out", "qkv"), sum_fsdp(text_out_total, text_qkv_total)):
        grads[name, 1] = total.astype(jnp.float32)
    grad_modulation = in_order(mine, far_grads[2].reshape(mine.shape))

    count = lax.axis_size(("seq", "fsdp") + DP)
    index = lax.axis_index(("seq", "fsdp") + DP)

    def cut_bias(total):
        return lax.dynamic_index_in_dim(total.reshape(2, count, -1), index, 1, keepdims=False)

    small = small.reshape(-1)
    front = front_sums[0].shape[0]
    per_stream = small[2 * front :].reshape(2, -1)
    sizes = [a.shape[0] for a in column_sums[0]]
    gb_qkv = cut_bias(small[: 2 * front].reshape(2, front))
    gb_out, gb_up, gb_down = [
        cut_bias(a) for a in jnp.split(per_stream, [sizes[0], sizes[0] + sizes[1]], axis=1)
    ]
    grads_qkv, grads_out, grads_up, grads_down = [
        jnp.stack([grads[name, s] for s in range(2)]) for name in ("qkv", "out", "up", "down")
    ]
    halves = (image_half, text_half)
    return (
        *[in_order(outs[s][: halves[s]], far_outs[s]) for s in range(2)],
        *[in_order(input_grads[s][: halves[s]], far_grads[s].astype(jnp.float32)) for s in range(2)],
        grad_modulation,
        grads_qkv,
        gb_qkv,
        grads_out,
        gb_out,
        grads_up,
        gb_up,
        grads_down,
        gb_down,
    )


def solution(mesh):
    seq, fsdp, dp = (mesh.shape[name] for name in ("seq", "fsdp", "dp"))
    split = Mesh(mesh.devices.reshape(seq, fsdp, dp // 2, 2), ("seq", "fsdp", "y", "core"))
    batch = ("fsdp",) + DP
    tokens = P(batch, "seq", None)
    weight, bias = P(None, "fsdp", None), P(None, "fsdp")
    in_specs = (tokens, tokens, P(batch, None, None, None), P(batch))
    in_specs += (weight, bias) * 4 + (tokens, tokens)
    everywhere = ("seq",) + batch
    grad_w, grad_b = P(None, everywhere, None), P(None, everywhere)
    out_specs = (tokens,) * 4 + (P(batch, None, None, None),) + (grad_w, grad_b) * 4
    return jax.shard_map(local, mesh=split, in_specs=in_specs, out_specs=out_specs, check_vma=False)
```

```python
import functools

import jax
import jax.numpy as jnp
from jax import lax
from jax.experimental import pallas as pl
from jax.experimental.pallas import tpu as pltpu
from jax.sharding import Mesh, PartitionSpec as P

EPSILON = 1e-06
HEAD_DIM=64
MASKED=-1000000000.0
def dot(a,b,ca,cb):
    return lax.dot_general(a,b,(((ca,),(cb,)),((),())),preferred_element_type=jnp.float32)

def attn_fwd_kernel(ti,tt,tq,len_ref,qi,ki,vi,qt,kt,vt,oi,ot,lse,ktp,vtp):
    tp=ktp.shape[0]
    ktp[...]=jnp.zeros_like(ktp); vtp[...]=jnp.zeros_like(vtp)
    ktp[:tt,:]=kt[...]; vtp[:tt,:]=vt[...]
    n_len=len_ref[0]; half=len_ref[1]; mine=len_ref[2]
    r=lax.broadcasted_iota(jnp.int32,(1,tp),1)
    pos=jnp.where(r<half,mine*half+r,(1-mine)*half+r-half)
    valid=(r<2*half)&(pos<n_len)
    lane=lax.broadcasted_iota(jnp.int32,(1,2*HEAD_DIM),1)
    k_img=ki[...]; v_img=vi[...]; k_txt=ktp[...]; v_txt=vtp[...]
    def one(q,rows):
        outs=[];lses=[]
        for h in range(2):
            qh=jnp.where((lane<HEAD_DIM)==(h==0),q.astype(jnp.float32)*(HEAD_DIM**-0.5),0.0).astype(jnp.bfloat16)
            s1=dot(qh,k_img,1,1); s2=dot(qh,k_txt,1,1)
            s2=jnp.where(valid,s2,MASKED)
            m=jnp.maximum(jnp.max(s1,axis=1,keepdims=True),jnp.max(s2,axis=1,keepdims=True))
            e1=jnp.exp(s1-m); e2=jnp.exp(s2-m)
            l=jnp.sum(e1,axis=1,keepdims=True)+jnp.sum(e2,axis=1,keepdims=True)
            inv=1.0/l
            o=dot((e1*inv).astype(jnp.bfloat16),v_img,1,0)+dot((e2*inv).astype(jnp.bfloat16),v_txt,1,0)
            outs.append(o); lses.append(m+jnp.log(l))
        o=jnp.where(lane<HEAD_DIM,outs[0],outs[1]).astype(jnp.bfloat16)
        both=jnp.where(lane<HEAD_DIM,jnp.broadcast_to(lses[0],(rows,128)),jnp.broadcast_to(lses[1],(rows,128)))
        return o,both.T
    def step(i,_):
        start=pl.multiple_of(i*tq,tq)
        o,b=one(qi[pl.ds(start,tq),:],tq)
        oi[pl.ds(start,tq),:]=o
        lse[0,0:1,pl.ds(start,tq)]=b[0:1]; lse[0,1:2,pl.ds(start,tq)]=b[64:65]
        return 0
    lax.fori_loop(0,ti//tq,step,0)
    qpad=jnp.concatenate([qt[...],jnp.zeros((tp-tt,128),jnp.bfloat16)],axis=0)
    o,b=one(qpad,tp)
    ot[...]=o[:tt]
    lse[0,0:1,ti:ti+tp]=b[0:1]; lse[0,1:2,ti:ti+tp]=b[64:65]

def attn_bwd_kernel(ti,tt,tq,len_ref,qi,ki,vi,qt,kt,vt,oi,ot,di,dt,lse,outi,outt,ktp,vtp,dk1,dk2,dv1,dv2,dqi,dqt):
    j=pl.program_id(1)
    tp=ktp.shape[0]
    @pl.when(j==0)
    def _():
        ktp[...]=jnp.zeros_like(ktp); vtp[...]=jnp.zeros_like(vtp)
        ktp[:tt,:]=kt[...]; vtp[:tt,:]=vt[...]
        n_len=len_ref[0]; half=len_ref[1]; mine=len_ref[2]
        r=lax.broadcasted_iota(jnp.int32,(tp,1),0)
        pos=jnp.where(r<half,mine*half+r,(1-mine)*half+r-half)
        valid=(r<2*half)&(pos<n_len)
        lane=lax.broadcasted_iota(jnp.int32,(1,128),1)
        sub=lax.broadcasted_iota(jnp.int32,(8,128),0); lane8=lax.broadcasted_iota(jnp.int32,(8,128),1)
        sel=jnp.where((lane8//HEAD_DIM)==sub,1.0,0.0).astype(jnp.bfloat16)
        k_img=ki[...]; v_img=vi[...]; k_txt=ktp[...]; v_txt=vtp[...]
        for ref in (dk1,dk2,dv1,dv2): ref[...]=jnp.zeros_like(ref)
        def one(q,do,o,ls):
            prod=do.astype(jnp.float32)*o.astype(jnp.float32)
            hi=prod.astype(jnp.bfloat16); lo=(prod-hi.astype(jnp.float32)).astype(jnp.bfloat16)
            dsum=dot(sel,hi,1,1)+dot(sel,lo,1,1)
            qs=(q.astype(jnp.float32)*(HEAD_DIM**-0.5))
            dof=do.astype(jnp.float32)
            dqs=[]
            for h in range(2):
                mk=(lane<HEAD_DIM)==(h==0)
                qh=jnp.where(mk,qs,0.0).astype(jnp.bfloat16)
                dh=jnp.where(mk,dof,0.0).astype(jnp.bfloat16)
                L=ls[h:h+1]; D=dsum[h:h+1]
                s1=dot(k_img,qh,1,1); s2=dot(k_txt,qh,1,1)
                p1=jnp.exp(s1-L); p2=jnp.where(valid,jnp.exp(s2-L),0.0)
                dp1=dot(v_img,dh,1,1); dp2=dot(v_txt,dh,1,1)
                ds1=(p1*(dp1-D)).astype(jnp.bfloat16); ds2=(p2*(dp2-D)).astype(jnp.bfloat16)
                dv1[...]+=dot(p1.astype(jnp.bfloat16),dh,1,0)
                dv2[...]+=dot(p2.astype(jnp.bfloat16),dh,1,0)
                dk1[...]+=dot(ds1,qh,1,0)
                dk2[...]+=dot(ds2,qh,1,0)
                dqs.append(dot(ds1,k_img,0,0)+dot(ds2,k_txt,0,0))
            return (jnp.where(lane<HEAD_DIM,dqs[0],dqs[1])*(HEAD_DIM**-0.5)).astype(jnp.bfloat16)
        def step(i,_):
            start=pl.multiple_of(i*tq,tq)
            sl=pl.ds(start,tq)
            dqi[sl,:]=one(qi[sl,:],di[sl,:],oi[sl,:],lse[0,:,sl])
            return 0
        lax.fori_loop(0,ti//tq,step,0)
        pad=lambda a: jnp.concatenate([a,jnp.zeros((tp-tt,128),jnp.bfloat16)],axis=0)
        dqt[...]=one(pad(qt[...]),pad(dt[...]),pad(ot[...]),lse[0,:,ti:ti+tp])[:tt]
        outi[...]=dqi[...]; outt[...]=dqt[...]
    @pl.when(j==1)
    def _():
        outi[...]=dk1[...].astype(jnp.bfloat16); outt[...]=dk2[:tt,:].astype(jnp.bfloat16)
    @pl.when(j==2)
    def _():
        outi[...]=dv1[...].astype(jnp.bfloat16); outt[...]=dv2[:tt,:].astype(jnp.bfloat16)


def normalize(values):
    row_mean = jnp.mean(values, axis=-1, keepdims=True)
    centred = values - row_mean
    variance = jnp.mean(centred * centred, axis=-1, keepdims=True)
    inverse = lax.rsqrt(variance + EPSILON)
    return (centred * inverse, inverse)


def normalize_back(normed, inverse, upstream):
    mean_one = jnp.mean(upstream, axis=-1, keepdims=True)
    mean_two = jnp.mean(upstream * normed, axis=-1, keepdims=True)
    return inverse * (upstream - mean_one - normed * mean_two)


def linear(values, weight, offset):
    return jnp.dot(values, weight, preferred_element_type=jnp.float32) + offset.astype(jnp.float32)


def linear_back(upstream, weight):
    return dot(upstream, weight, 1, 1)


def gelu_both(values):
    inner = jnp.tanh(0.7978845608028654 * values * (1.0 + 0.044715 * values * values))
    half = 0.5 * (1.0 + inner)
    slope = half + 0.5 * values * (1.0 - inner * inner) * (0.7978845608028654 * (1.0 + 0.134145 * values * values))
    return (values * half).astype(jnp.bfloat16), slope.astype(jnp.bfloat16)


def column_sum(values):
    return dot(jnp.ones((8, values.shape[0]), values.dtype), values, 1, 0)[0]


DP = ("y", "core")


def coords():
    dp = lax.axis_index(DP)
    return lax.axis_index("seq"), lax.axis_index("fsdp"), dp // 4, (dp // 2) % 2, dp % 2


def flip_x(a):
    return lax.ppermute(a, "seq", [(0, 1), (1, 0)])


def flip_y(a):
    return lax.ppermute(a, DP, [(i, i ^ 2) for i in range(lax.axis_size(DP))])


def flip_core(a):
    return lax.ppermute(a, DP, [(i, i ^ 1) for i in range(lax.axis_size(DP))])


def shift_z(a, k):
    n = lax.axis_size("fsdp")
    return lax.ppermute(a, "fsdp", [(i, (i + k) % n) for i in range(n)])


def shift_group(a, k):
    n = lax.axis_size(DP)
    return lax.ppermute(a, DP, [(i, (i + 4 * k) % n) for i in range(n)])


def after(value, *earlier):
    return lax.optimization_barrier((value, *earlier))[0]


def enter(z_too=True, y_too=True, core_too=True):
    fs = lax.axis_size("fsdp")
    x, z, _, y, c = coords()
    targets = [{"seq": 1 - x}]
    if y_too:
        targets.append({"y": lax.axis_index("y") + 1 - 2 * y})
    if core_too:
        targets.append({"core": 1 - c})
    if z_too:
        targets += [{"fsdp": lax.rem(z + k, fs)} for k in range(1, fs)]
    barrier = pltpu.get_barrier_semaphore()
    for target in targets:
        pl.semaphore_signal(barrier, inc=1, device_id=target, device_id_type=pl.DeviceIdType.MESH)
    pl.semaphore_wait(barrier, len(targets))


def swap_copies(srcs, dsts, sems):
    x = lax.axis_index("seq")
    return [
        pltpu.make_async_remote_copy(
            src_ref=src,
            dst_ref=dst,
            send_sem=sems.at[i, 0],
            recv_sem=sems.at[i, 1],
            device_id={"seq": 1 - x},
            device_id_type=pl.DeviceIdType.MESH,
        )
        for i, (src, dst) in enumerate(zip(srcs, dsts))
    ]


def gather_plan(units, shards, outs, bufs, local_sem, send_sem, recv_sem):
    fs = lax.axis_size("fsdp")
    count = len(units)
    kinds = ("first", "second", "core0", "forward", "core1", "core2", "core3")
    x, z, _, y, c = coords()
    to_x, to_y, to_core = {"seq": 1 - x}, {"y": lax.axis_index("y") + 1 - 2 * y}, {"core": 1 - c}

    def remote(src, dst, u, slot, target):
        return pltpu.make_async_remote_copy(
            src_ref=src,
            dst_ref=dst,
            send_sem=send_sem.at[u, slot],
            recv_sem=recv_sem.at[u, slot],
            device_id=target,
            device_id_type=pl.DeviceIdType.MESH,
        )

    def spot(u, from_z, dx, dy, cc):
        _, r, cols = units[u][0].shape
        q, h = r // 4, cols // 2
        xx = 1 - x if dx else x
        yy = 1 - y if dy else y
        row = pl.multiple_of(from_z * r + (xx * 2 + yy) * q, 16)
        return outs[u].at[pl.ds(row, q), pl.ds(pl.multiple_of(cc * h, 128), h)]

    def copy(u, kind, k):
        _, r, cols = units[u][0].shape
        q, h = r // 4, cols // 2
        if kind == "z":
            dst = spot(u, lax.rem(z - k + 1 + fs, fs), 0, 0, c)
            row = pl.multiple_of((x * 2 + y) * q, 16)
            own_piece = shards[u].at[units[u][1], pl.ds(row, q), pl.ds(pl.multiple_of(c * h, 128), h)]
            return remote(own_piece if k == 1 else dst, dst, u, k - 1, {"fsdp": lax.rem(z + 1, fs)})
        x_first = units[u][2]
        slot = (1 + kinds.index(kind)) * (fs - 1) + k - 1
        via = (1, 0) if x_first else (0, 1)
        other = (0, 1) if x_first else (1, 0)
        where, target = {
            "first": ((0, 0), to_x if x_first else to_y),
            "second": ((0, 0), to_y if x_first else to_x),
            "core0": ((0, 0), to_core),
            "forward": (via, to_y if x_first else to_x),
            "core1": (via, to_core),
            "core2": (other, to_core),
            "core3": ((1, 1), to_core),
        }[kind]
        place = spot(u, lax.rem(z - k + fs, fs), *where, c)
        return remote(place, place, u, slot, target)

    def fetch(u):
        return pltpu.make_async_copy(shards[u].at[units[u][1]], bufs[u], local_sem.at[u, 0])

    def own(u):
        r = units[u][0].shape[1]
        return pltpu.make_async_copy(
            bufs[u], outs[u].at[pl.ds(pl.multiple_of(z * r, 16), r), :], local_sem.at[u, 1]
        )

    ahead = min(2, count)
    order = [(u, k) for k in range(1, fs) for u in range(count)]

    def begin():
        for u, k in order[:ahead]:
            copy(u, "z", k).start()
        for u in range(count):
            fetch(u).start()
        for u in range(count):
            fetch(u).wait()
            own(u).start()

    def act(i):
        if i < len(order):
            u, k = order[i]
            copy(u, "z", k).wait_recv()
            if i + ahead < len(order):
                copy(order[i + ahead][0], "z", order[i + ahead][1]).start()
            for kind in ("first", "second", "core0"):
                copy(u, kind, k).start()
        if 0 <= i - lag < len(order):
            u, k = order[i - lag]
            copy(u, "first", k).wait_recv()
            copy(u, "forward", k).start()
            copy(u, "core1", k).start()
        if 0 <= i - 2 * lag < len(order):
            u, k = order[i - 2 * lag]
            copy(u, "second", k).wait_recv()
            copy(u, "core2", k).start()
            copy(u, "forward", k).wait_recv()
            copy(u, "core3", k).start()

    lag = 2
    actions = [functools.partial(act, i) for i in range(len(order) + 2 * lag)]

    def end():
        for u in range(count):
            for k in range(1, fs):
                for kind in ("core0", "core1", "core2", "core3"):
                    copy(u, kind, k).wait_recv()
                for kind in ("z",) + kinds:
                    copy(u, kind, k).wait_send()
            own(u).wait()

    return begin, actions, end


def gather_shapes(units):
    fs = lax.axis_size("fsdp")
    return [jax.ShapeDtypeStruct((u[0].shape[1] * fs, u[0].shape[2]), u[0].dtype) for u in units]


def gather_scratch(units, swaps):
    fs = lax.axis_size("fsdp")
    return [pltpu.VMEM(u[0].shape[1:], u[0].dtype) for u in units] + [
        pltpu.SemaphoreType.DMA((len(units), 2)),
        pltpu.SemaphoreType.DMA((len(units), 8 * (fs - 1))),
        pltpu.SemaphoreType.DMA((len(units), 8 * (fs - 1))),
        pltpu.SemaphoreType.DMA((max(len(swaps), 1), 2)),
    ]


def gather_weights(units, swaps, collective_id):
    count, n = len(units), len(units) + len(swaps)

    def kernel(*refs):
        shards, near, outs, far = refs[:count], refs[count:n], refs[n : n + count], refs[n + count : 2 * n]
        enter()
        swapped = swap_copies(near, far, refs[-1])
        for cp in swapped:
            cp.start()
        begin, actions, end = gather_plan(units, shards, outs, refs[2 * n : 2 * n + count], *refs[-4:-1])
        begin()
        for action in actions:
            action()
        end()
        for cp in swapped:
            cp.wait()

    results = pl.pallas_call(
        kernel,
        out_shape=gather_shapes(units) + [jax.ShapeDtypeStruct(a.shape, a.dtype) for a in swaps],
        in_specs=[pl.BlockSpec(memory_space=pl.ANY)] * n,
        out_specs=[pl.BlockSpec(memory_space=pl.ANY)] * n,
        scratch_shapes=gather_scratch(units, swaps),
        compiler_params=pltpu.CompilerParams(
            collective_id=collective_id, has_side_effects=True, vmem_limit_bytes=48 << 20
        ),
        name="gather_weights",
    )(*[u[0] for u in units], *swaps)
    return results[:count], results[count:]


def attend_and_gather(qkv_i, qkv_t, info, tq, units, swaps, collective_id):
    ti, w3 = qkv_i.shape
    tt, w, tp = qkv_t.shape[0], w3 // 3, 256
    steps = w // 128
    count, n = len(units), len(units) + len(swaps)
    bi = lambda off: pl.BlockSpec((ti, 128), lambda p, s, off=off: (0, p + off * steps))
    bt = lambda off: pl.BlockSpec((tt, 128), lambda p, s, off=off: (0, p + off * steps))

    def kernel(*refs):
        info_ref, attn_in = refs[0], refs[1:7]
        shards, near = refs[7 : 7 + count], refs[7 + count : 7 + n]
        attn_out, rest = refs[7 + n : 10 + n], refs[10 + n :]
        outs, far, pads = rest[:count], rest[count:n], rest[n : n + 2]
        step = pl.program_id(0)
        swapped = swap_copies(near, far, refs[-1])
        begin, actions, end = gather_plan(units, shards, outs, rest[n + 2 : n + 2 + count], *refs[-4:-1])

        @pl.when(step == 0)
        def _():
            enter()
            begin()
            for cp in swapped:
                cp.start()

        early = min(steps - 2, len(actions))
        for index in range(early):
            pl.when(step == index + 2)(actions[index])
        attn_fwd_kernel(ti, tt, tq, info_ref, *attn_in, *attn_out, *pads)

        @pl.when(step == steps - 1)
        def _():
            for action in actions[early:]:
                action()
            end()
            for cp in swapped:
                cp.wait()

    results = pl.pallas_call(
        kernel,
        grid_spec=pltpu.PrefetchScalarGridSpec(
            num_scalar_prefetch=1,
            grid=(steps,),
            in_specs=[bi(0), bi(1), bi(2), bt(0), bt(1), bt(2)] + [pl.BlockSpec(memory_space=pl.ANY)] * n,
            out_specs=[bi(0), bt(0), pl.BlockSpec((1, 8, ti + tp), lambda p, s: (p, 0, 0))]
            + [pl.BlockSpec(memory_space=pl.ANY)] * n,
            scratch_shapes=[pltpu.VMEM((tp, 128), jnp.bfloat16)] * 2 + gather_scratch(units, swaps),
        ),
        out_shape=[
            jax.ShapeDtypeStruct((ti, w), jnp.bfloat16),
            jax.ShapeDtypeStruct((tt, w), jnp.bfloat16),
            jax.ShapeDtypeStruct((steps, 8, ti + tp), jnp.float32),
        ]
        + gather_shapes(units)
        + [jax.ShapeDtypeStruct(a.shape, a.dtype) for a in swaps],
        compiler_params=pltpu.CompilerParams(
            collective_id=collective_id, has_side_effects=True, vmem_limit_bytes=56 << 20
        ),
        name="attend_and_gather",
    )(info, qkv_i, qkv_i, qkv_i, qkv_t, qkv_t, qkv_t, *[u[0] for u in units], *swaps)
    return results[:3], results[3 : 3 + count], results[3 + count :]


def reduce_plan(units, ins, outs, scratch, totals, load_sem, send_sem, recv_sem, out_sem):
    fs = lax.axis_size("fsdp")
    count = len(units)
    x, z, _, y, c = coords()
    to_x, to_y = {"seq": 1 - x}, {"y": lax.axis_index("y") + 1 - 2 * y}
    f32 = lambda a: a.astype(jnp.float32)

    def remote(u, slot, src, dst, target):
        return pltpu.make_async_remote_copy(
            src_ref=src,
            dst_ref=dst,
            send_sem=send_sem.at[u, slot],
            recv_sem=recv_sem.at[u, slot],
            device_id=target,
            device_id_type=pl.DeviceIdType.MESH,
        )

    def rows(u, k, mine):
        index, x_first, start, width = units[u]
        zz = lax.rem(z + k, fs)
        cols = pl.ds(start, width)
        if x_first:
            return ins[index].at[x if mine else 1 - x, zz, :, :, :, :, cols]
        return ins[index].at[:, zz, :, y if mine else 1 - y, :, :, cols]

    def load(u, k):
        return pltpu.make_async_copy(rows(u, k, True), scratch[4 * u].at[k - 1], load_sem.at[u, k - 1])

    def side(u, ref, k, mine):
        x_first = units[u][1]
        index = (y if mine else 1 - y) if x_first else (x if mine else 1 - x)
        return ref.at[k - 1, :, index] if x_first else ref.at[k - 1, index]

    def hop(u, stage, k):
        part, recv_one, recv_two, recv_three = scratch[4 * u : 4 * u + 4]
        x_first = units[u][1]
        if stage == 1:
            return remote(u, k - 1, rows(u, k, False), recv_one.at[k - 1], to_x if x_first else to_y)
        if stage == 2:
            return remote(u, fs + k - 1, side(u, part, k, False), recv_two.at[k - 1], to_y if x_first else to_x)
        return remote(
            u, 2 * fs + k - 1, recv_two.at[k - 1], recv_three.at[k - 1], {"fsdp": lax.rem(z + k, fs)}
        )

    def second(u, k):
        part, recv_one = scratch[4 * u : 4 * u + 2]
        load(u, k).wait()
        if k + ahead > fs:
            hop(u, 1, k).wait_recv()
        spot = side(u, part, k, False)
        spot[...] = (f32(spot[...]) + f32(side(u, recv_one, k, False)[...])).astype(jnp.bfloat16)
        hop(u, 2, k).start()

    def third(u, k):
        part, recv_one, recv_two = scratch[4 * u : 4 * u + 3]
        hop(u, 2, k).wait_recv()
        total = f32(side(u, part, k, True)[...]) + f32(side(u, recv_one, k, True)[...]) + f32(recv_two[k - 1])
        if k < fs:
            recv_two[k - 1] = total.astype(jnp.bfloat16)
            hop(u, 3, k).start()
        else:
            index, _, start, width = units[u]
            totals[index][:, :, :, start : start + width] = total

    ahead = 1

    def begin():
        for k in range(1, fs + 1):
            for u in range(count):
                if k <= ahead:
                    hop(u, 1, k).start()
                load(u, k).start()

    def stage(k):
        if k + ahead <= fs:
            for u in range(count):
                hop(u, 1, k).wait_recv()
            for u in range(count):
                hop(u, 1, k + ahead).start()
        for u in range(count):
            if k <= fs:
                second(u, k)
        for u in range(count):
            if k > 1:
                third(u, k - 1)

    actions = [functools.partial(stage, k) for k in range(1, fs + 2)]

    def end():
        for u in range(count):
            index, _, start, width = units[u]
            total = totals[index][:, :, :, start : start + width]
            for k in range(1, fs):
                hop(u, 3, k).wait_recv()
                total = total + f32(scratch[4 * u + 3][k - 1])
            totals[index][:, :, :, start : start + width] = total
        stores, sends = [], []
        for i, (total, out) in enumerate(zip(totals, outs)):
            h = total.shape[-1]
            place = out.at[:, :, pl.ds(pl.multiple_of(c * h, 128), h)]
            stores.append(pltpu.make_async_copy(total.at[:, c], place, out_sem.at[i, 0]))
            sends.append(
                pltpu.make_async_remote_copy(
                    src_ref=total.at[:, 1 - c],
                    dst_ref=place,
                    send_sem=out_sem.at[i, 1],
                    recv_sem=out_sem.at[i, 2],
                    device_id={"core": 1 - c},
                    device_id_type=pl.DeviceIdType.MESH,
                )
            )
        for cp in stores + sends:
            cp.start()
        for u in range(count):
            for k in range(1, fs + 1):
                for number in (1, 2, 3) if k < fs else (1, 2):
                    hop(u, number, k).wait_send()
        for cp in stores + sends:
            cp.wait()

    return begin, actions, end


def reduce_views(partials):
    fs, groups = lax.axis_size("fsdp"), lax.axis_size(DP) // 4
    return [p.reshape(2, fs, groups, 2, 2, -1, p.shape[1]) for p in partials]


def reduce_scratch(arrays, units, swaps):
    fs, groups = lax.axis_size("fsdp"), lax.axis_size(DP) // 4
    scratch = []
    for index, x_first, _, width in units:
        rows = arrays[index].shape[5]
        both = (groups, 2, 2, rows, width) if x_first else (2, groups, 2, rows, width)
        one = (groups, 2, rows, width)
        for shape in ((fs, *both), (fs, *both), (fs, *one), (fs - 1, *one)):
            scratch.append(pltpu.VMEM(shape, jnp.bfloat16))
    scratch += [pltpu.VMEM((groups, 2, *a.shape[5:]), jnp.float32) for a in arrays]
    return scratch + [
        pltpu.SemaphoreType.DMA((len(units), fs)),
        pltpu.SemaphoreType.DMA((len(units), 3 * fs)),
        pltpu.SemaphoreType.DMA((len(units), 3 * fs)),
        pltpu.SemaphoreType.DMA((len(arrays), 3)),
        pltpu.SemaphoreType.DMA((max(len(swaps), 1), 2)),
    ]


def reduce_shapes(arrays, swaps):
    groups = lax.axis_size(DP) // 4
    return [jax.ShapeDtypeStruct((groups, a.shape[5], 2 * a.shape[6]), jnp.float32) for a in arrays] + [
        jax.ShapeDtypeStruct(a.shape, a.dtype) for a in swaps
    ]


def finish_reduce(results):
    finals = []
    for total in results:
        groups, g = total.shape[0], lax.axis_index(DP) // 4
        at = lambda i: lax.dynamic_index_in_dim(total, i, 0, keepdims=False)
        mine = at(g)
        for k in range(1, groups):
            mine = mine + shift_group(at((g + k) % groups), k)
        finals.append(mine)
    return finals


def reduce_weights(partials, units, swaps, small, earlier, collective_id):
    fs, groups = lax.axis_size("fsdp"), lax.axis_size(DP) // 4
    arrays = reduce_views(partials)
    held = len(arrays)
    n, size = held + len(swaps), 4 * len(units)
    hops = 3 + fs - 1

    def kernel(*refs):
        ins, near, small_in = refs[:held], refs[held:n], refs[n]
        refs = refs[: n + 1] + refs[n + 1 + len(earlier) :]
        outs, far, small_out = refs[n + 1 : n + 1 + held], refs[n + 1 + held : 2 * n + 1], refs[2 * n + 1]
        rest = refs[2 * n + 2 :]
        scratch, totals = rest[:size], rest[size : size + held]
        staged, landed, small_sem = rest[size + held : size + held + 3]
        x, z, _, y, c = coords()
        enter()
        begin, actions, end = reduce_plan(units, ins, outs, scratch, totals, *refs[-5:-1])
        swapped = swap_copies(near, far, refs[-1])
        targets = [{"core": 1 - c}, {"seq": 1 - x}, {"y": lax.axis_index("y") + 1 - 2 * y}]
        targets += [{"fsdp": lax.rem(z + k, fs)} for k in range(1, fs)]

        def small_hop(i):
            return pltpu.make_async_remote_copy(
                src_ref=staged.at[min(i, 3)],
                dst_ref=landed.at[i],
                send_sem=small_sem.at[0, i],
                recv_sem=small_sem.at[1, i],
                device_id=targets[i],
                device_id_type=pl.DeviceIdType.MESH,
            )

        staged[0] = small_in[...]
        small_hop(0).start()
        begin()
        for cp in swapped:
            cp.start()
        for index, action in enumerate(actions):
            action()
            if index < 3:
                small_hop(index).wait_recv()
                staged[index + 1] = staged[index] + landed[index]
                for i in (index + 1,) if index < 2 else range(3, hops):
                    small_hop(i).start()
        end()
        total = staged[3]
        for i in range(3, hops):
            small_hop(i).wait_recv()
            total = total + landed[i]
        small_out[...] = total
        for i in range(hops):
            small_hop(i).wait_send()
        for cp in swapped:
            cp.wait()

    results = pl.pallas_call(
        kernel,
        out_shape=reduce_shapes(arrays, swaps) + [jax.ShapeDtypeStruct(small.shape, small.dtype)],
        in_specs=[pl.BlockSpec(memory_space=pl.ANY)] * n
        + [pl.BlockSpec(memory_space=pltpu.VMEM)]
        + [pl.BlockSpec(memory_space=pl.ANY)] * len(earlier),
        out_specs=[pl.BlockSpec(memory_space=pl.ANY)] * n + [pl.BlockSpec(memory_space=pltpu.VMEM)],
        scratch_shapes=(lambda base: base[: size + held]
        + [
            pltpu.VMEM((4, *small.shape), small.dtype),
            pltpu.VMEM((hops, *small.shape), small.dtype),
            pltpu.SemaphoreType.DMA((2, hops)),
        ]
        + base[size + held :])(reduce_scratch(arrays, units, swaps)),
        compiler_params=pltpu.CompilerParams(
            collective_id=collective_id, has_side_effects=True, vmem_limit_bytes=56 << 20
        ),
        name="reduce_weights",
    )(*arrays, *swaps, small, *earlier)
    total = results[-1]
    if groups > 1:
        total = total + sum(shift_group(total, k) for k in range(1, groups))
    return finish_reduce(results[:held]), results[held:-1], total


def attend_back_and_reduce(qkv_i, qkv_t, o_i, o_t, d_i, d_t, lse, info, tq, partials, units, swaps, earlier, collective_id):
    ti, w3 = qkv_i.shape
    tt, w, tp = qkv_t.shape[0], w3 // 3, 256
    steps = w // 128
    arrays = reduce_views(partials)
    held = len(arrays)
    n, size = held + len(swaps), 4 * len(units)
    bi = lambda off: pl.BlockSpec((ti, 128), lambda p, j, s, off=off: (0, p + off * steps))
    bt = lambda off: pl.BlockSpec((tt, 128), lambda p, j, s, off=off: (0, p + off * steps))

    def kernel(*refs):
        info_ref, attn_in = refs[0], refs[1:12]
        ins, near = refs[12 : 12 + held], refs[12 + held : 12 + n]
        refs = refs[: 12 + n] + refs[12 + n + len(earlier) :]
        attn_out, rest = refs[12 + n : 14 + n], refs[14 + n :]
        outs, far, mine = rest[:held], rest[held:n], rest[n : n + 8]
        scratch, totals = rest[n + 8 : n + 8 + size], rest[n + 8 + size : n + 8 + size + held]
        pair, part = pl.program_id(0), pl.program_id(1)
        begin, actions, end = reduce_plan(units, ins, outs, scratch, totals, *refs[-5:-1])
        swapped = swap_copies(near, far, refs[-1])

        @pl.when((pair == 0) & (part == 0))
        def _():
            enter()
            begin()
            for cp in swapped:
                cp.start()

        times = (3, 6, 8, 11)
        early = min(len(times), len(actions) - 1)
        for index, at in zip(range(early), times):
            pl.when((pair == at) & (part == 0))(actions[index])
        attn_bwd_kernel(ti, tt, tq, info_ref, *attn_in, *attn_out, *mine)

        @pl.when((pair == steps - 1) & (part == 2))
        def _():
            for action in actions[early:]:
                action()
            end()
            for cp in swapped:
                cp.wait()

    results = pl.pallas_call(
        kernel,
        grid_spec=pltpu.PrefetchScalarGridSpec(
            num_scalar_prefetch=1,
            grid=(steps, 3),
            in_specs=[bi(0), bi(1), bi(2), bt(0), bt(1), bt(2), bi(0), bt(0), bi(0), bt(0)]
            + [pl.BlockSpec((1, 8, ti + tp), lambda p, j, s: (p, 0, 0))]
            + [pl.BlockSpec(memory_space=pl.ANY)] * (n + len(earlier)),
            out_specs=[
                pl.BlockSpec((ti, 128), lambda p, j, s: (0, p + j * steps)),
                pl.BlockSpec((tt, 128), lambda p, j, s: (0, p + j * steps)),
            ]
            + [pl.BlockSpec(memory_space=pl.ANY)] * n,
            scratch_shapes=[pltpu.VMEM((tp, 128), jnp.bfloat16)] * 2
            + [pltpu.VMEM((ti, 128), jnp.float32), pltpu.VMEM((tp, 128), jnp.float32)] * 2
            + [pltpu.VMEM((ti, 128), jnp.bfloat16), pltpu.VMEM((tt, 128), jnp.bfloat16)]
            + reduce_scratch(arrays, units, swaps),
        ),
        out_shape=[jax.ShapeDtypeStruct((ti, w3), jnp.bfloat16), jax.ShapeDtypeStruct((tt, w3), jnp.bfloat16)]
        + reduce_shapes(arrays, swaps),
        compiler_params=pltpu.CompilerParams(
            collective_id=collective_id, has_side_effects=True, vmem_limit_bytes=60 << 20
        ),
        name="attend_back_and_reduce",
    )(info, qkv_i, qkv_i, qkv_i, qkv_t, qkv_t, qkv_t, o_i, o_t, d_i, d_t, lse, *arrays, *swaps, *earlier)
    return results[:2], finish_reduce(results[2 : 2 + held]), results[2 + held :]


def gather_offloaded(shard, stream, earlier=()):
    x, _, _, _, _ = coords()
    share = shard.shape[1] // (2 * lax.axis_size(DP))
    start = (x * lax.axis_size(DP) + lax.axis_index(DP)) * share
    piece = lax.dynamic_slice(shard, (stream, start, 0), (1, share, shard.shape[2]))[0]
    return lax.all_gather(after(piece, *earlier), ("fsdp", "seq", "y", "core"), axis=0, tiled=True)


def gather_plane(*values):
    both = jnp.concatenate(values, axis=1) if len(values) > 1 else values[0]
    both = lax.all_gather(both, ("seq", "y", "core"), axis=0, tiled=True)
    edges = [0]
    for v in values:
        edges.append(edges[-1] + v.shape[1])
    return [both[:, a:b] for a, b in zip(edges, edges[1:])]


def own_blocks(values, axis):
    fs, n = lax.axis_size("fsdp"), lax.axis_size(DP)
    size = values.shape[axis] // (2 * fs * n)
    start = (lax.axis_index("seq") * fs * n + lax.axis_index(DP)) * size
    return jnp.concatenate(
        [lax.dynamic_slice_in_dim(values, start + f * n * size, size, axis) for f in range(fs)], axis=axis
    )


def sum_fsdp(*totals):
    fs = totals[0].shape[0]
    width = totals[0].shape[-1]
    flat = jnp.concatenate([t.astype(jnp.bfloat16).reshape(fs, -1, width) for t in totals], axis=1)
    mine = lax.psum_scatter(flat.reshape(-1, width), "fsdp", scatter_dimension=0, tiled=True)
    result, start = [], 0
    for t in totals:
        rows = t.size // (fs * width)
        result.append(mine[start : start + rows].reshape(t.shape[1:]))
        start += rows
    return result


def plane_total(left, right):
    total = dot(own_blocks(left, 1), right, 0, 0)
    return total.reshape(lax.axis_size("fsdp"), -1, total.shape[1]).astype(jnp.bfloat16)


def plane_mlp_totals(modded, d_mlp, weight_up, bias_up, weight_down):
    fs = lax.axis_size("fsdp")
    hidden = linear(modded, own_blocks(weight_up, 1), own_blocks(bias_up, 0))
    active, slope = gelu_both(hidden)
    d_active = linear_back(d_mlp, own_blocks(weight_down, 0))
    d_hidden = (slope.astype(jnp.float32) * d_active).astype(jnp.bfloat16)
    down = dot(active, d_mlp, 0, 0).astype(jnp.bfloat16)
    up = dot(modded, d_hidden, 0, 0).astype(jnp.bfloat16)
    rows, units = up.shape
    up = up.reshape(2, fs, rows // (2 * fs), units).transpose(1, 0, 2, 3)
    return down.reshape(fs, -1, down.shape[1]), up


def spread_up(mine):
    fs, n = lax.axis_size("fsdp"), lax.axis_size(DP)
    _, rows, units = mine.shape
    spread = lax.all_gather(mine.reshape(-1, units), ("seq", "y", "core"), axis=0, tiled=True)
    spread = spread.reshape(2 * n, 2, n, rows // n, units)
    spread = lax.dynamic_index_in_dim(spread, lax.axis_index("seq"), 1, keepdims=False)
    spread = lax.dynamic_index_in_dim(spread, lax.axis_index(DP), 1, keepdims=False)
    spread = spread.reshape(2, n, spread.shape[1], fs, -1).transpose(2, 0, 3, 1, 4)
    return spread.reshape(spread.shape[0], -1).astype(jnp.float32)


def gather_small(value):
    fs = lax.axis_size("fsdp")
    z = lax.axis_index("fsdp")
    stack = jnp.stack([value] + [shift_z(value, k) for k in range(1, fs)])
    ordered = [lax.dynamic_index_in_dim(stack, (z - j) % fs, 0, keepdims=False) for j in range(fs)]
    return jnp.stack(ordered, axis=1)


def wgrad_kernel(sel_ref, a0, b0, a1, b1, out, a0t, a1t):
    @pl.when(pl.program_id(1) == 0)
    def _():
        a0t[...] = a0[...].T
        a1t[...] = a1[...].T

    out[...] = (dot(a0t[...], b0[...], 1, 0) + dot(a1t[...], b1[...], 1, 0)).astype(out.dtype)


def wgrad(a0, b0, a1, b1, row_half, col_half):
    tokens, rows = a0.shape
    cols = b0.shape[1]
    tr = tc = 768
    halves = 1 if row_half is None else 2
    nr, nc = rows // halves // tr, cols // 2 // tc
    row_start = jnp.int32(0) if row_half is None else row_half * nr
    a_spec = pl.BlockSpec((tokens, tr), lambda i, j, s: (0, s[0] + i))
    b_spec = pl.BlockSpec((tokens, tc), lambda i, j, s: (0, s[1] + j))
    return pl.pallas_call(
        wgrad_kernel,
        grid_spec=pltpu.PrefetchScalarGridSpec(
            num_scalar_prefetch=1,
            grid=(nr, nc),
            in_specs=[a_spec, b_spec, a_spec, b_spec],
            out_specs=pl.BlockSpec((tr, tc), lambda i, j, s: (i, j)),
            scratch_shapes=[pltpu.VMEM((tr, tokens), a0.dtype)] * 2,
        ),
        out_shape=jax.ShapeDtypeStruct((rows // halves, cols // 2), jnp.bfloat16),
        compiler_params=pltpu.CompilerParams(vmem_limit_bytes=48 << 20),
        cost_estimate=pl.CostEstimate(
            flops=2 * tokens * (rows // halves) * cols,
            bytes_accessed=2 * tokens * (rows + cols) + rows * cols,
            transcendentals=0,
        ),
        name="wgrad",
    )(jnp.stack([row_start, col_half * nc]).astype(jnp.int32), a0, b0, a1, b1)


def partial_grad(left, right, far_left, far_right):
    return wgrad(left, right, far_left, far_right, None, lax.axis_index("core"))


def local(
    image_in,
    text_in,
    modulation,
    text_len,
    w_qkv,
    b_qkv,
    w_out,
    b_out,
    w_up,
    b_up,
    w_down,
    b_down,
    d_image,
    d_text,
):
    x, z, g, y, c = coords()
    image_half, text_half = image_in.shape[1], text_in.shape[1]
    width = image_in.shape[2]
    text_rows = -(-2 * text_half // 16) * 16

    def take(arr, index=x):
        return lax.dynamic_index_in_dim(arr, index, 0, keepdims=False)

    def join(near, far, rows):
        pad = jnp.zeros((rows - 2 * near.shape[0], width), near.dtype)
        return jnp.concatenate([near, far, pad], axis=0)

    def in_order(near, far):
        return jnp.where(x == 0, jnp.stack([near, far]), jnp.stack([far, near]))

    gathered, far = gather_weights(
        [(w_qkv, 0, True), (w_qkv, 1, False)], [take(image_in, 1 - x), take(text_in, 1 - x)], 0
    )
    weight_qkv = gathered
    streams = (join(take(image_in), far[0], 2 * image_half), join(take(text_in), far[1], text_rows))
    text_weights = [gather_offloaded(w_out, 1, (weight_qkv[0],))]
    gains = take(modulation)
    info = jnp.stack([take(text_len), jnp.int32(text_half), x.astype(jnp.int32)])
    small = gather_small(jnp.concatenate([b_qkv, b_out, b_up, b_down], axis=1))
    biases, start = [], 0
    for b in (b_qkv, b_out, b_up, b_down):
        biases.append(small[:, :, start : start + b.shape[1]].reshape(2, -1).astype(jnp.float32))
        start += b.shape[1]
    bias_qkv, bias_out, bias_up, bias_down = biases

    fronts = []
    for s in range(2):
        mod = gains[s]
        normed, inverse = normalize(streams[s].astype(jnp.float32))
        modded = (normed * (1.0 + mod[1]) + mod[0]).astype(jnp.bfloat16)
        projected = linear(modded, weight_qkv[s], bias_qkv[s]).astype(jnp.bfloat16)
        fronts.append((normed, inverse, modded, projected))
    (att_i, att_t, lse), image_weights, far = attend_and_gather(
        fronts[0][3],
        fronts[1][3],
        info,
        2 * image_half,
        [(w_out, 0, True), (w_up, 0, False), (w_down, 0, True)],
        [take(d_image, 1 - x), take(d_text, 1 - x)],
        1,
    )
    cotangents = (join(take(d_image), far[0], 2 * image_half), join(take(d_text), far[1], text_rows))
    text_weights += [gather_offloaded(w, 1, (image_weights[0],)) for w in (w_up, w_down)]
    weight_out, weight_up, weight_down = zip(image_weights, text_weights)

    outs, backs, column_sums, parts = [], [], [], {}
    token = att_i
    for s in range(2):
        mod = gains[s]
        attended = after((att_i, att_t)[s], token)
        upstream = cotangents[s].astype(jnp.float32)
        d_mlp = (mod[5] * upstream).astype(jnp.bfloat16)
        branch = linear(attended, weight_out[s], bias_out[s])
        middle = streams[s].astype(jnp.float32) + mod[2] * branch
        normed_two, inverse_two = normalize(middle)
        modded_two = (normed_two * (1.0 + mod[4]) + mod[3]).astype(jnp.bfloat16)
        if s == 1:
            text_mlp = gather_plane(modded_two, d_mlp, fronts[1][2])
        hidden = linear(modded_two, weight_up[s], bias_up[s])
        active, slope = gelu_both(hidden)
        if s == 0:
            far_active, far_d_mlp = flip_core(active), flip_core(d_mlp)
        mlp_out = linear(active, weight_down[s], bias_down[s])
        outs.append((middle + mod[5] * mlp_out).astype(jnp.bfloat16))
        d_gate_two = jnp.sum(upstream * mlp_out, axis=0)
        if s == 0:
            parts["down"] = partial_grad(after(active, outs[s]), d_mlp, far_active, far_d_mlp)
            d_mlp = after(d_mlp, parts["down"])
        d_active = linear_back(d_mlp, weight_down[s])
        d_hidden = (slope.astype(jnp.float32) * d_active).astype(jnp.bfloat16)
        if s == 0:
            far_d_hidden, far_modded_two = flip_core(d_hidden), flip_core(modded_two)
        d_modded_two = linear_back(d_hidden, weight_up[s])
        d_shift_two = jnp.sum(d_modded_two, axis=0)
        d_scale_two = jnp.sum(d_modded_two * normed_two, axis=0)
        d_middle = upstream + normalize_back(normed_two, inverse_two, d_modded_two * (1.0 + mod[4]))
        d_gate_one = jnp.sum(d_middle * branch, axis=0)
        d_branch = (mod[2] * d_middle).astype(jnp.bfloat16)
        if s == 0:
            parts["up"] = partial_grad(after(modded_two, d_branch), d_hidden, far_modded_two, far_d_hidden)
            far_attended, far_d_branch = flip_core(attended), flip_core(d_branch)
            d_branch = after(d_branch, parts["up"])
        else:
            text_out = (attended, d_branch)
        d_attended = linear_back(d_branch, weight_out[s]).astype(jnp.bfloat16)
        if s == 0:
            parts["out"] = partial_grad(after(attended, d_attended), d_branch, far_attended, far_d_branch)
            token = parts["out"]
        column_sums.append([column_sum(a) for a in (d_branch, d_hidden, d_mlp)])
        backs.append((d_attended, d_middle, d_gate_one, d_shift_two, d_scale_two, d_gate_two))
    sent = [outs[0][image_half:], outs[1][text_half : 2 * text_half]]
    text_totals = plane_mlp_totals(text_mlp[0], after(text_mlp[1], backs[1][0]), weight_up[1], bias_up[1], weight_down[1])
    far_text_modded = text_mlp[2]
    d_front, reduced, far_outs = attend_back_and_reduce(
        fronts[0][3],
        fronts[1][3],
        att_i,
        att_t,
        backs[0][0],
        backs[1][0],
        lse,
        info,
        image_half // 2,
        [parts["down"], parts["up"], parts["out"]],
        [(0, True, 0, parts["down"].shape[1]), (1, False, 0, parts["up"].shape[1]), (2, True, 0, parts["out"].shape[1])],
        sent,
        text_totals,
        2,
    )
    text_qkv, *text_out = gather_plane(d_front[1], *text_out)
    text_down, text_up = sum_fsdp(*text_totals)
    text_up = spread_up(text_up)
    text_out_total = plane_total(*text_out)
    far_front, far_modded = flip_core(d_front[0]), flip_core(fronts[0][2])
    grads = {("down", 0): reduced[0], ("up", 0): reduced[1], ("out", 0): reduced[2]}
    input_grads, gain_grads = [], []
    for s in range(2):
        mod = gains[s]
        normed, inverse, modded, _ = fronts[s]
        d_attended, d_middle, d_gate_one, d_shift_two, d_scale_two, d_gate_two = backs[s]
        d_modded = linear_back(d_front[s], weight_qkv[s])
        d_shift_one = jnp.sum(d_modded, axis=0)
        d_scale_one = jnp.sum(d_modded * normed, axis=0)
        input_grads.append(d_middle + normalize_back(normed, inverse, d_modded * (1.0 + mod[1])))
        gain_grads.append(
            jnp.stack([d_shift_one, d_scale_one, d_gate_one, d_shift_two, d_scale_two, d_gate_two])
        )
    mine = jnp.stack(gain_grads)
    part = partial_grad(after(fronts[0][2], *input_grads), d_front[0], far_modded, far_front)
    text_qkv_total = plane_total(far_text_modded, after(text_qkv, part))
    cols = part.shape[1]
    sent = [input_grads[0][image_half:].astype(jnp.bfloat16), input_grads[1][text_half : 2 * text_half].astype(jnp.bfloat16)]
    front_sums = [column_sum(d_front[s]) for s in range(2)]
    small = jnp.concatenate([front_sums[s] for s in range(2)] + [v for s in range(2) for v in column_sums[s]])
    reduced, far_grads, small = reduce_weights(
        [part],
        [(0, True, 0, cols // 2), (0, False, cols // 2, cols // 2)],
        sent + [mine.reshape(-1, width)],
        small.reshape(-1, 128),
        [text_qkv_total, text_out_total],
        3,
    )
    grads["qkv", 0] = reduced[0]
    grads["down", 1], grads["up", 1] = text_down.astype(jnp.float32), text_up
    for name, total in zip(("out", "qkv"), sum_fsdp(text_out_total, text_qkv_total)):
        grads[name, 1] = total.astype(jnp.float32)
    grad_modulation = in_order(mine, far_grads[2].reshape(mine.shape))

    count = lax.axis_size(("seq", "fsdp") + DP)
    index = lax.axis_index(("seq", "fsdp") + DP)

    def cut_bias(total):
        return lax.dynamic_index_in_dim(total.reshape(2, count, -1), index, 1, keepdims=False)

    small = small.reshape(-1)
    front = front_sums[0].shape[0]
    per_stream = small[2 * front :].reshape(2, -1)
    sizes = [a.shape[0] for a in column_sums[0]]
    gb_qkv = cut_bias(small[: 2 * front].reshape(2, front))
    gb_out, gb_up, gb_down = [
        cut_bias(a) for a in jnp.split(per_stream, [sizes[0], sizes[0] + sizes[1]], axis=1)
    ]
    grads_qkv, grads_out, grads_up, grads_down = [
        jnp.stack([grads[name, s] for s in range(2)]) for name in ("qkv", "out", "up", "down")
    ]
    halves = (image_half, text_half)
    return (
        *[in_order(outs[s][: halves[s]], far_outs[s]) for s in range(2)],
        *[in_order(input_grads[s][: halves[s]], far_grads[s].astype(jnp.float32)) for s in range(2)],
        grad_modulation,
        grads_qkv,
        gb_qkv,
        grads_out,
        gb_out,
        grads_up,
        gb_up,
        grads_down,
        gb_down,
    )


def solution(mesh):
    seq, fsdp, dp = (mesh.shape[name] for name in ("seq", "fsdp", "dp"))
    split = Mesh(mesh.devices.reshape(seq, fsdp, dp // 2, 2), ("seq", "fsdp", "y", "core"))
    batch = ("fsdp",) + DP
    tokens = P(batch, "seq", None)
    weight, bias = P(None, "fsdp", None), P(None, "fsdp")
    in_specs = (tokens, tokens, P(batch, None, None, None), P(batch))
    in_specs += (weight, bias) * 4 + (tokens, tokens)
    everywhere = ("seq",) + batch
    grad_w, grad_b = P(None, everywhere, None), P(None, everywhere)
    out_specs = (tokens,) * 4 + (P(batch, None, None, None),) + (grad_w, grad_b) * 4
    return jax.shard_map(local, mesh=split, in_specs=in_specs, out_specs=out_specs, check_vma=False)
```
